128 devices in a mesh: slab: 4 (over y_lo, core), vel: 32 (over x, y_hi, z).
Axes of the slice: x: 4, y: 4 (y_hi: 2, y_lo: 2; y = y_hi * 2 + y_lo), z: 4, core: 2. Of those that a mesh axis runs over, the one named last changes fastest.
Arguments:
- dist: float32 [24576, 16, 128], P('vel', 'slab'), may hold values from -6 to 6
- speeds: float32 [3, 24576], P(None, 'vel'), may hold values from -4 to 4
- weights: float32 [24576], P('vel'), may hold values from 0.5 to 2
- collision: float32 [16, 128], P('slab'), may hold values from 0.3 to 3
- wall_values: float32 [2, 24576], P(None, 'vel'), may hold values from -6 to 6
- wall_kind: int32 [2, 24576], P(None, 'vel'), may hold values from 0 to 1
Outputs:
- final_dist: float32 [24576, 16, 128], P('vel', 'slab')
- settled: float32 [5, 16, 128], P(None, 'slab')
The draws below stay inside these ranges and needn't reach their ends.
Inputs may be any that keep to these rules, and one draw needn't show every extreme that they name: `wall_kind`: 1 lets the wall's value enter for velocities leaving that wall, 0 makes the wall absorbing.
All inputs are finite; a program needn't handle non-finite values.
Results may differ from the reference program's by a relative error of at most 0.0003.
Values sent between devices are 32-bit elements; how exact they have to be, the bound alone decides.
A program may use at most 64 MiB of HBM per device.

```python
import math
import jax
import jax.numpy as jnp
from jax import lax

VELS = 24576
NY = 128
ITERS = 2
JACOBI = 2
NX = 16
N_VEL = 32


def set_ends(drawn, key, least, high):
    dims = drawn.shape
    place = [jax.random.randint(jax.random.fold_in(key, axis), (), 0, dims[axis]) for axis in range(len(dims))]
    drawn = drawn.at[tuple(place)].set(least)
    longest = dims.index(max(dims))
    place[longest] = (place[longest] + 1) % dims[longest]
    return drawn.at[tuple(place)].set(high)


def level_of(key, extent, split, low, high):
    gain, own = 1.0, jax.random.fold_in(key, 6)
    for axis_at, shards_of in split:
        heights = jnp.exp(jax.random.uniform(jax.random.fold_in(own, axis_at), (shards_of,), jnp.float32, low / len(split), high / len(split)))
        gain = gain * jnp.repeat(heights, extent[axis_at] // shards_of).reshape([-1 if axis == axis_at else 1 for axis in range(len(extent))])
    return gain


def noise(stream_key, dims, scale, reach, cuts=(), dtype=jnp.bfloat16):
    values = jax.random.normal(stream_key, dims, jnp.float32) * scale
    if len(cuts) > 0:
        values = level_of(stream_key, dims, cuts, -0.22, 0.18) * values
    return jnp.clip(values, min=-reach, max=reach).astype(dtype)


def setup_inputs(seed: int = 0) -> dict:
    arg_keys = jax.random.split(jax.random.key(seed), 7)
    dist = noise(arg_keys[0], (VELS, NX, NY), 1.0, 6.0, ((0, 32), (1, 4)), jnp.float32)
    speeds = noise(arg_keys[1], (3, VELS), 1.0, 4.0, ((1, 32),), jnp.float32)
    weights = jnp.clip(jnp.exp(math.log(2.0) - 1.3862944 * jax.random.uniform(arg_keys[2], (VELS,), jnp.float32) ** level_of(arg_keys[2], (VELS,), ((0, 32),), -0.2, 0.2)), 0.5, 2.0)
    collision = jnp.clip(jnp.exp(math.log(3.0) - 2.3025851 * jax.random.uniform(arg_keys[3], (NX, NY), jnp.float32) ** level_of(arg_keys[3], (NX, NY), ((0, 4),), -0.2, 0.2)), 0.3, 3.0)
    wall_values = noise(arg_keys[4], (2, VELS), 1.0, 6.0, ((1, 32),), jnp.float32)
    wall_kind = set_ends(jax.random.randint(arg_keys[5], (2, VELS), 0, 2), jax.random.fold_in(arg_keys[5], 1), 0, 1).astype(jnp.int32)
    return dict(dist=dist, speeds=speeds, weights=weights, collision=collision, wall_values=wall_values, wall_kind=wall_kind)


PRECISE = lax.Precision.HIGHEST


def moment_rows(speeds):
    speed_x, speed_y, speed_z = speeds[0], speeds[1], speeds[2]
    square = speed_x * speed_x + speed_y * speed_y + speed_z * speed_z
    third = square / 3.0
    return jnp.stack([jnp.ones_like(speed_x), speed_x, speed_y, speed_z, 2.0 / 3.0 * square - 1.0,
                      speed_x * (square - 2.5), speed_y * (square - 2.5), speed_z * (square - 2.5),
                      speed_x * speed_x - third, speed_x * speed_y, speed_x * speed_z,
                      speed_y * speed_y - third, speed_y * speed_z])


def shape_rows(speeds):
    speed_x, speed_y, speed_z = speeds[0], speeds[1], speeds[2]
    square = speed_x * speed_x + speed_y * speed_y + speed_z * speed_z
    factor = 4.0 / 45.0 * (square - 2.5)
    return jnp.stack([jnp.ones_like(speed_x), 2.0 * speed_x, 2.0 * speed_y, 2.0 * speed_z, square - 1.5,
                      factor * speed_x, factor * speed_y, factor * speed_z], axis=1)


def pad_cells(values):
    return jnp.pad(values, ((0, 0), (1, 1), (1, 1)))


def macro_fields(moment, collision, widen):
    widened = widen(moment)

    def diff_x(which):
        return 0.5 * (widened[which, 2:, 1:-1] - widened[which, :-2, 1:-1])

    def diff_y(which):
        return 0.5 * (widened[which, 1:-1, 2:] - widened[which, 1:-1, :-2])

    fluxes = jnp.stack([-(diff_x(1) + diff_y(2)), -(diff_x(8) + diff_y(9)), -(diff_x(9) + diff_y(11)),
                        -(diff_x(10) + diff_y(12)), -(diff_x(5) + diff_y(6))])
    target = moment[:5] + fluxes
    stiffness = 1.0 / collision
    beside_all = widened[:5]
    settled = moment[:5]
    for jacobi_turn in range(JACOBI):
        if jacobi_turn > 0:
            beside_all = widen(settled)
        neighbours = beside_all[:, 2:, 1:-1] + beside_all[:, :-2, 1:-1] + beside_all[:, 1:-1, 2:] + beside_all[:, 1:-1, :-2]
        settled = (target + stiffness * neighbours) / (1.0 + 4.0 * stiffness)
    return settled


def combine(earlier, later):
    return (earlier[0] * later[0], later[0] * earlier[1] + later[1])


def sweep_across(factor, source, axis):
    return lax.associative_scan(combine, (factor, source), axis=axis)


def along_y(values, speed_y):
    cross_rate = (jnp.abs(speed_y) * values.shape[2])[:, None, None]
    forward = (speed_y >= 0)[:, None, None]
    factor = jnp.broadcast_to(cross_rate / (1.0 + cross_rate), values.shape)
    source = values / (1.0 + cross_rate)
    source = jnp.where(forward, source, source[:, :, ::-1])
    result = sweep_across(factor, source, 2)[1]
    return jnp.where(forward, result, result[:, :, ::-1])


def upwind_terms(values, equilibrium, speed_x, collision, cells):
    cross_rate = (jnp.abs(speed_x) * cells)[:, None, None]
    denominator = 1.0 + cross_rate + collision[None]
    factor = cross_rate / denominator
    source = (values + collision[None] * equilibrium) / denominator
    forward = (speed_x >= 0)[:, None, None]
    factor = jnp.where(forward, factor, factor[:, ::-1, :])
    source = jnp.where(forward, source, source[:, ::-1, :])
    return factor, source, forward


def transport(values, equilibrium, speed_x, speed_y, inflow, collision):
    factor, source, forward = upwind_terms(values, equilibrium, speed_x, collision, NX)
    product, accrued = sweep_across(factor, source, 1)
    entering = jnp.where(speed_x >= 0, inflow[0], inflow[1])[:, None, None]
    flipped = product * entering + accrued
    inner = jnp.where(forward, flipped, flipped[:, ::-1, :])
    return along_y(inner, speed_y)


def reference(dist, speeds, weights, collision, wall_values, wall_kind):
    inflow = wall_values * wall_kind.astype(jnp.float32)
    rows = moment_rows(speeds) * weights[None] / VELS
    shapes = shape_rows(speeds)
    block = VELS // N_VEL
    field = dist
    settled = jnp.zeros((5, NX, NY), jnp.float32)
    for outer_turn in range(ITERS):
        moment = jnp.einsum('kv,vxy->kxy', rows, field, precision=PRECISE)
        settled = macro_fields(moment, collision, pad_cells)
        drive = jnp.concatenate([settled, moment[5:8]], 0)

        def one_block(pieces):
            values, shape_block, speed_x, speed_y, inflow_block = pieces
            equilibrium = jnp.einsum('vk,kxy->vxy', shape_block, drive, precision=PRECISE)
            return transport(values, equilibrium, speed_x, speed_y, inflow_block, collision)

        result = lax.map(one_block, (field.reshape(N_VEL, block, NX, NY), shapes.reshape(N_VEL, block, 8),
                                     speeds[0].reshape(N_VEL, block), speeds[1].reshape(N_VEL, block),
                                     inflow.reshape(2, N_VEL, block).transpose(1, 0, 2)))
        field = result.reshape(VELS, NX, NY)
    return field, settled
```

```python
import jax
import jax.numpy as jnp
from jax import lax
from jax.experimental import pallas as pl
from jax.experimental.pallas import tpu as pltpu
from jax.sharding import PartitionSpec as P

VELS = 24576
ITERS = 2
JACOBI = 2
NX = 16
NY = 128
SLABS = 4
XL = NX // SLABS
V = VELS // 32
VB = 128
NB = V // VB
PAD = NX - XL
KR = 16
HALF = XL * NY // 2
STEPS = (1, 2, 4, 8, 16, 32, 64)

f32 = jnp.float32
bf16 = jnp.bfloat16
MESH = pl.DeviceIdType.MESH


def split(value):
    high = value.astype(bf16)
    return high, (value - high.astype(f32)).astype(bf16)


def dot(a, b):
    return jnp.dot(a, b, preferred_element_type=f32)


def lanes(shape):
    return lax.broadcasted_iota(jnp.int32, shape, 1)


def mirrored(value):
    return jnp.take_along_axis(value, NY - 1 - lanes(value.shape), axis=1)


def transport_kernel(
    dist, speeds, weights, collision, wall_values, wall_kind,
    out, settled_out,
    draw, gd, fhi, flo, fac, wgt, inv_own, prod, ycoef, ascale, bscale, fxs, fys,
    near, far, outa, outb, rows_t, rows_p, rows_g, shp, col,
    b1, b2, b3, cbuf, crow, dpad, rhs, drive_s,
    dsem, osem, bsend, brecv, ysend, yrecv, csend, crecv, nsend, nrecv, fsend, frecv,
):
    slab = lax.axis_index("slab")
    vel = lax.axis_index("vel")
    px = vel // 8
    py = (vel // 4) % 2
    pz = vel % 4
    edge = jnp.logical_or(slab == 0, slab == SLABS - 1)
    middle = jnp.logical_and(slab > 0, slab < SLABS - 1)
    low_side = slab < 2
    partner = jnp.where(low_side, 1 - slab, 5 - slab)
    across = 3 - slab

    def device(s, x, y, z):
        return {"slab": s, "vel": (x * 2 + y) * 4 + z}

    loads = [
        pltpu.make_async_copy(dist.at[:, x, :], draw.at[x], dsem.at[x]) for x in range(XL)
    ]
    for load in loads:
        load.start()

    peers = []
    for d in range(1, 4):
        peers.append(device(slab, (px + d) % 4, py, pz))
    for d in range(1, 4):
        peers.append(device(slab, px, py, (pz + d) % 4))
    group = py * 4 + slab
    yz = []
    for d in range(1, 8):
        other = (group + d) % 8
        yz.append(device(other % 4, px, other // 4, pz))
    barrier = pltpu.get_barrier_semaphore()
    for peer in peers + yz:
        pl.semaphore_signal(barrier, inc=1, device_id=peer, device_id_type=MESH)

    cx, cy, cz = speeds[0:1, :], speeds[1:2, :], speeds[2:3, :]
    wt = weights[0:1, :]
    square = cx * cx + cy * cy + cz * cz
    third = square / 3.0
    heat = square - 2.5
    one = jnp.ones_like(cx)
    zero = jnp.zeros_like(cx)
    phi = [
        one, cx, cy, cz, 2.0 / 3.0 * square - 1.0, cx * heat, cy * heat, cz * heat,
        cx, cx * cx - third, cx * cy, cx * cz, cx * heat, cy * cy - third, cy * cz, zero,
    ]
    scale = wt / VELS
    fx = jnp.where(cx >= 0, 1.0, 0.0)
    fy = jnp.where(cy >= 0, 1.0, 0.0)
    rows = jnp.concatenate([p * scale for p in phi], axis=0)
    rows_hi, rows_lo = split(rows)
    rows_p[0:KR, :] = rows_hi
    rows_p[KR : 2 * KR, :] = rows_lo
    masks = [fx * fy, fx * (1.0 - fy), (1.0 - fx) * fy, (1.0 - fx) * (1.0 - fy)]
    for g in range(4):
        m = masks[g].astype(bf16)
        rows_g[g * KR : (g + 1) * KR, :] = rows_hi * m
        rows_g[4 * KR + g * KR : 4 * KR + (g + 1) * KR, :] = rows_lo * m

    for x in range(XL):
        loads[x].wait()
        def cast(i, c, x=x):
            at = pl.ds(i * VB, VB)
            hi, lo = split(draw[x, at, :])
            fhi[at, x * NY : (x + 1) * NY] = hi
            flo[at, x * NY : (x + 1) * NY] = lo
            return c
        lax.fori_loop(0, NB, cast, 0)
    first = dot(rows_p[...], fhi[...])
    moment = first[0:KR] + first[KR : 2 * KR] + dot(rows_p[0:KR, :], flo[...])

    pl.semaphore_wait(barrier, 13)

    axes = ((px, lambda o: device(slab, o, py, pz)), (pz, lambda o: device(slab, px, py, o)))

    def exchange(buf, stage, it, piece):
        me, to = axes[(stage + piece) % 2]
        sent = []
        for d in range(1, 4):
            copy = pltpu.make_async_remote_copy(
                src_ref=buf.at[it, piece, me],
                dst_ref=buf.at[it, piece, me],
                send_sem=bsend.at[it, stage, piece, d - 1],
                recv_sem=brecv.at[it, stage, piece, d - 1],
                device_id=to((me + d) % 4),
                device_id_type=MESH,
            )
            copy.start()
            sent.append(copy)
        return sent

    def arrived(buf, stage, it, piece):
        me, to = axes[(stage + piece) % 2]
        for d in range(1, 4):
            source = (me + 4 - d) % 4
            pltpu.make_async_remote_copy(
                src_ref=buf.at[it, piece, source],
                dst_ref=buf.at[it, piece, source],
                send_sem=bsend.at[it, stage, piece, d - 1],
                recv_sem=brecv.at[it, stage, piece, d - 1],
                device_id=to(source),
                device_id_type=MESH,
            ).wait_recv()
        return (buf[it, piece, 0] + buf[it, piece, 1]) + (buf[it, piece, 2] + buf[it, piece, 3])

    def spread(it, piece):
        sent = []
        for d in range(1, 8):
            copy = pltpu.make_async_remote_copy(
                src_ref=b3.at[it, piece, group],
                dst_ref=b3.at[it, piece, group],
                send_sem=ysend.at[it, piece, d - 1],
                recv_sem=yrecv.at[it, piece, d - 1],
                device_id=yz[d - 1],
                device_id_type=MESH,
            )
            copy.start()
            sent.append(copy)
        return sent

    def spread_arrived(it, piece):
        for d in range(1, 8):
            source = (group + 8 - d) % 8
            pltpu.make_async_remote_copy(
                src_ref=b3.at[it, piece, source],
                dst_ref=b3.at[it, piece, source],
                send_sem=ysend.at[it, piece, d - 1],
                recv_sem=yrecv.at[it, piece, d - 1],
                device_id=yz[d - 1],
                device_id_type=MESH,
            ).wait_recv()

    def start_reduce(it, value):
        sent = []
        for piece in range(2):
            b1[it, piece, axes[piece % 2][0]] = value[:, piece * HALF : (piece + 1) * HALF]
            sent += exchange(b1, 0, it, piece)
        return sent

    def second_stage(it):
        sent = []
        for piece in range(2):
            total = arrived(b1, 0, it, piece)
            b2[it, piece, axes[(1 + piece) % 2][0]] = total
            sent += exchange(b2, 1, it, piece)
        return sent

    def third_stage(it):
        sent = []
        for piece in range(2):
            b3[it, piece, group] = arrived(b2, 1, it, piece)
            sent += spread(it, piece)
        return sent

    sent = start_reduce(0, moment)
    for d in range(1, 4):
        copy = pltpu.make_async_remote_copy(
            src_ref=collision,
            dst_ref=cbuf.at[slab],
            send_sem=csend.at[d - 1],
            recv_sem=crecv.at[d - 1],
            device_id=device((slab + d) % 4, px, py, pz),
            device_id_type=MESH,
        )
        copy.start()
        sent.append(copy)
    cbuf[slab] = collision[...]

    rows_t[...] = jnp.zeros_like(rows_t)
    inflow = wall_values[...] * wall_kind[...].astype(f32)
    rate_x = jnp.abs(cx) * NX
    rate_y = jnp.abs(cy) * NY
    rows_t[0:1, :] = rate_x
    rows_t[1:2, :] = rate_y / (1.0 + rate_y)
    rows_t[2:3, :] = 1.0 / (1.0 + rate_y)
    rows_t[3:4, :] = jnp.where(low_side, inflow[0:1], inflow[1:2])
    rows_t[4:5, :] = fx
    rows_t[5:6, :] = fy
    for i in range(NB):
        at = slice(i * VB, (i + 1) * VB)
        col[at, :] = jnp.transpose(rows_t[:, at])
    factor = 4.0 / 45.0 * heat
    psi = jnp.concatenate(
        [one, 2.0 * cx, 2.0 * cy, 2.0 * cz, square - 1.5, factor * cx, factor * cy, factor * cz],
        axis=0,
    )
    psi_hi = psi.astype(bf16).astype(f32)
    psi_lo = psi - psi_hi
    for g in range(4):
        rows_t[g * 32 : g * 32 + 8, :] = psi_hi * masks[g]
        rows_t[g * 32 + 8 : g * 32 + 16, :] = psi_hi * masks[g]
        rows_t[g * 32 + 16 : g * 32 + 24, :] = psi_lo * masks[g]
        rows_t[g * 32 + 24 : g * 32 + 32, :] = psi_lo * masks[g]
    for i in range(NB):
        at = slice(i * VB, (i + 1) * VB)
        shp[at, :] = jnp.transpose(rows_t[:, at]).astype(bf16)

    lane = lanes((VB, NY))

    def send_out(buf, target, send, recv, it, i, to):
        at = pl.ds(i * VB, VB)
        pltpu.make_async_remote_copy(
            src_ref=buf.at[it, at],
            dst_ref=target.at[it, at],
            send_sem=send.at[it, i],
            recv_sem=recv.at[it, i],
            device_id=device(to, px, py, pz),
            device_id_type=MESH,
        ).start()

    def wait_in(target, send, recv, it, i):
        at = pl.ds(i * VB, VB)
        pltpu.make_async_remote_copy(
            src_ref=target.at[it, at],
            dst_ref=target.at[it, at],
            send_sem=send.at[it, i],
            recv_sem=recv.at[it, i],
            device_id=device(partner, px, py, pz),
            device_id_type=MESH,
        ).wait_recv()

    def wait_out(buf, target, send, recv, it, i):
        at = pl.ds(i * VB, VB)
        pltpu.make_async_remote_copy(
            src_ref=buf.at[it, at],
            dst_ref=target.at[it, at],
            send_sem=send.at[it, i],
            recv_sem=recv.at[it, i],
            device_id=device(partner, px, py, pz),
            device_id_type=MESH,
        ).wait_send()

    own = collision[...]
    own_back = mirrored(jnp.concatenate([own, own], axis=0))

    def sweep_source(fields, at, it, i):
        total = inv_own[0, at, :] * fields[0]
        gd[0, at, :] = total
        for q in range(1, XL):
            total = fac[PAD + q, at, :] * total + inv_own[q, at, :] * fields[q]
            gd[q, at, :] = total

        @pl.when(edge)
        def _():
            outa[it, at, :] = prod[at, :] * near[it, at, :] + total
            send_out(outa, near, nsend, nrecv, it, i, partner)

    def prepare(i, c):
        at = pl.ds(i * VB, VB)
        cols = col[at, :]
        wide = lambda k: jnp.broadcast_to(cols[:, k : k + 1], (VB, NY))
        a = wide(0)
        ascale[at, :] = a
        power = wide(1)
        for k, step in enumerate(STEPS):
            ycoef[k, at, :] = jnp.where(lane >= step, power, 0.0)
            power = power * power
        bscale[at, :] = wide(2)
        fxv, fyv = wide(4), wide(5)
        fxs[at, :] = fxv
        fys[at, :] = fyv
        forward, upward = fxv > 0.5, fyv > 0.5

        @pl.when(edge)
        def _():
            for it in range(ITERS):
                near[it, at, :] = wide(3)

        index = jnp.where(upward, lane, NY - 1 - lane)
        product = None
        fields = []
        for q in range(XL):
            m = XL - 1 - q
            rate = jnp.where(
                forward,
                jnp.where(upward, own[q : q + 1], own_back[q : q + 1]),
                jnp.where(upward, own[m : m + 1], own_back[m : m + 1]),
            )
            inv = 1.0 / (1.0 + a + rate)
            f = a * inv
            inv_own[q, at, :] = inv
            fac[PAD + q, at, :] = f
            wgt[PAD + q, at, :] = rate * inv
            product = f if product is None else product * f
            picked = jnp.where(forward, draw[q, at, :], draw[m, at, :])
            fields.append(jnp.take_along_axis(picked, index, axis=1))
        prod[at, :] = product
        sweep_source(fields, at, 0, i)
        return c

    lax.fori_loop(0, NB, prepare, 0)

    def chain_across(it):
        @pl.when(middle)
        def _():
            def step(i, c):
                at = pl.ds(i * VB, VB)
                wait_in(near, nsend, nrecv, it, i)
                outa[it, at, :] = prod[at, :] * near[it, at, :] + gd[XL - 1, at, :]
                send_out(outa, far, fsend, frecv, it, i, across)
                return c
            lax.fori_loop(0, NB, step, 0)

    def chain_back(it):
        @pl.when(middle)
        def _():
            def step(i, c):
                at = pl.ds(i * VB, VB)
                wait_in(far, fsend, frecv, it, i)
                outb[it, at, :] = prod[at, :] * far[it, at, :] + gd[XL - 1, at, :]
                pltpu.make_async_remote_copy(
                    src_ref=outb.at[it, at],
                    dst_ref=far.at[it, at],
                    send_sem=nsend.at[it, i],
                    recv_sem=frecv.at[it, i],
                    device_id=device(partner, px, py, pz),
                    device_id_type=MESH,
                ).start()
                return c
            lax.fori_loop(0, NB, step, 0)

    def drain_chain(it):
        @pl.when(middle)
        def _():
            def step(i, c):
                wait_out(outa, far, fsend, frecv, it, i)
                wait_out(outb, far, nsend, frecv, it, i)
                return c
            lax.fori_loop(0, NB, step, 0)

        @pl.when(edge)
        def _():
            def step(i, c):
                wait_out(outa, near, nsend, nrecv, it, i)
                return c
            lax.fori_loop(0, NB, step, 0)

    sent += second_stage(0)
    chain_across(0)

    for d in range(1, 4):
        source = (slab + 4 - d) % 4
        pltpu.make_async_remote_copy(
            src_ref=collision,
            dst_ref=cbuf.at[source],
            send_sem=csend.at[d - 1],
            recv_sem=crecv.at[d - 1],
            device_id=device(source, px, py, pz),
            device_id_type=MESH,
        ).wait_recv()
    crow[...] = jnp.zeros_like(crow)
    everywhere = jnp.concatenate([cbuf[s] for s in range(SLABS)], axis=0)
    turned = mirrored(everywhere)
    for i in range(NX):
        crow[0, PAD + i] = jnp.broadcast_to(everywhere[i : i + 1], (8, NY))
        crow[1, PAD + i] = jnp.broadcast_to(turned[i : i + 1], (8, NY))

    def upstream(start, stop):
        def at_cell(r, c):
            ahead = XL * slab + r
            behind = XL * slab + PAD + NX - 1 - r
            c_ff = crow[0, ahead][0:1]
            c_fb = crow[1, ahead][0:1]
            c_bf = crow[0, behind][0:1]
            c_bb = crow[1, behind][0:1]
            def block(i, c):
                at = pl.ds(i * VB, VB)
                a = ascale[at, :]
                forward, upward = fxs[at, :] > 0.5, fys[at, :] > 0.5
                rate = jnp.where(
                    forward, jnp.where(upward, c_ff, c_fb), jnp.where(upward, c_bf, c_bb)
                )
                inv = 1.0 / (1.0 + a + rate)
                fac[r, at, :] = a * inv
                wgt[r, at, :] = rate * inv
                return c
            lax.fori_loop(0, NB, block, 0)
            return c
        lax.fori_loop(start, stop, at_cell, 0)

    upstream(0, 5)
    sent += third_stage(0)
    upstream(5, PAD)
    chain_back(0)

    cell = lanes((8, NY))
    sub = lax.broadcasted_iota(jnp.int32, (8, NY), 0)

    def above(value):
        return jnp.where(cell < NY - 1, pltpu.roll(value, NY - 1, 1), 0.0)

    def below(value):
        return jnp.where(cell >= 1, pltpu.roll(value, 1, 1), 0.0)

    def macro(it):
        for piece in range(2):
            spread_arrived(it, piece)
        head, flux = [], []
        for i in range(NX):
            s, x = i // XL, i % XL
            piece, at = x // 2, slice((x % 2) * NY, (x % 2 + 1) * NY)
            head.append(b3[it, piece, s, 0:8, at] + b3[it, piece, 4 + s, 0:8, at])
            flux.append(b3[it, piece, s, 8:16, at] + b3[it, piece, 4 + s, 8:16, at])
        nothing = jnp.zeros((8, NY), f32)
        target, kappa, down = [], [], []
        for i in range(NX):
            a, b = head[i], flux[i]
            cross = jnp.concatenate([a[2:3], b[2:3], b[5:6], b[6:7], a[6:7], b[7:8], b[7:8], b[7:8]], axis=0)
            right = flux[i + 1] if i + 1 < NX else nothing
            left = flux[i - 1] if i > 0 else nothing
            target.append(a - (0.5 * (right - left) + 0.5 * (above(cross) - below(cross))))
            stiff = 1.0 / crow[0, PAD + i]
            kappa.append(stiff)
            down.append(1.0 / (1.0 + 4.0 * stiff))
        settled = head
        for _ in range(JACOBI):
            after = []
            for i in range(NX):
                right = settled[i + 1] if i + 1 < NX else nothing
                left = settled[i - 1] if i > 0 else nothing
                around = right + left + above(settled[i]) + below(settled[i])
                after.append((target[i] + kappa[i] * around) * down[i])
            settled = after
        dpad[...] = jnp.zeros_like(dpad)
        for i in range(NX):
            drive = jnp.where(sub < 5, settled[i], head[i])
            drive_s[i] = drive
            hi, lo = split(drive)
            dpad[0, PAD + i] = jnp.concatenate([hi, lo], axis=0)
            hi, lo = split(mirrored(drive))
            dpad[1, PAD + i] = jnp.concatenate([hi, lo], axis=0)
        for r in range(NX):
            ahead = XL * slab + r
            behind = XL * slab + PAD + NX - 1 - r
            at = slice(r * NY, (r + 1) * NY)
            for g, tile in enumerate(
                (dpad[0, ahead], dpad[1, ahead], dpad[0, behind], dpad[1, behind])
            ):
                rhs[g * 32 : g * 32 + 16, at] = tile
                rhs[g * 32 + 16 : g * 32 + 32, at] = tile

    def main(it):
        last = it == ITERS - 1

        def block(i, c):
            at = pl.ds(i * VB, VB)
            eq = dot(shp[at, :], rhs[...])
            enter = wgt[0, at, :] * eq[:, 0:NY]
            for r in range(1, PAD):
                enter = fac[r, at, :] * enter + wgt[r, at, :] * eq[:, r * NY : (r + 1) * NY]

            @pl.when(edge)
            def _():
                wait_in(far, fsend, frecv, it, i)

            forward = fxs[at, :] > 0.5
            from_near = jnp.where(low_side, fxs[at, :], 1.0 - fxs[at, :]) > 0.5
            enter = enter + jnp.where(from_near, near[it, at, :], far[it, at, :])
            fields = []
            for q in range(XL):
                r = PAD + q
                enter = fac[r, at, :] * enter + wgt[r, at, :] * eq[:, r * NY : (r + 1) * NY]
                h = (gd[q, at, :] + enter) * bscale[at, :]
                for k, step in enumerate(STEPS):
                    h = h + ycoef[k, at, :] * pltpu.roll(h, step, 1)
                if last:
                    gd[q, at, :] = h
                else:
                    hi, lo = split(h)
                    fhi[at, q * NY : (q + 1) * NY] = hi
                    flo[at, q * NY : (q + 1) * NY] = lo
                    fields.append(h)
            if last:
                for q in range(XL):
                    pltpu.make_async_copy(gd.at[q, at], out.at[q, at], osem.at[q, i]).start()
            else:
                sweep_source(fields, at, it + 1, i)
            return c

        lax.fori_loop(0, NB, block, 0)

    for it in range(ITERS):
        macro(it)
        main(it)
        if it < ITERS - 1:
            first = dot(rows_g[...], fhi[...])
            groups = first[0 : 4 * KR] + first[4 * KR : 8 * KR] + dot(rows_g[0 : 4 * KR, :], flo[...])
            turn = lambda t: jnp.concatenate(
                [t[:, x * NY : (x + 1) * NY] for x in reversed(range(XL))], axis=1
            )
            up = groups[0:KR] + turn(groups[2 * KR : 3 * KR])
            down = groups[KR : 2 * KR] + turn(groups[3 * KR : 4 * KR])
            moment = up + jnp.concatenate(
                [mirrored(down[:, x * NY : (x + 1) * NY]) for x in range(XL)], axis=1
            )
            sent += start_reduce(it + 1, moment)
            chain_across(it + 1)
            sent += second_stage(it + 1)
            chain_back(it + 1)
            sent += third_stage(it + 1)

    for x in range(XL):
        settled_out[:, x, :] = drive_s[XL * slab + x][0:5]

    def drain(i, c):
        at = pl.ds(i * VB, VB)
        for q in range(XL):
            pltpu.make_async_copy(gd.at[q, at], out.at[q, at], osem.at[q, i]).wait()
        return c

    lax.fori_loop(0, NB, drain, 0)
    for it in range(ITERS):
        drain_chain(it)
    for copy in sent:
        copy.wait_send()


def order_kernel(field, speeds, settled, out, settled_out):
    signs = jnp.transpose(speeds[...])
    forward = jnp.broadcast_to(signs[:, 0:1], (VB, NY)) >= 0
    upward = jnp.broadcast_to(signs[:, 1:2], (VB, NY)) >= 0
    lane = lanes((VB, NY))
    index = jnp.where(upward, lane, NY - 1 - lane)
    for x in range(XL):
        picked = jnp.where(forward, field[x], field[XL - 1 - x])
        out[pl.ds(x, VB, stride=XL), :] = jnp.take_along_axis(picked, index, axis=1)
    settled_out[...] = settled[...]


def on_device(dist, speeds, weights, collision, wall_values, wall_kind):
    vmem = pl.BlockSpec(memory_space=pltpu.VMEM)
    hbm = pl.BlockSpec(memory_space=pl.ANY)
    dma = pltpu.SemaphoreType.DMA
    full = (V, NY)
    scratch = [
        pltpu.VMEM((XL, *full), f32),
        pltpu.VMEM((XL, *full), f32),
        pltpu.VMEM((V, XL * NY), bf16),
        pltpu.VMEM((V, XL * NY), bf16),
        pltpu.VMEM((NX, *full), f32),
        pltpu.VMEM((NX, *full), f32),
        pltpu.VMEM((XL, *full), f32),
        pltpu.VMEM(full, f32),
        pltpu.VMEM((len(STEPS), *full), f32),
        pltpu.VMEM(full, f32),
        pltpu.VMEM(full, f32),
        pltpu.VMEM(full, f32),
        pltpu.VMEM(full, f32),
        pltpu.VMEM((ITERS, *full), f32),
        pltpu.VMEM((ITERS, *full), f32),
        pltpu.VMEM((ITERS, *full), f32),
        pltpu.VMEM((ITERS, *full), f32),
        pltpu.VMEM((128, V), f32),
        pltpu.VMEM((2 * KR, V), bf16),
        pltpu.VMEM((8 * KR, V), bf16),
        pltpu.VMEM((V, 128), bf16),
        pltpu.VMEM((V, 128), f32),
        pltpu.VMEM((ITERS, 2, 4, KR, HALF), f32),
        pltpu.VMEM((ITERS, 2, 4, KR, HALF), f32),
        pltpu.VMEM((ITERS, 2, 8, KR, HALF), f32),
        pltpu.VMEM((SLABS, XL, NY), f32),
        pltpu.VMEM((2, NX + 2 * PAD, 8, NY), f32),
        pltpu.VMEM((2, NX + 2 * PAD, 16, NY), bf16),
        pltpu.VMEM((128, NX * NY), bf16),
        pltpu.VMEM((NX, 8, NY), f32),
        dma((XL,)),
        dma((XL, NB)),
        dma((ITERS, 2, 2, 3)),
        dma((ITERS, 2, 2, 3)),
        dma((ITERS, 2, 7)),
        dma((ITERS, 2, 7)),
        dma((3,)),
        dma((3,)),
        dma((ITERS, NB)),
        dma((ITERS, NB)),
        dma((ITERS, NB)),
        dma((ITERS, NB)),
    ]
    field, settled = pl.pallas_call(
        transport_kernel,
        out_shape=(
            jax.ShapeDtypeStruct((XL, *full), f32),
            jax.ShapeDtypeStruct((5, XL, NY), f32),
        ),
        in_specs=[hbm] + [vmem] * 5,
        out_specs=(hbm, vmem),
        scratch_shapes=scratch,
        compiler_params=pltpu.CompilerParams(
            collective_id=0, has_side_effects=True, vmem_limit_bytes=60 * 1024 * 1024
        ),
        name="transport",
    )(dist, speeds, weights[None], collision, wall_values, wall_kind)
    rows, settled = pl.pallas_call(
        order_kernel,
        grid=(NB,),
        out_shape=(
            jax.ShapeDtypeStruct((V * XL, NY), f32),
            jax.ShapeDtypeStruct((5, XL, NY), f32),
        ),
        in_specs=[
            pl.BlockSpec((XL, VB, NY), lambda i: (0, i, 0)),
            pl.BlockSpec((3, VB), lambda i: (0, i)),
            pl.BlockSpec((5, XL, NY), lambda i: (0, 0, 0)),
        ],
        out_specs=(
            pl.BlockSpec((VB * XL, NY), lambda i: (i, 0)),
            pl.BlockSpec((5, XL, NY), lambda i: (0, 0, 0)),
        ),
        name="order",
    )(field, speeds, settled)
    return rows.reshape(V, XL, NY), settled


def solution(mesh):
    return jax.shard_map(
        on_device,
        mesh=mesh,
        in_specs=(
            P("vel", "slab", None),
            P(None, "vel"),
            P("vel"),
            P("slab", None),
            P(None, "vel"),
            P(None, "vel"),
        ),
        out_specs=(P("vel", "slab", None), P(None, "slab", None)),
        check_vma=False,
    )
```

```python
import jax
import jax.numpy as jnp
from jax import lax
from jax.experimental import pallas as pl
from jax.experimental.pallas import tpu as pltpu
from jax.sharding import PartitionSpec as P

VELS = 24576
ITERS = 2
JACOBI = 2
NX = 16
NY = 128
SLABS = 4
XL = NX // SLABS
V = VELS // 32
VB = 128
NB = V // VB
PAD = NX - XL
KR = 16
ROWS = 13
LAG = 2
HALF = XL * NY // 2
STEPS = (1, 2, 4, 8, 16, 32, 64)

f32 = jnp.float32
bf16 = jnp.bfloat16
MESH = pl.DeviceIdType.MESH


def split(value):
    high = value.astype(bf16)
    return high, (value - high.astype(f32)).astype(bf16)


def dot(a, b):
    return jnp.dot(a, b, preferred_element_type=f32)


def lanes(shape):
    return lax.broadcasted_iota(jnp.int32, shape, 1)


def mirrored(value):
    return jnp.take_along_axis(value, NY - 1 - lanes(value.shape), axis=1)


def transport_kernel(
    dist, speeds_in, weights_in, collision_in, values_in, kind_in,
    out, settled_out,
    draw, gd, fhi, flo, fac, wgt, inv_own, prod, ycoef, ascale, bscale, fxs, fys,
    near, far, outa, outb, rows_t, rows_p, rows_g, shp, col,
    b1, b2, b3, cbuf, crow, dpad, rhs, drive_s,
    speeds, weights, collision, wall_values, wall_kind,
    dsem, ssem, bsend, brecv, ysend, yrecv, csend, crecv, nsend, nrecv, fsend, frecv,
):
    slab = lax.axis_index("slab")
    vel = lax.axis_index("vel")
    px = vel // 8
    py = (vel // 4) % 2
    pz = vel % 4
    edge = jnp.logical_or(slab == 0, slab == SLABS - 1)
    middle = jnp.logical_and(slab > 0, slab < SLABS - 1)
    low_side = slab < 2
    partner = jnp.where(low_side, 1 - slab, 5 - slab)
    across = 3 - slab

    def device(s, x, y, z):
        return {"slab": s, "vel": (x * 2 + y) * 4 + z}

    loads = [
        pltpu.make_async_copy(dist.at[:, x, :], draw.at[x], dsem.at[x]) for x in range(XL)
    ]
    small = [
        pltpu.make_async_copy(source, target, ssem.at[n])
        for n, (source, target) in enumerate((
            (speeds_in, speeds), (weights_in, weights), (collision_in, collision),
            (values_in, wall_values), (kind_in, wall_kind),
        ))
    ]
    for load in small + loads:
        load.start()

    peers = []
    for d in range(1, 4):
        peers.append(device(slab, (px + d) % 4, py, pz))
    for d in range(1, 4):
        peers.append(device(slab, px, py, (pz + d) % 4))
    group = py * 4 + slab
    yz = []
    for d in range(1, 8):
        other = (group + d) % 8
        yz.append(device(other % 4, px, other // 4, pz))
    barrier = pltpu.get_barrier_semaphore()
    for peer in peers + yz:
        pl.semaphore_signal(barrier, inc=1, device_id=peer, device_id_type=MESH)

    for load in small:
        load.wait()
    cx, cy, cz = speeds[0:1, :], speeds[1:2, :], speeds[2:3, :]
    wt = weights[...].reshape(1, V)
    square = cx * cx + cy * cy + cz * cz
    third = square / 3.0
    heat = square - 2.5
    one = jnp.ones_like(cx)
    zero = jnp.zeros_like(cx)
    phi = [
        one, cx, cy, cz, 2.0 / 3.0 * square - 1.0, cx * heat, cy * heat, cz * heat,
        cx * cx - third, cx * cy, cx * cz, cy * cy - third, cy * cz, zero, zero, zero,
    ]
    scale = wt / VELS
    fx = jnp.where(cx >= 0, 1.0, 0.0)
    fy = jnp.where(cy >= 0, 1.0, 0.0)
    rows = jnp.concatenate([p * scale for p in phi], axis=0)
    rows_hi, rows_lo = split(rows)
    rows_p[0:KR, :] = rows_hi
    rows_p[KR : 2 * KR, :] = rows_lo
    masks = [fx * fy, fx * (1.0 - fy), (1.0 - fx) * fy, (1.0 - fx) * (1.0 - fy)]
    for g in range(4):
        m = masks[g].astype(bf16)
        rows_g[g * KR : (g + 1) * KR, :] = rows_hi * m
        rows_g[4 * KR + g * KR : 4 * KR + (g + 1) * KR, :] = rows_lo * m

    for x in range(XL):
        loads[x].wait()
        def cast(i, c, x=x):
            at = pl.ds(i * VB, VB)
            hi, lo = split(draw[x, at, :])
            fhi[at, x * NY : (x + 1) * NY] = hi
            flo[at, x * NY : (x + 1) * NY] = lo
            return c
        lax.fori_loop(0, NB, cast, 0)
    first = dot(rows_p[...], fhi[...])
    moment = first[0:KR] + first[KR : 2 * KR] + dot(rows_p[0:KR, :], flo[...])

    pl.semaphore_wait(barrier, 13)

    axes = ((px, lambda o: device(slab, o, py, pz)), (pz, lambda o: device(slab, px, py, o)))

    def exchange(buf, stage, it, piece):
        me, to = axes[(stage + piece) % 2]
        sent = []
        for d in range(1, 4):
            copy = pltpu.make_async_remote_copy(
                src_ref=buf.at[it, piece, me],
                dst_ref=buf.at[it, piece, me],
                send_sem=bsend.at[it, stage, piece, d - 1],
                recv_sem=brecv.at[it, stage, piece, d - 1],
                device_id=to((me + d) % 4),
                device_id_type=MESH,
            )
            copy.start()
            sent.append(copy)
        return sent

    def arrived(buf, stage, it, piece):
        me, to = axes[(stage + piece) % 2]
        for d in range(1, 4):
            source = (me + 4 - d) % 4
            pltpu.make_async_remote_copy(
                src_ref=buf.at[it, piece, source],
                dst_ref=buf.at[it, piece, source],
                send_sem=bsend.at[it, stage, piece, d - 1],
                recv_sem=brecv.at[it, stage, piece, d - 1],
                device_id=to(source),
                device_id_type=MESH,
            ).wait_recv()
        return (buf[it, piece, 0] + buf[it, piece, 1]) + (buf[it, piece, 2] + buf[it, piece, 3])

    def spread(it, piece):
        sent = []
        for d in range(1, 8):
            copy = pltpu.make_async_remote_copy(
                src_ref=b3.at[it, piece, group],
                dst_ref=b3.at[it, piece, group],
                send_sem=ysend.at[it, piece, d - 1],
                recv_sem=yrecv.at[it, piece, d - 1],
                device_id=yz[d - 1],
                device_id_type=MESH,
            )
            copy.start()
            sent.append(copy)
        return sent

    def spread_arrived(it, piece):
        for d in range(1, 8):
            source = (group + 8 - d) % 8
            pltpu.make_async_remote_copy(
                src_ref=b3.at[it, piece, source],
                dst_ref=b3.at[it, piece, source],
                send_sem=ysend.at[it, piece, d - 1],
                recv_sem=yrecv.at[it, piece, d - 1],
                device_id=yz[d - 1],
                device_id_type=MESH,
            ).wait_recv()

    def start_reduce(it, value):
        sent = []
        for piece in range(2):
            b1[it, piece, axes[piece % 2][0]] = value[0:ROWS, piece * HALF : (piece + 1) * HALF]
            sent += exchange(b1, 0, it, piece)
        return sent

    def second_stage(it):
        sent = []
        for piece in range(2):
            total = arrived(b1, 0, it, piece)
            b2[it, piece, axes[(1 + piece) % 2][0]] = total
            sent += exchange(b2, 1, it, piece)
        return sent

    def third_stage(it):
        sent = []
        for piece in range(2):
            b3[it, piece, group] = arrived(b2, 1, it, piece)
            sent += spread(it, piece)
        return sent

    sent = start_reduce(0, moment)
    for d in range(1, 4):
        copy = pltpu.make_async_remote_copy(
            src_ref=collision,
            dst_ref=cbuf.at[slab],
            send_sem=csend.at[d - 1],
            recv_sem=crecv.at[d - 1],
            device_id=device((slab + d) % 4, px, py, pz),
            device_id_type=MESH,
        )
        copy.start()
        sent.append(copy)
    cbuf[slab] = collision[...]

    rows_t[...] = jnp.zeros_like(rows_t)
    inflow = wall_values[...] * wall_kind[...].astype(f32)
    rate_x = jnp.abs(cx) * NX
    rate_y = jnp.abs(cy) * NY
    rows_t[0:1, :] = rate_x
    rows_t[1:2, :] = rate_y / (1.0 + rate_y)
    rows_t[2:3, :] = 1.0 / (1.0 + rate_y)
    rows_t[3:4, :] = jnp.where(low_side, inflow[0:1], inflow[1:2])
    rows_t[4:5, :] = fx
    rows_t[5:6, :] = fy
    for i in range(NB):
        at = slice(i * VB, (i + 1) * VB)
        col[at, :] = jnp.transpose(rows_t[:, at])
    factor = 4.0 / 45.0 * heat
    psi = jnp.concatenate(
        [one, 2.0 * cx, 2.0 * cy, 2.0 * cz, square - 1.5, factor * cx, factor * cy, factor * cz],
        axis=0,
    )
    psi_hi = psi.astype(bf16).astype(f32)
    psi_lo = psi - psi_hi
    for g in range(4):
        rows_t[g * 32 : g * 32 + 8, :] = psi_hi * masks[g]
        rows_t[g * 32 + 8 : g * 32 + 16, :] = psi_hi * masks[g]
        rows_t[g * 32 + 16 : g * 32 + 24, :] = psi_lo * masks[g]
        rows_t[g * 32 + 24 : g * 32 + 32, :] = psi_lo * masks[g]
    for i in range(NB):
        at = slice(i * VB, (i + 1) * VB)
        shp[at, :] = jnp.transpose(rows_t[:, at]).astype(bf16)

    lane = lanes((VB, NY))

    def send_out(buf, target, send, recv, it, i, to):
        at = pl.ds(i * VB, VB)
        pltpu.make_async_remote_copy(
            src_ref=buf.at[it, at],
            dst_ref=target.at[it, at],
            send_sem=send.at[it, i],
            recv_sem=recv.at[it, i],
            device_id=device(to, px, py, pz),
            device_id_type=MESH,
        ).start()

    def wait_in(target, send, recv, it, i):
        at = pl.ds(i * VB, VB)
        pltpu.make_async_remote_copy(
            src_ref=target.at[it, at],
            dst_ref=target.at[it, at],
            send_sem=send.at[it, i],
            recv_sem=recv.at[it, i],
            device_id=device(partner, px, py, pz),
            device_id_type=MESH,
        ).wait_recv()

    def wait_out(buf, target, send, recv, it, i):
        at = pl.ds(i * VB, VB)
        pltpu.make_async_remote_copy(
            src_ref=buf.at[it, at],
            dst_ref=target.at[it, at],
            send_sem=send.at[it, i],
            recv_sem=recv.at[it, i],
            device_id=device(partner, px, py, pz),
            device_id_type=MESH,
        ).wait_send()

    own = collision[...]
    own_back = mirrored(jnp.concatenate([own, own], axis=0))

    def pass_on(it, i):
        at = pl.ds(i * VB, VB)
        wait_in(near, nsend, nrecv, it, i)
        outa[it, at, :] = prod[at, :] * near[it, at, :] + gd[XL - 1, at, :]
        send_out(outa, far, fsend, frecv, it, i, across)

    def sweep_source(fields, at, it, i):
        total = inv_own[0, at, :] * fields[0]
        gd[0, at, :] = total
        for q in range(1, XL):
            total = fac[PAD + q, at, :] * total + inv_own[q, at, :] * fields[q]
            gd[q, at, :] = total

        @pl.when(edge)
        def _():
            outa[it, at, :] = prod[at, :] * near[it, at, :] + total
            send_out(outa, near, nsend, nrecv, it, i, partner)

        @pl.when(jnp.logical_and(middle, i >= LAG))
        def _():
            pass_on(it, i - LAG)

    def prepare(i, c):
        at = pl.ds(i * VB, VB)
        cols = col[at, :]
        wide = lambda k: jnp.broadcast_to(cols[:, k : k + 1], (VB, NY))
        a = wide(0)
        ascale[at, :] = a
        power = wide(1)
        for k, step in enumerate(STEPS):
            ycoef[k, at, :] = jnp.where(lane >= step, power, 0.0)
            power = power * power
        bscale[at, :] = wide(2)
        fxv, fyv = wide(4), wide(5)
        fxs[at, :] = fxv
        fys[at, :] = fyv
        forward, upward = fxv > 0.5, fyv > 0.5

        @pl.when(edge)
        def _():
            for it in range(ITERS):
                near[it, at, :] = wide(3)

        index = jnp.where(upward, lane, NY - 1 - lane)
        product = None
        fields = []
        for q in range(XL):
            m = XL - 1 - q
            rate = jnp.where(
                forward,
                jnp.where(upward, own[q : q + 1], own_back[q : q + 1]),
                jnp.where(upward, own[m : m + 1], own_back[m : m + 1]),
            )
            inv = 1.0 / (1.0 + a + rate)
            f = a * inv
            inv_own[q, at, :] = inv
            fac[PAD + q, at, :] = f
            wgt[PAD + q, at, :] = rate * inv
            product = f if product is None else product * f
            picked = jnp.where(forward, draw[q, at, :], draw[m, at, :])
            fields.append(jnp.take_along_axis(picked, index, axis=1))
        prod[at, :] = product
        sweep_source(fields, at, 0, i)
        return c

    lax.fori_loop(0, NB, prepare, 0)

    def chain_across(it):
        @pl.when(middle)
        def _():
            def step(i, c):
                pass_on(it, i)
                return c
            lax.fori_loop(NB - LAG, NB, step, 0)

    def chain_back(it):
        @pl.when(middle)
        def _():
            def step(i, c):
                at = pl.ds(i * VB, VB)
                wait_in(far, fsend, frecv, it, i)
                outb[it, at, :] = prod[at, :] * far[it, at, :] + gd[XL - 1, at, :]
                pltpu.make_async_remote_copy(
                    src_ref=outb.at[it, at],
                    dst_ref=far.at[it, at],
                    send_sem=nsend.at[it, i],
                    recv_sem=frecv.at[it, i],
                    device_id=device(partner, px, py, pz),
                    device_id_type=MESH,
                ).start()
                return c
            lax.fori_loop(0, NB, step, 0)

    def drain_chain(it):
        @pl.when(middle)
        def _():
            def step(i, c):
                wait_out(outa, far, fsend, frecv, it, i)
                wait_out(outb, far, nsend, frecv, it, i)
                return c
            lax.fori_loop(0, NB, step, 0)

        @pl.when(edge)
        def _():
            def step(i, c):
                wait_out(outa, near, nsend, nrecv, it, i)
                return c
            lax.fori_loop(0, NB, step, 0)

    sent += second_stage(0)
    chain_across(0)

    for d in range(1, 4):
        source = (slab + 4 - d) % 4
        pltpu.make_async_remote_copy(
            src_ref=collision,
            dst_ref=cbuf.at[source],
            send_sem=csend.at[d - 1],
            recv_sem=crecv.at[d - 1],
            device_id=device(source, px, py, pz),
            device_id_type=MESH,
        ).wait_recv()
    crow[...] = jnp.zeros_like(crow)
    everywhere = jnp.concatenate([cbuf[s] for s in range(SLABS)], axis=0)
    turned = mirrored(everywhere)
    for i in range(NX):
        crow[0, PAD + i] = jnp.broadcast_to(everywhere[i : i + 1], (8, NY))
        crow[1, PAD + i] = jnp.broadcast_to(turned[i : i + 1], (8, NY))

    def upstream(start, stop):
        def at_cell(r, c):
            ahead = XL * slab + r
            behind = XL * slab + PAD + NX - 1 - r
            c_ff = crow[0, ahead][0:1]
            c_fb = crow[1, ahead][0:1]
            c_bf = crow[0, behind][0:1]
            c_bb = crow[1, behind][0:1]
            def block(i, c):
                at = pl.ds(i * VB, VB)
                a = ascale[at, :]
                forward, upward = fxs[at, :] > 0.5, fys[at, :] > 0.5
                rate = jnp.where(
                    forward, jnp.where(upward, c_ff, c_fb), jnp.where(upward, c_bf, c_bb)
                )
                inv = 1.0 / (1.0 + a + rate)
                fac[r, at, :] = a * inv
                wgt[r, at, :] = rate * inv
                return c
            lax.fori_loop(0, NB, block, 0)
            return c
        lax.fori_loop(start, stop, at_cell, 0)

    upstream(0, 5)
    sent += third_stage(0)
    chain_back(0)
    upstream(5, PAD)

    cell = lanes((8, NY))
    sub = lax.broadcasted_iota(jnp.int32, (8, NY), 0)

    def above(value):
        return jnp.where(cell < NY - 1, pltpu.roll(value, NY - 1, 1), 0.0)

    def below(value):
        return jnp.where(cell >= 1, pltpu.roll(value, 1, 1), 0.0)

    def macro(it):
        for piece in range(2):
            spread_arrived(it, piece)
        head, flux = [], []
        for i in range(NX):
            s, x = i // XL, i % XL
            piece, at = x // 2, slice((x % 2) * NY, (x % 2 + 1) * NY)
            head.append(b3[it, piece, s, 0:8, at] + b3[it, piece, 4 + s, 0:8, at])
            flux.append(b3[it, piece, s, 8:ROWS, at] + b3[it, piece, 4 + s, 8:ROWS, at])
        nothing = jnp.zeros((8, NY), f32)
        along = [
            jnp.concatenate([a[1:2], b[0:3], a[5:6], a[5:8]], axis=0) for a, b in zip(head, flux)
        ]
        target, kappa, down = [], [], []
        for i in range(NX):
            a, b = head[i], flux[i]
            cross = jnp.concatenate([a[2:3], b[1:2], b[3:5], a[6:7], a[5:8]], axis=0)
            right = along[i + 1] if i + 1 < NX else nothing
            left = along[i - 1] if i > 0 else nothing
            target.append(a - (0.5 * (right - left) + 0.5 * (above(cross) - below(cross))))
            stiff = 1.0 / crow[0, PAD + i]
            kappa.append(stiff)
            down.append(1.0 / (1.0 + 4.0 * stiff))
        settled = head
        for _ in range(JACOBI):
            after = []
            for i in range(NX):
                right = settled[i + 1] if i + 1 < NX else nothing
                left = settled[i - 1] if i > 0 else nothing
                around = right + left + above(settled[i]) + below(settled[i])
                after.append((target[i] + kappa[i] * around) * down[i])
            settled = after
        dpad[...] = jnp.zeros_like(dpad)
        for i in range(NX):
            drive = jnp.where(sub < 5, settled[i], head[i])
            drive_s[i] = drive
            hi, lo = split(drive)
            dpad[0, PAD + i] = jnp.concatenate([hi, lo], axis=0)
            hi, lo = split(mirrored(drive))
            dpad[1, PAD + i] = jnp.concatenate([hi, lo], axis=0)
        for r in range(NX):
            ahead = XL * slab + r
            behind = XL * slab + PAD + NX - 1 - r
            at = slice(r * NY, (r + 1) * NY)
            for g, tile in enumerate(
                (dpad[0, ahead], dpad[1, ahead], dpad[0, behind], dpad[1, behind])
            ):
                rhs[g * 32 : g * 32 + 16, at] = tile
                rhs[g * 32 + 16 : g * 32 + 32, at] = tile

    def main(it):
        last = it == ITERS - 1

        def block(i, c):
            at = pl.ds(i * VB, VB)
            eq = dot(shp[at, :], rhs[...])
            enter = wgt[0, at, :] * eq[:, 0:NY]
            for r in range(1, PAD):
                enter = fac[r, at, :] * enter + wgt[r, at, :] * eq[:, r * NY : (r + 1) * NY]

            @pl.when(edge)
            def _():
                wait_in(far, fsend, frecv, it, i)

            forward = fxs[at, :] > 0.5
            from_near = jnp.where(low_side, fxs[at, :], 1.0 - fxs[at, :]) > 0.5
            enter = enter + jnp.where(from_near, near[it, at, :], far[it, at, :])
            fields = []
            for q in range(XL):
                r = PAD + q
                enter = fac[r, at, :] * enter + wgt[r, at, :] * eq[:, r * NY : (r + 1) * NY]
                h = (gd[q, at, :] + enter) * bscale[at, :]
                for k, step in enumerate(STEPS):
                    h = h + ycoef[k, at, :] * pltpu.roll(h, step, 1)
                fields.append(h)
                if not last:
                    hi, lo = split(h)
                    fhi[at, q * NY : (q + 1) * NY] = hi
                    flo[at, q * NY : (q + 1) * NY] = lo
            if last:
                index = jnp.where(fys[at, :] > 0.5, lane, NY - 1 - lane)
                for x in range(XL):
                    picked = jnp.where(forward, fields[x], fields[XL - 1 - x])
                    out[pl.ds(i * VB * XL + x, VB, stride=XL), :] = jnp.take_along_axis(
                        picked, index, axis=1
                    )
            else:
                sweep_source(fields, at, it + 1, i)
            return c

        lax.fori_loop(0, NB, block, 0)

    for it in range(ITERS):
        macro(it)
        main(it)
        if it < ITERS - 1:
            first = dot(rows_g[...], fhi[...])
            groups = first[0 : 4 * KR] + first[4 * KR : 8 * KR] + dot(rows_g[0 : 4 * KR, :], flo[...])
            turn = lambda t: jnp.concatenate(
                [t[:, x * NY : (x + 1) * NY] for x in reversed(range(XL))], axis=1
            )
            up = groups[0:KR] + turn(groups[2 * KR : 3 * KR])
            down = groups[KR : 2 * KR] + turn(groups[3 * KR : 4 * KR])
            moment = up + jnp.concatenate(
                [mirrored(down[:, x * NY : (x + 1) * NY]) for x in range(XL)], axis=1
            )
            sent += start_reduce(it + 1, moment)
            chain_across(it + 1)
            sent += second_stage(it + 1)
            chain_back(it + 1)
            sent += third_stage(it + 1)

    for x in range(XL):
        settled_out[:, x, :] = drive_s[XL * slab + x][0:5]

    for it in range(ITERS):
        drain_chain(it)
    for copy in sent:
        copy.wait_send()


def on_device(dist, speeds, weights, collision, wall_values, wall_kind):
    vmem = pl.BlockSpec(memory_space=pltpu.VMEM)
    hbm = pl.BlockSpec(memory_space=pltpu.HBM)
    dma = pltpu.SemaphoreType.DMA
    full = (V, NY)
    scratch = [
        pltpu.VMEM((XL, *full), f32),
        pltpu.VMEM((XL, *full), f32),
        pltpu.VMEM((V, XL * NY), bf16),
        pltpu.VMEM((V, XL * NY), bf16),
        pltpu.VMEM((NX, *full), f32),
        pltpu.VMEM((NX, *full), f32),
        pltpu.VMEM((XL, *full), f32),
        pltpu.VMEM(full, f32),
        pltpu.VMEM((len(STEPS), *full), f32),
        pltpu.VMEM(full, f32),
        pltpu.VMEM(full, f32),
        pltpu.VMEM(full, f32),
        pltpu.VMEM(full, f32),
        pltpu.VMEM((ITERS, *full), f32),
        pltpu.VMEM((ITERS, *full), f32),
        pltpu.VMEM((ITERS, *full), f32),
        pltpu.VMEM((ITERS, *full), f32),
        pltpu.VMEM((128, V), f32),
        pltpu.VMEM((2 * KR, V), bf16),
        pltpu.VMEM((8 * KR, V), bf16),
        pltpu.VMEM((V, 128), bf16),
        pltpu.VMEM((V, 128), f32),
        pltpu.VMEM((ITERS, 2, 4, ROWS, HALF), f32),
        pltpu.VMEM((ITERS, 2, 4, ROWS, HALF), f32),
        pltpu.VMEM((ITERS, 2, 8, ROWS, HALF), f32),
        pltpu.VMEM((SLABS, XL, NY), f32),
        pltpu.VMEM((2, NX + 2 * PAD, 8, NY), f32),
        pltpu.VMEM((2, NX + 2 * PAD, 16, NY), bf16),
        pltpu.VMEM((128, NX * NY), bf16),
        pltpu.VMEM((NX, 8, NY), f32),
        pltpu.VMEM((3, V), f32),
        pltpu.VMEM((V,), f32),
        pltpu.VMEM((XL, NY), f32),
        pltpu.VMEM((2, V), f32),
        pltpu.VMEM((2, V), jnp.int32),
        dma((XL,)),
        dma((5,)),
        dma((ITERS, 2, 2, 3)),
        dma((ITERS, 2, 2, 3)),
        dma((ITERS, 2, 7)),
        dma((ITERS, 2, 7)),
        dma((3,)),
        dma((3,)),
        dma((ITERS, NB)),
        dma((ITERS, NB)),
        dma((ITERS, NB)),
        dma((ITERS, NB)),
    ]
    rows, settled = pl.pallas_call(
        transport_kernel,
        out_shape=(
            jax.ShapeDtypeStruct((V * XL, NY), f32),
            jax.ShapeDtypeStruct((5, XL, NY), f32),
        ),
        in_specs=[hbm] * 6,
        out_specs=(vmem, vmem),
        scratch_shapes=scratch,
        compiler_params=pltpu.CompilerParams(
            collective_id=0, has_side_effects=True, vmem_limit_bytes=50000000
        ),
        name="transport",
    )(*(
        pltpu.with_memory_space_constraint(value, pltpu.HBM)
        for value in (dist, speeds, weights, collision, wall_values, wall_kind)
    ))
    return rows.reshape(V, XL, NY), settled


def solution(mesh):
    return jax.shard_map(
        on_device,
        mesh=mesh,
        in_specs=(
            P("vel", "slab", None),
            P(None, "vel"),
            P("vel"),
            P("slab", None),
            P(None, "vel"),
            P(None, "vel"),
        ),
        out_specs=(P("vel", "slab", None), P(None, "slab", None)),
        check_vma=False,
    )
```

```python
import jax
import jax.numpy as jnp
from jax import lax
from jax.experimental import pallas as pl
from jax.experimental.pallas import tpu as pltpu
from jax.sharding import PartitionSpec as P

VELS = 24576
ITERS = 2
JACOBI = 2
NX = 16
NY = 128
SLABS = 4
XL = NX // SLABS
V = VELS // 32
VB = 128
NB = V // VB
CB = 256
NC = V // CB
PAD = NX - XL
KR = 16
ROWS = 13
LAG = 1
HALF = XL * NY // 2
SEG = NY // 8
TABLE = SEG + 4

f32 = jnp.float32
bf16 = jnp.bfloat16
MESH = pl.DeviceIdType.MESH


def split(value):
    high = value.astype(bf16)
    return high, (value - high.astype(f32)).astype(bf16)


def dot(a, b):
    return jnp.dot(a, b, preferred_element_type=f32)


def lanes(shape):
    return lax.broadcasted_iota(jnp.int32, shape, 1)


def pick(value, index):
    return jnp.take_along_axis(value, index, axis=1)


def cell_at(lane):
    return (lane % 8) * SEG + lane // 8


def lane_of(cell):
    return (cell % SEG) * 8 + cell // SEG


def swept(value):
    return pick(value, cell_at(lanes(value.shape)))


def swept_back(value):
    return pick(value, NY - 1 - cell_at(lanes(value.shape)))


def restored(value):
    return pick(value, lane_of(lanes(value.shape)))


def restored_back(value):
    return pick(value, lane_of(NY - 1 - lanes(value.shape)))


def transport_kernel(
    dist, speeds_in, weights_in, collision_in, values_in, kind_in,
    out, settled_out,
    draw, gd, fhi, flo, fac, wgt, inv_own, prod, yrow, ascale, fxs, fys,
    near, far, outa, outb, rows_t, rows_p, rows_g, shp, col,
    b1, b2, b3, cbuf, crow, dpad, rhs, drive_s,
    speeds, weights, collision, wall_values, wall_kind,
    dsem, ssem, bsend, brecv, ysend, yrecv, csend, crecv, nsend, nrecv, fsend, frecv,
):
    slab = lax.axis_index("slab")
    vel = lax.axis_index("vel")
    px = vel // 8
    py = (vel // 4) % 2
    pz = vel % 4
    edge = jnp.logical_or(slab == 0, slab == SLABS - 1)
    middle = jnp.logical_and(slab > 0, slab < SLABS - 1)
    low_side = slab < 2
    partner = jnp.where(low_side, 1 - slab, 5 - slab)
    across = 3 - slab
    beside = jnp.where(low_side, 2, 0)

    def device(s, x, y, z):
        return {"slab": s, "vel": (x * 2 + y) * 4 + z}

    loads = [
        pltpu.make_async_copy(dist.at[:, x, :], draw.at[x], dsem.at[x]) for x in range(XL)
    ]
    small = [
        pltpu.make_async_copy(source, target, ssem.at[n])
        for n, (source, target) in enumerate((
            (speeds_in, speeds), (weights_in, weights), (collision_in, collision),
            (values_in, wall_values), (kind_in, wall_kind),
        ))
    ]
    for load in small + loads:
        load.start()

    peers = []
    for d in range(1, 4):
        peers.append(device(slab, (px + d) % 4, py, pz))
    for d in range(1, 4):
        peers.append(device(slab, px, py, (pz + d) % 4))
    group = py * 4 + slab
    yz = []
    for d in range(1, 8):
        other = (group + d) % 8
        yz.append(device(other % 4, px, other // 4, pz))
    barrier = pltpu.get_barrier_semaphore()
    for peer in peers + yz:
        pl.semaphore_signal(barrier, inc=1, device_id=peer, device_id_type=MESH)

    for load in small:
        load.wait()
    cx, cy, cz = speeds[0:1, :], speeds[1:2, :], speeds[2:3, :]
    wt = weights[...].reshape(1, V)
    square = cx * cx + cy * cy + cz * cz
    third = square / 3.0
    heat = square - 2.5
    one = jnp.ones_like(cx)
    zero = jnp.zeros_like(cx)
    phi = [
        one, cx, cy, cz, 2.0 / 3.0 * square - 1.0, cx * heat, cy * heat, cz * heat,
        cx * cx - third, cx * cy, cx * cz, cy * cy - third, cy * cz, zero, zero, zero,
    ]
    scale = wt / VELS
    fx = jnp.where(cx >= 0, 1.0, 0.0)
    fy = jnp.where(cy >= 0, 1.0, 0.0)
    rows = jnp.concatenate([p * scale for p in phi], axis=0)
    rows_hi, rows_lo = split(rows)
    rows_p[0:KR, :] = rows_hi
    rows_p[KR : 2 * KR, :] = rows_lo
    masks = [fx * fy, fx * (1.0 - fy), (1.0 - fx) * fy, (1.0 - fx) * (1.0 - fy)]
    for g in range(4):
        m = masks[g].astype(bf16)
        rows_g[g * KR : (g + 1) * KR, :] = rows_hi * m
        rows_g[4 * KR + g * KR : 4 * KR + (g + 1) * KR, :] = rows_lo * m

    for x in range(XL):
        loads[x].wait()
        def cast(i, c, x=x):
            at = pl.ds(i * VB, VB)
            hi, lo = split(draw[x, at, :])
            fhi[at, x * NY : (x + 1) * NY] = hi
            flo[at, x * NY : (x + 1) * NY] = lo
            return c
        lax.fori_loop(0, NB, cast, 0)
    first = dot(rows_p[...], fhi[...])
    moment = first[0:KR] + first[KR : 2 * KR] + dot(rows_p[0:KR, :], flo[...])

    pl.semaphore_wait(barrier, 13)

    axes = ((px, lambda o: device(slab, o, py, pz)), (pz, lambda o: device(slab, px, py, o)))

    def exchange(buf, stage, it, piece):
        me, to = axes[(stage + piece) % 2]
        sent = []
        for d in range(1, 4):
            copy = pltpu.make_async_remote_copy(
                src_ref=buf.at[it, piece, me],
                dst_ref=buf.at[it, piece, me],
                send_sem=bsend.at[it, stage, piece, d - 1],
                recv_sem=brecv.at[it, stage, piece, d - 1],
                device_id=to((me + d) % 4),
                device_id_type=MESH,
            )
            copy.start()
            sent.append(copy)
        return sent

    def arrived(buf, stage, it, piece):
        me, to = axes[(stage + piece) % 2]
        for d in range(1, 4):
            source = (me + 4 - d) % 4
            pltpu.make_async_remote_copy(
                src_ref=buf.at[it, piece, source],
                dst_ref=buf.at[it, piece, source],
                send_sem=bsend.at[it, stage, piece, d - 1],
                recv_sem=brecv.at[it, stage, piece, d - 1],
                device_id=to(source),
                device_id_type=MESH,
            ).wait_recv()
        return (buf[it, piece, 0] + buf[it, piece, 1]) + (buf[it, piece, 2] + buf[it, piece, 3])

    def hand(it, piece, n, slot, y, s):
        index = (y * 4 + s + 8 - slot) % 8 - 1
        copy = pltpu.make_async_remote_copy(
            src_ref=b3.at[it, piece, slot],
            dst_ref=b3.at[it, piece, slot],
            send_sem=ysend.at[it, piece, n],
            recv_sem=yrecv.at[it, piece, index],
            device_id=device(s, px, y, pz),
            device_id_type=MESH,
        )
        copy.start()
        return copy

    def spread(it, piece):
        targets = [(1 - py, slab)]
        for y in (py, 1 - py):
            targets += [(y, beside), (y, beside + 1)]
        targets.append((py, partner))
        return [hand(it, piece, n, group, y, s) for n, (y, s) in enumerate(targets)]

    def forward_far(it):
        sent = []
        for piece in range(2):
            source = (group + 4) % 8
            pltpu.make_async_remote_copy(
                src_ref=b3.at[it, piece, source],
                dst_ref=b3.at[it, piece, source],
                send_sem=ysend.at[it, piece, 3],
                recv_sem=yrecv.at[it, piece, 3],
                device_id=yz[3],
                device_id_type=MESH,
            ).wait_recv()
            sent.append(hand(it, piece, 6, source, py, partner))
        return sent

    def spread_arrived(it, piece):
        for d in (1, 2, 3, 5, 6, 7):
            source = (group + 8 - d) % 8
            pltpu.make_async_remote_copy(
                src_ref=b3.at[it, piece, source],
                dst_ref=b3.at[it, piece, source],
                send_sem=ysend.at[it, piece, d - 1],
                recv_sem=yrecv.at[it, piece, d - 1],
                device_id=yz[d - 1],
                device_id_type=MESH,
            ).wait_recv()

    def start_reduce(it, value):
        sent = []
        for piece in range(2):
            b1[it, piece, axes[piece % 2][0]] = value[0:ROWS, piece * HALF : (piece + 1) * HALF]
            sent += exchange(b1, 0, it, piece)
        return sent

    def second_stage(it):
        sent = []
        for piece in range(2):
            total = arrived(b1, 0, it, piece)
            b2[it, piece, axes[(1 + piece) % 2][0]] = total
            sent += exchange(b2, 1, it, piece)
        return sent

    def third_stage(it):
        sent = []
        for piece in range(2):
            b3[it, piece, group] = arrived(b2, 1, it, piece)
            sent += spread(it, piece)
        return sent

    sent = start_reduce(0, moment)
    for d in range(1, 4):
        copy = pltpu.make_async_remote_copy(
            src_ref=collision,
            dst_ref=cbuf.at[slab],
            send_sem=csend.at[d - 1],
            recv_sem=crecv.at[d - 1],
            device_id=device((slab + d) % 4, px, py, pz),
            device_id_type=MESH,
        )
        copy.start()
        sent.append(copy)
    cbuf[slab] = collision[...]

    rows_t[...] = jnp.zeros_like(rows_t)
    inflow = wall_values[...] * wall_kind[...].astype(f32)
    rate_x = jnp.abs(cx) * NX
    rate_y = jnp.abs(cy) * NY
    rows_t[0:1, :] = rate_x
    ratio = rate_y / (1.0 + rate_y)
    powers = [ratio]
    for _ in range(SEG - 1):
        powers.append(powers[-1] * ratio)
    powers.append(powers[-1] * powers[-1])
    powers.append(powers[-1] * powers[-1])
    powers += [zero, 1.0 / (1.0 + rate_y)]
    for n, power in enumerate(powers):
        for i in range(NB):
            yrow[i, n : n + 1, :] = power[:, i * VB : (i + 1) * VB]
    rows_t[3:4, :] = jnp.where(low_side, inflow[0:1], inflow[1:2])
    rows_t[4:5, :] = fx
    rows_t[5:6, :] = fy
    for i in range(NB):
        at = slice(i * VB, (i + 1) * VB)
        col[at, :] = jnp.transpose(rows_t[:, at])
    factor = 4.0 / 45.0 * heat
    psi = jnp.concatenate(
        [one, 2.0 * cx, 2.0 * cy, 2.0 * cz, square - 1.5, factor * cx, factor * cy, factor * cz],
        axis=0,
    )
    psi_hi = psi.astype(bf16).astype(f32)
    psi_lo = psi - psi_hi
    for g in range(4):
        rows_t[g * 32 : g * 32 + 8, :] = psi_hi * masks[g]
        rows_t[g * 32 + 8 : g * 32 + 16, :] = psi_hi * masks[g]
        rows_t[g * 32 + 16 : g * 32 + 24, :] = psi_lo * masks[g]
        rows_t[g * 32 + 24 : g * 32 + 32, :] = psi_lo * masks[g]
    for i in range(NB):
        at = slice(i * VB, (i + 1) * VB)
        shp[at, :] = jnp.transpose(rows_t[:, at]).astype(bf16)

    lane = lanes((VB, NY))

    def send_out(buf, target, send, recv, it, i, to):
        at = pl.ds(i * CB, CB)
        pltpu.make_async_remote_copy(
            src_ref=buf.at[it, at],
            dst_ref=target.at[it, at],
            send_sem=send.at[it, i],
            recv_sem=recv.at[it, i],
            device_id=device(to, px, py, pz),
            device_id_type=MESH,
        ).start()

    def wait_in(target, send, recv, it, i):
        at = pl.ds(i * CB, CB)
        pltpu.make_async_remote_copy(
            src_ref=target.at[it, at],
            dst_ref=target.at[it, at],
            send_sem=send.at[it, i],
            recv_sem=recv.at[it, i],
            device_id=device(partner, px, py, pz),
            device_id_type=MESH,
        ).wait_recv()

    def wait_out(buf, target, send, recv, it, i):
        at = pl.ds(i * CB, CB)
        pltpu.make_async_remote_copy(
            src_ref=buf.at[it, at],
            dst_ref=target.at[it, at],
            send_sem=send.at[it, i],
            recv_sem=recv.at[it, i],
            device_id=device(partner, px, py, pz),
            device_id_type=MESH,
        ).wait_send()

    twice = jnp.concatenate([collision[...], collision[...]], axis=0)
    own, own_back = swept(twice), swept_back(twice)

    def pass_on(it, i):
        at = pl.ds(i * CB, CB)
        wait_in(near, nsend, nrecv, it, i)
        outa[it, at, :] = prod[at, :] * near[it, at, :] + gd[XL - 1, at, :]
        send_out(outa, far, fsend, frecv, it, i, across)

    def sweep_source(fields, at):
        total = inv_own[0, at, :] * fields[0]
        gd[0, at, :] = total
        for q in range(1, XL):
            total = fac[PAD + q, at, :] * total + inv_own[q, at, :] * fields[q]
            gd[q, at, :] = total

    def chain_step(it, c):
        @pl.when(edge)
        def _():
            at = pl.ds(c * CB, CB)
            outa[it, at, :] = prod[at, :] * near[it, at, :] + gd[XL - 1, at, :]
            send_out(outa, near, nsend, nrecv, it, c, partner)

        @pl.when(jnp.logical_and(middle, c >= LAG))
        def _():
            pass_on(it, c - LAG)

    def in_groups(block, it):
        def group_of(c, carry):
            lax.fori_loop(c * (CB // VB), (c + 1) * (CB // VB), block, 0)
            if it is not None:
                chain_step(it, c)
            return carry
        lax.fori_loop(0, NC, group_of, 0)

    def prepare(i, c):
        at = pl.ds(i * VB, VB)
        cols = col[at, :]
        wide = lambda k: jnp.broadcast_to(cols[:, k : k + 1], (VB, NY))
        a = wide(0)
        ascale[at, :] = a
        fxv, fyv = wide(4), wide(5)
        fxs[at, :] = fxv
        fys[at, :] = fyv
        forward, upward = fxv > 0.5, fyv > 0.5

        @pl.when(edge)
        def _():
            for it in range(ITERS):
                near[it, at, :] = wide(3)

        index = jnp.where(upward, cell_at(lane), NY - 1 - cell_at(lane))
        product = None
        fields = []
        for q in range(XL):
            m = XL - 1 - q
            rate = jnp.where(
                forward,
                jnp.where(upward, own[q : q + 1], own_back[q : q + 1]),
                jnp.where(upward, own[m : m + 1], own_back[m : m + 1]),
            )
            inv = 1.0 / (1.0 + a + rate)
            f = a * inv
            inv_own[q, at, :] = inv
            fac[PAD + q, at, :] = f
            wgt[PAD + q, at, :] = rate * inv
            product = f if product is None else product * f
            picked = jnp.where(forward, draw[q, at, :], draw[m, at, :])
            fields.append(jnp.take_along_axis(picked, index, axis=1))
        prod[at, :] = product
        sweep_source(fields, at)
        return c

    in_groups(prepare, 0)

    def chain_across(it):
        @pl.when(middle)
        def _():
            def step(i, c):
                pass_on(it, i)
                return c
            lax.fori_loop(NC - LAG, NC, step, 0)

    def chain_back(it):
        @pl.when(middle)
        def _():
            def step(i, c):
                at = pl.ds(i * CB, CB)
                wait_in(far, fsend, frecv, it, i)
                outb[it, at, :] = prod[at, :] * far[it, at, :] + gd[XL - 1, at, :]
                pltpu.make_async_remote_copy(
                    src_ref=outb.at[it, at],
                    dst_ref=far.at[it, at],
                    send_sem=nsend.at[it, i],
                    recv_sem=frecv.at[it, i],
                    device_id=device(partner, px, py, pz),
                    device_id_type=MESH,
                ).start()
                return c
            lax.fori_loop(0, NC, step, 0)

    def drain_chain(it):
        @pl.when(middle)
        def _():
            def step(i, c):
                wait_out(outa, far, fsend, frecv, it, i)
                wait_out(outb, far, nsend, frecv, it, i)
                return c
            lax.fori_loop(0, NC, step, 0)

        @pl.when(edge)
        def _():
            def step(i, c):
                wait_out(outa, near, nsend, nrecv, it, i)
                return c
            lax.fori_loop(0, NC, step, 0)

    sent += second_stage(0)
    chain_across(0)

    for d in range(1, 4):
        source = (slab + 4 - d) % 4
        pltpu.make_async_remote_copy(
            src_ref=collision,
            dst_ref=cbuf.at[source],
            send_sem=csend.at[d - 1],
            recv_sem=crecv.at[d - 1],
            device_id=device(source, px, py, pz),
            device_id_type=MESH,
        ).wait_recv()
    crow[...] = jnp.zeros_like(crow)
    everywhere = jnp.concatenate([cbuf[s] for s in range(SLABS)], axis=0)
    ahead_rows, back_rows = swept(everywhere), swept_back(everywhere)
    for i in range(NX):
        for n, source in enumerate((ahead_rows, back_rows, everywhere)):
            crow[n, PAD + i] = jnp.broadcast_to(source[i : i + 1], (8, NY))

    def upstream(start, stop):
        def at_cell(r, c):
            ahead = XL * slab + r
            behind = XL * slab + PAD + NX - 1 - r
            c_ff = crow[0, ahead][0:1]
            c_fb = crow[1, ahead][0:1]
            c_bf = crow[0, behind][0:1]
            c_bb = crow[1, behind][0:1]
            def block(i, c):
                at = pl.ds(i * VB, VB)
                a = ascale[at, :]
                forward, upward = fxs[at, :] > 0.5, fys[at, :] > 0.5
                rate = jnp.where(
                    forward, jnp.where(upward, c_ff, c_fb), jnp.where(upward, c_bf, c_bb)
                )
                inv = 1.0 / (1.0 + a + rate)
                fac[r, at, :] = a * inv
                wgt[r, at, :] = rate * inv
                return c
            lax.fori_loop(0, NB, block, 0)
            return c
        lax.fori_loop(start, stop, at_cell, 0)

    upstream(0, 5)
    sent += third_stage(0)
    chain_back(0)
    upstream(5, PAD)
    sent += forward_far(0)

    cell = lanes((8, NY))
    sub = lax.broadcasted_iota(jnp.int32, (8, NY), 0)

    def above(value):
        return jnp.where(cell < NY - 1, pltpu.roll(value, NY - 1, 1), 0.0)

    def below(value):
        return jnp.where(cell >= 1, pltpu.roll(value, 1, 1), 0.0)

    def macro(it):
        for piece in range(2):
            spread_arrived(it, piece)
        head, flux = [], []
        for i in range(NX):
            s, x = i // XL, i % XL
            piece, at = x // 2, slice((x % 2) * NY, (x % 2 + 1) * NY)
            head.append(b3[it, piece, s, 0:8, at] + b3[it, piece, 4 + s, 0:8, at])
            flux.append(b3[it, piece, s, 8:ROWS, at] + b3[it, piece, 4 + s, 8:ROWS, at])
        nothing = jnp.zeros((8, NY), f32)
        along = [
            jnp.concatenate([a[1:2], b[0:3], a[5:6], a[5:8]], axis=0) for a, b in zip(head, flux)
        ]
        target, kappa, down = [], [], []
        for i in range(NX):
            a, b = head[i], flux[i]
            cross = jnp.concatenate([a[2:3], b[1:2], b[3:5], a[6:7], a[5:8]], axis=0)
            right = along[i + 1] if i + 1 < NX else nothing
            left = along[i - 1] if i > 0 else nothing
            target.append(a - (0.5 * (right - left) + 0.5 * (above(cross) - below(cross))))
            stiff = 1.0 / crow[2, PAD + i]
            kappa.append(stiff)
            down.append(1.0 / (1.0 + 4.0 * stiff))
        settled = head
        for _ in range(JACOBI):
            after = []
            for i in range(NX):
                right = settled[i + 1] if i + 1 < NX else nothing
                left = settled[i - 1] if i > 0 else nothing
                around = right + left + above(settled[i]) + below(settled[i])
                after.append((target[i] + kappa[i] * around) * down[i])
            settled = after
        dpad[...] = jnp.zeros_like(dpad)
        for i in range(NX):
            drive = jnp.where(sub < 5, settled[i], head[i])
            drive_s[i] = drive
            hi, lo = split(swept(drive))
            dpad[0, PAD + i] = jnp.concatenate([hi, lo], axis=0)
            hi, lo = split(swept_back(drive))
            dpad[1, PAD + i] = jnp.concatenate([hi, lo], axis=0)
        for r in range(NX):
            ahead = XL * slab + r
            behind = XL * slab + PAD + NX - 1 - r
            at = slice(r * NY, (r + 1) * NY)
            for g, tile in enumerate(
                (dpad[0, ahead], dpad[1, ahead], dpad[0, behind], dpad[1, behind])
            ):
                rhs[g * 32 : g * 32 + 16, at] = tile
                rhs[g * 32 + 16 : g * 32 + 32, at] = tile

    segment = lax.broadcasted_iota(jnp.int32, (8, NY), 0)

    def along_y(g, table):
        columns = jnp.transpose(g)
        ratio, scale = table[0:1], table[SEG + 3 : SEG + 4]
        inner = []
        for t in range(SEG):
            h = columns[8 * t : 8 * t + 8] * scale
            inner.append(h + ratio * inner[-1] if t else h)
        ends = inner[-1]
        for n, step in enumerate((1, 2, 4)):
            moved = jnp.where(segment >= step, pltpu.roll(ends, step, 0), 0.0)
            k = SEG - 1 + n
            ends = ends + table[k : k + 1] * moved
        carry = jnp.where(segment >= 1, pltpu.roll(ends, 1, 0), 0.0)
        whole = [inner[t] + table[t : t + 1] * carry for t in range(SEG)]
        return jnp.transpose(jnp.concatenate(whole, axis=0))

    def main(it):
        last = it == ITERS - 1

        @pl.when(edge)
        def _():
            def ready(i, c):
                wait_in(far, fsend, frecv, it, i)
                return c
            lax.fori_loop(0, NC, ready, 0)

        def block(i, c):
            at = pl.ds(i * VB, VB)
            eq = dot(shp[at, :], rhs[...])
            enter = wgt[0, at, :] * eq[:, 0:NY]
            for r in range(1, PAD):
                enter = fac[r, at, :] * enter + wgt[r, at, :] * eq[:, r * NY : (r + 1) * NY]
            forward = fxs[at, :] > 0.5
            from_near = jnp.where(low_side, fxs[at, :], 1.0 - fxs[at, :]) > 0.5
            enter = enter + jnp.where(from_near, near[it, at, :], far[it, at, :])
            fields = []
            for q in range(XL):
                r = PAD + q
                enter = fac[r, at, :] * enter + wgt[r, at, :] * eq[:, r * NY : (r + 1) * NY]
                h = along_y(gd[q, at, :] + enter, yrow[i])
                fields.append(h)
                if not last:
                    hi, lo = split(h)
                    fhi[at, q * NY : (q + 1) * NY] = hi
                    flo[at, q * NY : (q + 1) * NY] = lo
            if last:
                index = jnp.where(fys[at, :] > 0.5, lane_of(lane), lane_of(NY - 1 - lane))
                for x in range(XL):
                    picked = jnp.where(forward, fields[x], fields[XL - 1 - x])
                    out[pl.ds(i * VB * XL + x, VB, stride=XL), :] = jnp.take_along_axis(
                        picked, index, axis=1
                    )
            else:
                sweep_source(fields, at)
            return c

        in_groups(block, None if last else it + 1)

    for it in range(ITERS):
        macro(it)
        main(it)
        if it < ITERS - 1:
            first = dot(rows_g[...], fhi[...])
            groups = first[0 : 4 * KR] + first[4 * KR : 8 * KR] + dot(rows_g[0 : 4 * KR, :], flo[...])
            turn = lambda t: jnp.concatenate(
                [t[:, x * NY : (x + 1) * NY] for x in reversed(range(XL))], axis=1
            )
            up = groups[0:KR] + turn(groups[2 * KR : 3 * KR])
            down = groups[KR : 2 * KR] + turn(groups[3 * KR : 4 * KR])
            spans = [slice(x * NY, (x + 1) * NY) for x in range(XL)]
            moment = jnp.concatenate(
                [restored(up[:, at]) + restored_back(down[:, at]) for at in spans], axis=1
            )
            sent += start_reduce(it + 1, moment)
            chain_across(it + 1)
            sent += second_stage(it + 1)
            chain_back(it + 1)
            sent += third_stage(it + 1)
            sent += forward_far(it + 1)

    for x in range(XL):
        settled_out[:, x, :] = drive_s[XL * slab + x][0:5]

    for it in range(ITERS):
        drain_chain(it)
    for copy in sent:
        copy.wait_send()


def on_device(dist, speeds, weights, collision, wall_values, wall_kind):
    vmem = pl.BlockSpec(memory_space=pltpu.VMEM)
    hbm = pl.BlockSpec(memory_space=pltpu.HBM)
    dma = pltpu.SemaphoreType.DMA
    full = (V, NY)
    scratch = [
        pltpu.VMEM((XL, *full), f32),
        pltpu.VMEM((XL, *full), f32),
        pltpu.VMEM((V, XL * NY), bf16),
        pltpu.VMEM((V, XL * NY), bf16),
        pltpu.VMEM((NX, *full), f32),
        pltpu.VMEM((NX, *full), f32),
        pltpu.VMEM((XL, *full), f32),
        pltpu.VMEM(full, f32),
        pltpu.VMEM((NB, TABLE, VB), f32),
        pltpu.VMEM(full, f32),
        pltpu.VMEM(full, f32),
        pltpu.VMEM(full, f32),
        pltpu.VMEM((ITERS, *full), f32),
        pltpu.VMEM((ITERS, *full), f32),
        pltpu.VMEM((ITERS, *full), f32),
        pltpu.VMEM((ITERS, *full), f32),
        pltpu.VMEM((128, V), f32),
        pltpu.VMEM((2 * KR, V), bf16),
        pltpu.VMEM((8 * KR, V), bf16),
        pltpu.VMEM((V, 128), bf16),
        pltpu.VMEM((V, 128), f32),
        pltpu.VMEM((ITERS, 2, 4, ROWS, HALF), f32),
        pltpu.VMEM((ITERS, 2, 4, ROWS, HALF), f32),
        pltpu.VMEM((ITERS, 2, 8, ROWS, HALF), f32),
        pltpu.VMEM((SLABS, XL, NY), f32),
        pltpu.VMEM((3, NX + 2 * PAD, 8, NY), f32),
        pltpu.VMEM((2, NX + 2 * PAD, 16, NY), bf16),
        pltpu.VMEM((128, NX * NY), bf16),
        pltpu.VMEM((NX, 8, NY), f32),
        pltpu.VMEM((3, V), f32),
        pltpu.VMEM((V,), f32),
        pltpu.VMEM((XL, NY), f32),
        pltpu.VMEM((2, V), f32),
        pltpu.VMEM((2, V), jnp.int32),
        dma((XL,)),
        dma((5,)),
        dma((ITERS, 2, 2, 3)),
        dma((ITERS, 2, 2, 3)),
        dma((ITERS, 2, 7)),
        dma((ITERS, 2, 7)),
        dma((3,)),
        dma((3,)),
        dma((ITERS, NC)),
        dma((ITERS, NC)),
        dma((ITERS, NC)),
        dma((ITERS, NC)),
    ]
    rows, settled = pl.pallas_call(
        transport_kernel,
        out_shape=(
            jax.ShapeDtypeStruct((V * XL, NY), f32),
            jax.ShapeDtypeStruct((5, XL, NY), f32),
        ),
        in_specs=[hbm] * 6,
        out_specs=(vmem, vmem),
        scratch_shapes=scratch,
        compiler_params=pltpu.CompilerParams(
            collective_id=0, has_side_effects=True, vmem_limit_bytes=50000000
        ),
        name="transport",
    )(*(
        pltpu.with_memory_space_constraint(value, pltpu.HBM)
        for value in (dist, speeds, weights, collision, wall_values, wall_kind)
    ))
    return rows.reshape(V, XL, NY), settled


def solution(mesh):
    return jax.shard_map(
        on_device,
        mesh=mesh,
        in_specs=(
            P("vel", "slab", None),
            P(None, "vel"),
            P("vel"),
            P("slab", None),
            P(None, "vel"),
            P(None, "vel"),
        ),
        out_specs=(P("vel", "slab", None), P(None, "slab", None)),
        check_vma=False,
    )
```

```python
import jax
import jax.numpy as jnp
from jax import lax
from jax.experimental import pallas as pl
from jax.experimental.pallas import tpu as pltpu
from jax.sharding import PartitionSpec as P

VELS = 24576
ITERS = 2
JACOBI = 2
NX = 16
NY = 128
SLABS = 4
XL = NX // SLABS
V = VELS // 32
VB = 128
NB = V // VB
CB = 256
NC = V // CB
PAD = NX - XL
KR = 16
ROWS = 13
LAG = 1
HALF = XL * NY // 2
SEG = NY // 8
TABLE = SEG + 4

f32 = jnp.float32
bf16 = jnp.bfloat16
MESH = pl.DeviceIdType.MESH


def split(value):
    high = value.astype(bf16)
    return high, (value - high.astype(f32)).astype(bf16)


def dot(a, b):
    return jnp.dot(a, b, preferred_element_type=f32)


def lanes(shape):
    return lax.broadcasted_iota(jnp.int32, shape, 1)


def pick(value, index):
    return jnp.take_along_axis(value, index, axis=1)


def cell_at(lane):
    return (lane % 8) * SEG + lane // 8


def lane_of(cell):
    return (cell % SEG) * 8 + cell // SEG


def swept(value):
    return pick(value, cell_at(lanes(value.shape)))


def swept_back(value):
    return pick(value, NY - 1 - cell_at(lanes(value.shape)))


def restored(value):
    return pick(value, lane_of(lanes(value.shape)))


def restored_back(value):
    return pick(value, lane_of(NY - 1 - lanes(value.shape)))


def transport_kernel(
    dist, speeds_in, weights_in, collision_in, values_in, kind_in,
    out, settled_out,
    draw, gd, fhi, flo, fac, wgt, inv_own, prod, yrow, ascale, fxs, fys,
    near, far, outa, outb, rows_t, rows_p, rows_g, shp, col,
    b1, b2, b3, cbuf, crow, dpad, rhs, drive_s,
    speeds, weights, collision, wall_values, wall_kind,
    dsem, ssem, bsend, brecv, ysend, yrecv, csend, crecv, nsend, nrecv, fsend, frecv,
):
    slab = lax.axis_index("slab")
    vel = lax.axis_index("vel")
    px = vel // 8
    py = (vel // 4) % 2
    pz = vel % 4
    edge = jnp.logical_or(slab == 0, slab == SLABS - 1)
    middle = jnp.logical_and(slab > 0, slab < SLABS - 1)
    low_side = slab < 2
    partner = jnp.where(low_side, 1 - slab, 5 - slab)
    across = 3 - slab
    beside = jnp.where(low_side, 2, 0)

    def device(s, x, y, z):
        return {"slab": s, "vel": (x * 2 + y) * 4 + z}

    loads = [
        pltpu.make_async_copy(
            dist.at[pl.ds(i * VB * XL, VB * XL)], draw.at[pl.ds(i * VB * XL, VB * XL)], dsem.at[i]
        )
        for i in range(NB)
    ]
    small = [
        pltpu.make_async_copy(source, target, ssem.at[n])
        for n, (source, target) in enumerate((
            (speeds_in, speeds), (weights_in, weights), (collision_in, collision),
            (values_in, wall_values), (kind_in, wall_kind),
        ))
    ]
    for load in small + loads:
        load.start()

    peers = []
    for d in range(1, 4):
        peers.append(device(slab, (px + d) % 4, py, pz))
    for d in range(1, 4):
        peers.append(device(slab, px, py, (pz + d) % 4))
    group = py * 4 + slab
    yz = []
    for d in range(1, 8):
        other = (group + d) % 8
        yz.append(device(other % 4, px, other // 4, pz))
    barrier = pltpu.get_barrier_semaphore()
    for peer in peers + yz:
        pl.semaphore_signal(barrier, inc=1, device_id=peer, device_id_type=MESH)

    for load in small:
        load.wait()
    cx, cy, cz = speeds[0:1, :], speeds[1:2, :], speeds[2:3, :]
    wt = weights[...].reshape(1, V)
    square = cx * cx + cy * cy + cz * cz
    third = square / 3.0
    heat = square - 2.5
    one = jnp.ones_like(cx)
    zero = jnp.zeros_like(cx)
    phi = [
        one, cx, cy, cz, 2.0 / 3.0 * square - 1.0, cx * heat, cy * heat, cz * heat,
        cx * cx - third, cx * cy, cx * cz, cy * cy - third, cy * cz, zero, zero, zero,
    ]
    scale = wt / VELS
    fx = jnp.where(cx >= 0, 1.0, 0.0)
    fy = jnp.where(cy >= 0, 1.0, 0.0)
    rows = jnp.concatenate([p * scale for p in phi], axis=0)
    rows_hi, rows_lo = split(rows)
    rows_p[0:KR, :] = rows_hi
    rows_p[KR : 2 * KR, :] = rows_lo
    masks = [fx * fy, fx * (1.0 - fy), (1.0 - fx) * fy, (1.0 - fx) * (1.0 - fy)]
    for g in range(4):
        m = masks[g].astype(bf16)
        rows_g[g * KR : (g + 1) * KR, :] = rows_hi * m
        rows_g[4 * KR + g * KR : 4 * KR + (g + 1) * KR, :] = rows_lo * m

    def cast(i, c):
        at = pl.ds(i * VB, VB)
        rows_at = pl.ds(i * VB * XL, VB * XL)
        pltpu.make_async_copy(dist.at[rows_at], draw.at[rows_at], dsem.at[i]).wait()
        for x in range(XL):
            hi, lo = split(draw[pl.ds(i * VB * XL + x, VB, stride=XL), :])
            fhi[at, x * NY : (x + 1) * NY] = hi
            flo[at, x * NY : (x + 1) * NY] = lo
        return c

    lax.fori_loop(0, NB, cast, 0)
    first = dot(rows_p[...], fhi[...])
    moment = first[0:KR] + first[KR : 2 * KR] + dot(rows_p[0:KR, :], flo[...])

    pl.semaphore_wait(barrier, 13)

    axes = ((px, lambda o: device(slab, o, py, pz)), (pz, lambda o: device(slab, px, py, o)))

    def exchange(buf, stage, it, piece):
        me, to = axes[(stage + piece) % 2]
        sent = []
        for d in range(1, 4):
            copy = pltpu.make_async_remote_copy(
                src_ref=buf.at[it, piece, me],
                dst_ref=buf.at[it, piece, me],
                send_sem=bsend.at[it, stage, piece, d - 1],
                recv_sem=brecv.at[it, stage, piece, d - 1],
                device_id=to((me + d) % 4),
                device_id_type=MESH,
            )
            copy.start()
            sent.append(copy)
        return sent

    def arrived(buf, stage, it, piece):
        me, to = axes[(stage + piece) % 2]
        for d in range(1, 4):
            source = (me + 4 - d) % 4
            pltpu.make_async_remote_copy(
                src_ref=buf.at[it, piece, source],
                dst_ref=buf.at[it, piece, source],
                send_sem=bsend.at[it, stage, piece, d - 1],
                recv_sem=brecv.at[it, stage, piece, d - 1],
                device_id=to(source),
                device_id_type=MESH,
            ).wait_recv()
        return (buf[it, piece, 0] + buf[it, piece, 1]) + (buf[it, piece, 2] + buf[it, piece, 3])

    def hand(it, piece, n, slot, y, s):
        index = (y * 4 + s + 8 - slot) % 8 - 1
        copy = pltpu.make_async_remote_copy(
            src_ref=b3.at[it, piece, slot],
            dst_ref=b3.at[it, piece, slot],
            send_sem=ysend.at[it, piece, n],
            recv_sem=yrecv.at[it, piece, index],
            device_id=device(s, px, y, pz),
            device_id_type=MESH,
        )
        copy.start()
        return copy

    def spread(it, piece):
        targets = [(1 - py, slab)]
        for y in (py, 1 - py):
            targets += [(y, beside), (y, beside + 1)]
        targets.append((py, partner))
        return [hand(it, piece, n, group, y, s) for n, (y, s) in enumerate(targets)]

    def forward_far(it):
        sent = []
        for piece in range(2):
            source = (group + 4) % 8
            pltpu.make_async_remote_copy(
                src_ref=b3.at[it, piece, source],
                dst_ref=b3.at[it, piece, source],
                send_sem=ysend.at[it, piece, 3],
                recv_sem=yrecv.at[it, piece, 3],
                device_id=yz[3],
                device_id_type=MESH,
            ).wait_recv()
            sent.append(hand(it, piece, 6, source, py, partner))
        return sent

    def spread_arrived(it, piece):
        for d in (1, 2, 3, 5, 6, 7):
            source = (group + 8 - d) % 8
            pltpu.make_async_remote_copy(
                src_ref=b3.at[it, piece, source],
                dst_ref=b3.at[it, piece, source],
                send_sem=ysend.at[it, piece, d - 1],
                recv_sem=yrecv.at[it, piece, d - 1],
                device_id=yz[d - 1],
                device_id_type=MESH,
            ).wait_recv()

    def start_reduce(it, value):
        sent = []
        for piece in range(2):
            b1[it, piece, axes[piece % 2][0]] = value[0:ROWS, piece * HALF : (piece + 1) * HALF]
            sent += exchange(b1, 0, it, piece)
        return sent

    def second_stage(it):
        sent = []
        for piece in range(2):
            total = arrived(b1, 0, it, piece)
            b2[it, piece, axes[(1 + piece) % 2][0]] = total
            sent += exchange(b2, 1, it, piece)
        return sent

    def third_stage(it):
        sent = []
        for piece in range(2):
            b3[it, piece, group] = arrived(b2, 1, it, piece)
            sent += spread(it, piece)
        return sent

    sent = start_reduce(0, moment)
    for d in range(1, 4):
        copy = pltpu.make_async_remote_copy(
            src_ref=collision,
            dst_ref=cbuf.at[slab],
            send_sem=csend.at[d - 1],
            recv_sem=crecv.at[d - 1],
            device_id=device((slab + d) % 4, px, py, pz),
            device_id_type=MESH,
        )
        copy.start()
        sent.append(copy)
    cbuf[slab] = collision[...]

    rows_t[...] = jnp.zeros_like(rows_t)
    inflow = wall_values[...] * wall_kind[...].astype(f32)
    rate_x = jnp.abs(cx) * NX
    rate_y = jnp.abs(cy) * NY
    rows_t[0:1, :] = rate_x
    ratio = rate_y / (1.0 + rate_y)
    powers = [ratio]
    for _ in range(SEG - 1):
        powers.append(powers[-1] * ratio)
    powers.append(powers[-1] * powers[-1])
    powers.append(powers[-1] * powers[-1])
    powers += [zero, 1.0 / (1.0 + rate_y)]
    for n, power in enumerate(powers):
        for i in range(NB):
            yrow[i, n : n + 1, :] = power[:, i * VB : (i + 1) * VB]
    rows_t[3:4, :] = jnp.where(low_side, inflow[0:1], inflow[1:2])
    rows_t[4:5, :] = fx
    rows_t[5:6, :] = fy
    for i in range(NB):
        at = slice(i * VB, (i + 1) * VB)
        col[at, :] = jnp.transpose(rows_t[:, at])
    factor = 4.0 / 45.0 * heat
    psi = jnp.concatenate(
        [one, 2.0 * cx, 2.0 * cy, 2.0 * cz, square - 1.5, factor * cx, factor * cy, factor * cz],
        axis=0,
    )
    psi_hi = psi.astype(bf16).astype(f32)
    psi_lo = psi - psi_hi
    for g in range(4):
        rows_t[g * 32 : g * 32 + 8, :] = psi_hi * masks[g]
        rows_t[g * 32 + 8 : g * 32 + 16, :] = psi_hi * masks[g]
        rows_t[g * 32 + 16 : g * 32 + 24, :] = psi_lo * masks[g]
        rows_t[g * 32 + 24 : g * 32 + 32, :] = psi_lo * masks[g]
    for i in range(NB):
        at = slice(i * VB, (i + 1) * VB)
        shp[at, :] = jnp.transpose(rows_t[:, at]).astype(bf16)

    lane = lanes((VB, NY))

    def send_out(buf, target, send, recv, it, i, to):
        at = pl.ds(i * CB, CB)
        pltpu.make_async_remote_copy(
            src_ref=buf.at[it, at],
            dst_ref=target.at[it, at],
            send_sem=send.at[it, i],
            recv_sem=recv.at[it, i],
            device_id=device(to, px, py, pz),
            device_id_type=MESH,
        ).start()

    def wait_in(target, send, recv, it, i):
        at = pl.ds(i * CB, CB)
        pltpu.make_async_remote_copy(
            src_ref=target.at[it, at],
            dst_ref=target.at[it, at],
            send_sem=send.at[it, i],
            recv_sem=recv.at[it, i],
            device_id=device(partner, px, py, pz),
            device_id_type=MESH,
        ).wait_recv()

    def wait_out(buf, target, send, recv, it, i):
        at = pl.ds(i * CB, CB)
        pltpu.make_async_remote_copy(
            src_ref=buf.at[it, at],
            dst_ref=target.at[it, at],
            send_sem=send.at[it, i],
            recv_sem=recv.at[it, i],
            device_id=device(partner, px, py, pz),
            device_id_type=MESH,
        ).wait_send()

    twice = jnp.concatenate([collision[...], collision[...]], axis=0)
    own, own_back = swept(twice), swept_back(twice)

    def pass_on(it, i):
        at = pl.ds(i * CB, CB)
        wait_in(near, nsend, nrecv, it, i)
        outa[it, at, :] = prod[at, :] * near[it, at, :] + gd[XL - 1, at, :]
        send_out(outa, far, fsend, frecv, it, i, across)

    def sweep_source(fields, at):
        total = inv_own[0, at, :] * fields[0]
        gd[0, at, :] = total
        for q in range(1, XL):
            total = fac[PAD + q, at, :] * total + inv_own[q, at, :] * fields[q]
            gd[q, at, :] = total

    def chain_step(it, c):
        @pl.when(edge)
        def _():
            at = pl.ds(c * CB, CB)
            outa[it, at, :] = prod[at, :] * near[it, at, :] + gd[XL - 1, at, :]
            send_out(outa, near, nsend, nrecv, it, c, partner)

        @pl.when(jnp.logical_and(middle, c >= LAG))
        def _():
            pass_on(it, c - LAG)

    def in_groups(block, it):
        def group_of(c, carry):
            for n in range(CB // VB):
                block(c * (CB // VB) + n, 0)
            if it is not None:
                chain_step(it, c)
            return carry
        lax.fori_loop(0, NC, group_of, 0)

    def prepare(i, c):
        at = pl.ds(i * VB, VB)
        cols = col[at, :]
        wide = lambda k: jnp.broadcast_to(cols[:, k : k + 1], (VB, NY))
        a = wide(0)
        ascale[at, :] = a
        fxv, fyv = wide(4), wide(5)
        fxs[at, :] = fxv
        fys[at, :] = fyv
        forward, upward = fxv > 0.5, fyv > 0.5

        @pl.when(edge)
        def _():
            for it in range(ITERS):
                near[it, at, :] = wide(3)

        index = jnp.where(upward, cell_at(lane), NY - 1 - cell_at(lane))
        product = None
        fields = []
        for q in range(XL):
            m = XL - 1 - q
            rate = jnp.where(
                forward,
                jnp.where(upward, own[q : q + 1], own_back[q : q + 1]),
                jnp.where(upward, own[m : m + 1], own_back[m : m + 1]),
            )
            inv = 1.0 / (1.0 + a + rate)
            f = a * inv
            inv_own[q, at, :] = inv
            fac[PAD + q, at, :] = f
            wgt[PAD + q, at, :] = rate * inv
            product = f if product is None else product * f
            picked = jnp.where(
                forward,
                draw[pl.ds(i * VB * XL + q, VB, stride=XL), :],
                draw[pl.ds(i * VB * XL + m, VB, stride=XL), :],
            )
            fields.append(jnp.take_along_axis(picked, index, axis=1))
        prod[at, :] = product
        sweep_source(fields, at)
        return c

    in_groups(prepare, 0)

    def chain_across(it):
        @pl.when(middle)
        def _():
            def step(i, c):
                pass_on(it, i)
                return c
            lax.fori_loop(NC - LAG, NC, step, 0)

    def chain_back(it):
        @pl.when(middle)
        def _():
            def step(i, c):
                at = pl.ds(i * CB, CB)
                wait_in(far, fsend, frecv, it, i)
                outb[it, at, :] = prod[at, :] * far[it, at, :] + gd[XL - 1, at, :]
                pltpu.make_async_remote_copy(
                    src_ref=outb.at[it, at],
                    dst_ref=far.at[it, at],
                    send_sem=nsend.at[it, i],
                    recv_sem=frecv.at[it, i],
                    device_id=device(partner, px, py, pz),
                    device_id_type=MESH,
                ).start()
                return c
            lax.fori_loop(0, NC, step, 0)

    def drain_chain(it):
        @pl.when(middle)
        def _():
            def step(i, c):
                wait_out(outa, far, fsend, frecv, it, i)
                wait_out(outb, far, nsend, frecv, it, i)
                return c
            lax.fori_loop(0, NC, step, 0)

        @pl.when(edge)
        def _():
            def step(i, c):
                wait_out(outa, near, nsend, nrecv, it, i)
                return c
            lax.fori_loop(0, NC, step, 0)

    sent += second_stage(0)
    chain_across(0)

    for d in range(1, 4):
        source = (slab + 4 - d) % 4
        pltpu.make_async_remote_copy(
            src_ref=collision,
            dst_ref=cbuf.at[source],
            send_sem=csend.at[d - 1],
            recv_sem=crecv.at[d - 1],
            device_id=device(source, px, py, pz),
            device_id_type=MESH,
        ).wait_recv()
    crow[...] = jnp.zeros_like(crow)
    everywhere = jnp.concatenate([cbuf[s] for s in range(SLABS)], axis=0)
    ahead_rows, back_rows = swept(everywhere), swept_back(everywhere)
    for i in range(NX):
        for n, source in enumerate((ahead_rows, back_rows, everywhere)):
            crow[n, PAD + i] = jnp.broadcast_to(source[i : i + 1], (8, NY))

    def upstream(start, stop):
        def at_cell(r, c):
            ahead = XL * slab + r
            behind = XL * slab + PAD + NX - 1 - r
            c_ff = crow[0, ahead][0:1]
            c_fb = crow[1, ahead][0:1]
            c_bf = crow[0, behind][0:1]
            c_bb = crow[1, behind][0:1]
            def block(i, c):
                at = pl.ds(i * VB, VB)
                a = ascale[at, :]
                forward, upward = fxs[at, :] > 0.5, fys[at, :] > 0.5
                rate = jnp.where(
                    forward, jnp.where(upward, c_ff, c_fb), jnp.where(upward, c_bf, c_bb)
                )
                inv = 1.0 / (1.0 + a + rate)
                fac[r, at, :] = a * inv
                wgt[r, at, :] = rate * inv
                return c
            lax.fori_loop(0, NB, block, 0)
            return c
        lax.fori_loop(start, stop, at_cell, 0)

    upstream(0, 5)
    sent += third_stage(0)
    chain_back(0)
    upstream(5, PAD)
    sent += forward_far(0)

    cell = lanes((8, NY))
    sub = lax.broadcasted_iota(jnp.int32, (8, NY), 0)

    def above(value):
        return jnp.where(cell < NY - 1, pltpu.roll(value, NY - 1, 1), 0.0)

    def below(value):
        return jnp.where(cell >= 1, pltpu.roll(value, 1, 1), 0.0)

    def macro(it):
        for piece in range(2):
            spread_arrived(it, piece)
        head, flux = [], []
        for i in range(NX):
            s, x = i // XL, i % XL
            piece, at = x // 2, slice((x % 2) * NY, (x % 2 + 1) * NY)
            head.append(b3[it, piece, s, 0:8, at] + b3[it, piece, 4 + s, 0:8, at])
            flux.append(b3[it, piece, s, 8:ROWS, at] + b3[it, piece, 4 + s, 8:ROWS, at])
        nothing = jnp.zeros((8, NY), f32)
        along = [
            jnp.concatenate([a[1:2], b[0:3], a[5:6], a[5:8]], axis=0) for a, b in zip(head, flux)
        ]
        target, kappa, down = [], [], []
        for i in range(NX):
            a, b = head[i], flux[i]
            cross = jnp.concatenate([a[2:3], b[1:2], b[3:5], a[6:7], a[5:8]], axis=0)
            right = along[i + 1] if i + 1 < NX else nothing
            left = along[i - 1] if i > 0 else nothing
            target.append(a - (0.5 * (right - left) + 0.5 * (above(cross) - below(cross))))
            stiff = 1.0 / crow[2, PAD + i]
            kappa.append(stiff)
            down.append(1.0 / (1.0 + 4.0 * stiff))
        settled = head
        for _ in range(JACOBI):
            after = []
            for i in range(NX):
                right = settled[i + 1] if i + 1 < NX else nothing
                left = settled[i - 1] if i > 0 else nothing
                around = right + left + above(settled[i]) + below(settled[i])
                after.append((target[i] + kappa[i] * around) * down[i])
            settled = after
        dpad[...] = jnp.zeros_like(dpad)
        for i in range(NX):
            drive = jnp.where(sub < 5, settled[i], head[i])
            drive_s[i] = drive
            hi, lo = split(swept(drive))
            dpad[0, PAD + i] = jnp.concatenate([hi, lo], axis=0)
            hi, lo = split(swept_back(drive))
            dpad[1, PAD + i] = jnp.concatenate([hi, lo], axis=0)
        for r in range(NX):
            ahead = XL * slab + r
            behind = XL * slab + PAD + NX - 1 - r
            at = slice(r * NY, (r + 1) * NY)
            for g, tile in enumerate(
                (dpad[0, ahead], dpad[1, ahead], dpad[0, behind], dpad[1, behind])
            ):
                rhs[g * 32 : g * 32 + 16, at] = tile
                rhs[g * 32 + 16 : g * 32 + 32, at] = tile

    segment = lax.broadcasted_iota(jnp.int32, (8, NY), 0)

    def along_y(g, table):
        columns = jnp.transpose(g)
        ratio, scale = table[0:1], table[SEG + 3 : SEG + 4]
        inner = []
        for t in range(SEG):
            h = columns[8 * t : 8 * t + 8] * scale
            inner.append(h + ratio * inner[-1] if t else h)
        ends = inner[-1]
        for n, step in enumerate((1, 2, 4)):
            moved = jnp.where(segment >= step, pltpu.roll(ends, step, 0), 0.0)
            k = SEG - 1 + n
            ends = ends + table[k : k + 1] * moved
        carry = jnp.where(segment >= 1, pltpu.roll(ends, 1, 0), 0.0)
        whole = [inner[t] + table[t : t + 1] * carry for t in range(SEG)]
        return jnp.transpose(jnp.concatenate(whole, axis=0))

    def main(it):
        last = it == ITERS - 1

        @pl.when(edge)
        def _():
            def ready(i, c):
                wait_in(far, fsend, frecv, it, i)
                return c
            lax.fori_loop(0, NC, ready, 0)

        def block(i, c):
            at = pl.ds(i * VB, VB)
            eq = dot(shp[at, :], rhs[...])
            enter = wgt[0, at, :] * eq[:, 0:NY]
            for r in range(1, PAD):
                enter = fac[r, at, :] * enter + wgt[r, at, :] * eq[:, r * NY : (r + 1) * NY]
            forward = fxs[at, :] > 0.5
            from_near = jnp.where(low_side, fxs[at, :], 1.0 - fxs[at, :]) > 0.5
            enter = enter + jnp.where(from_near, near[it, at, :], far[it, at, :])
            fields = []
            for q in range(XL):
                r = PAD + q
                enter = fac[r, at, :] * enter + wgt[r, at, :] * eq[:, r * NY : (r + 1) * NY]
                h = along_y(gd[q, at, :] + enter, yrow[i])
                fields.append(h)
                if not last:
                    hi, lo = split(h)
                    fhi[at, q * NY : (q + 1) * NY] = hi
                    flo[at, q * NY : (q + 1) * NY] = lo
            if last:
                index = jnp.where(fys[at, :] > 0.5, lane_of(lane), lane_of(NY - 1 - lane))
                for x in range(XL):
                    picked = jnp.where(forward, fields[x], fields[XL - 1 - x])
                    out[pl.ds(i * VB * XL + x, VB, stride=XL), :] = jnp.take_along_axis(
                        picked, index, axis=1
                    )
            else:
                sweep_source(fields, at)
            return c

        in_groups(block, None if last else it + 1)

    for it in range(ITERS):
        macro(it)
        main(it)
        if it < ITERS - 1:
            first = dot(rows_g[...], fhi[...])
            groups = first[0 : 4 * KR] + first[4 * KR : 8 * KR] + dot(rows_g[0 : 4 * KR, :], flo[...])
            turn = lambda t: jnp.concatenate(
                [t[:, x * NY : (x + 1) * NY] for x in reversed(range(XL))], axis=1
            )
            up = groups[0:KR] + turn(groups[2 * KR : 3 * KR])
            down = groups[KR : 2 * KR] + turn(groups[3 * KR : 4 * KR])
            spans = [slice(x * NY, (x + 1) * NY) for x in range(XL)]
            moment = jnp.concatenate(
                [restored(up[:, at]) + restored_back(down[:, at]) for at in spans], axis=1
            )
            sent += start_reduce(it + 1, moment)
            chain_across(it + 1)
            sent += second_stage(it + 1)
            chain_back(it + 1)
            sent += third_stage(it + 1)
            sent += forward_far(it + 1)
            for done in range(ITERS):
                drain_chain(done)
            for copy in sent:
                copy.wait_send()

    for x in range(XL):
        settled_out[:, x, :] = drive_s[XL * slab + x][0:5]


def on_device(dist, speeds, weights, collision, wall_values, wall_kind):
    vmem = pl.BlockSpec(memory_space=pltpu.VMEM)
    hbm = pl.BlockSpec(memory_space=pltpu.HBM)
    dma = pltpu.SemaphoreType.DMA
    full = (V, NY)
    scratch = [
        pltpu.VMEM((V * XL, NY), f32),
        pltpu.VMEM((XL, *full), f32),
        pltpu.VMEM((V, XL * NY), bf16),
        pltpu.VMEM((V, XL * NY), bf16),
        pltpu.VMEM((NX, *full), f32),
        pltpu.VMEM((NX, *full), f32),
        pltpu.VMEM((XL, *full), f32),
        pltpu.VMEM(full, f32),
        pltpu.VMEM((NB, TABLE, VB), f32),
        pltpu.VMEM(full, f32),
        pltpu.VMEM(full, f32),
        pltpu.VMEM(full, f32),
        pltpu.VMEM((ITERS, *full), f32),
        pltpu.VMEM((ITERS, *full), f32),
        pltpu.VMEM((ITERS, *full), f32),
        pltpu.VMEM((ITERS, *full), f32),
        pltpu.VMEM((128, V), f32),
        pltpu.VMEM((2 * KR, V), bf16),
        pltpu.VMEM((8 * KR, V), bf16),
        pltpu.VMEM((V, 128), bf16),
        pltpu.VMEM((V, 128), f32),
        pltpu.VMEM((ITERS, 2, 4, ROWS, HALF), f32),
        pltpu.VMEM((ITERS, 2, 4, ROWS, HALF), f32),
        pltpu.VMEM((ITERS, 2, 8, ROWS, HALF), f32),
        pltpu.VMEM((SLABS, XL, NY), f32),
        pltpu.VMEM((3, NX + 2 * PAD, 8, NY), f32),
        pltpu.VMEM((2, NX + 2 * PAD, 16, NY), bf16),
        pltpu.VMEM((128, NX * NY), bf16),
        pltpu.VMEM((NX, 8, NY), f32),
        pltpu.VMEM((3, V), f32),
        pltpu.VMEM((V,), f32),
        pltpu.VMEM((XL, NY), f32),
        pltpu.VMEM((2, V), f32),
        pltpu.VMEM((2, V), jnp.int32),
        dma((NB,)),
        dma((5,)),
        dma((ITERS, 2, 2, 3)),
        dma((ITERS, 2, 2, 3)),
        dma((ITERS, 2, 7)),
        dma((ITERS, 2, 7)),
        dma((3,)),
        dma((3,)),
        dma((ITERS, NC)),
        dma((ITERS, NC)),
        dma((ITERS, NC)),
        dma((ITERS, NC)),
    ]
    rows, settled = pl.pallas_call(
        transport_kernel,
        out_shape=(
            jax.ShapeDtypeStruct((V * XL, NY), f32),
            jax.ShapeDtypeStruct((5, XL, NY), f32),
        ),
        in_specs=[hbm] * 6,
        out_specs=(vmem, vmem),
        scratch_shapes=scratch,
        compiler_params=pltpu.CompilerParams(
            collective_id=0, has_side_effects=True, vmem_limit_bytes=50000000
        ),
        name="transport",
    )(*(
        pltpu.with_memory_space_constraint(value, pltpu.HBM)
        for value in (dist.reshape(V * XL, NY), speeds, weights, collision, wall_values, wall_kind)
    ))
    return rows.reshape(V, XL, NY), settled


def solution(mesh):
    return jax.shard_map(
        on_device,
        mesh=mesh,
        in_specs=(
            P("vel", "slab", None),
            P(None, "vel"),
            P("vel"),
            P("slab", None),
            P(None, "vel"),
            P(None, "vel"),
        ),
        out_specs=(P("vel", "slab", None), P(None, "slab", None)),
        check_vma=False,
    )
```

```python
import jax
import jax.numpy as jnp
from jax import lax
from jax.experimental import pallas as pl
from jax.experimental.pallas import tpu as pltpu
from jax.sharding import PartitionSpec as P

VELS = 24576
ITERS = 2
JACOBI = 2
NX = 16
NY = 128
SLABS = 4
XL = NX // SLABS
V = VELS // 32
VB = 128
NB = V // VB
CB = 256
NC = V // CB
PAD = NX - XL
KR = 16
ROWS = 13
LAG = 1
HALF = XL * NY // 2
SEG = NY // 8
TABLE = SEG + 4

f32 = jnp.float32
bf16 = jnp.bfloat16
MESH = pl.DeviceIdType.MESH


def split(value):
    high = value.astype(bf16)
    return high, (value - high.astype(f32)).astype(bf16)


def dot(a, b):
    return jnp.dot(a, b, preferred_element_type=f32)


def lanes(shape):
    return lax.broadcasted_iota(jnp.int32, shape, 1)


def pick(value, index):
    return jnp.take_along_axis(value, index, axis=1)


def cell_at(lane):
    return (lane % 8) * SEG + lane // 8


def lane_of(cell):
    return (cell % SEG) * 8 + cell // SEG


def swept(value):
    return pick(value, cell_at(lanes(value.shape)))


def swept_back(value):
    return pick(value, NY - 1 - cell_at(lanes(value.shape)))


def restored(value):
    return pick(value, lane_of(lanes(value.shape)))


def restored_back(value):
    return pick(value, lane_of(NY - 1 - lanes(value.shape)))


def transport_kernel(
    dist, speeds_in, weights_in, collision_in, values_in, kind_in,
    out, settled_out,
    draw, gd, fhi, flo, fac, wgt, inv_own, prod, yrow, ascale, run, kappa_s, down_s, fxs, fys,
    near, far, outa, outb, rows_t, rows_p, rows_g, shp, col,
    b1, b2, b3, cbuf, crow, dpad, rhs, drive_s,
    speeds, weights, collision, wall_values, wall_kind,
    dsem, ssem, bsend, brecv, ysend, yrecv, csend, crecv, nsend, nrecv, fsend, frecv,
):
    slab = lax.axis_index("slab")
    vel = lax.axis_index("vel")
    px = vel // 8
    py = (vel // 4) % 2
    pz = vel % 4
    edge = jnp.logical_or(slab == 0, slab == SLABS - 1)
    middle = jnp.logical_and(slab > 0, slab < SLABS - 1)
    low_side = slab < 2
    partner = jnp.where(low_side, 1 - slab, 5 - slab)
    across = 3 - slab
    beside = jnp.where(low_side, 2, 0)

    def device(s, x, y, z):
        return {"slab": s, "vel": (x * 2 + y) * 4 + z}

    loads = [
        pltpu.make_async_copy(
            dist.at[pl.ds(i * VB * XL, VB * XL)], draw.at[pl.ds(i * VB * XL, VB * XL)], dsem.at[i]
        )
        for i in range(NB)
    ]
    small = [
        pltpu.make_async_copy(source, target, ssem.at[n])
        for n, (source, target) in enumerate((
            (speeds_in, speeds), (weights_in, weights), (collision_in, collision),
            (values_in, wall_values), (kind_in, wall_kind),
        ))
    ]
    for load in small + loads:
        load.start()

    peers = []
    for d in range(1, 4):
        peers.append(device(slab, (px + d) % 4, py, pz))
    for d in range(1, 4):
        peers.append(device(slab, px, py, (pz + d) % 4))
    group = py * 4 + slab
    yz = []
    for d in range(1, 8):
        other = (group + d) % 8
        yz.append(device(other % 4, px, other // 4, pz))
    barrier = pltpu.get_barrier_semaphore()
    for peer in peers + yz:
        pl.semaphore_signal(barrier, inc=1, device_id=peer, device_id_type=MESH)

    for load in small:
        load.wait()
    cx, cy, cz = speeds[0:1, :], speeds[1:2, :], speeds[2:3, :]
    wt = weights[...].reshape(1, V)
    square = cx * cx + cy * cy + cz * cz
    third = square / 3.0
    heat = square - 2.5
    one = jnp.ones_like(cx)
    zero = jnp.zeros_like(cx)
    phi = [
        one, cx, cy, cz, 2.0 / 3.0 * square - 1.0, cx * heat, cy * heat, cz * heat,
        cx * cx - third, cx * cy, cx * cz, cy * cy - third, cy * cz, zero, zero, zero,
    ]
    scale = wt / VELS
    fx = jnp.where(cx >= 0, 1.0, 0.0)
    fy = jnp.where(cy >= 0, 1.0, 0.0)
    rows = jnp.concatenate([p * scale for p in phi], axis=0)
    rows_hi, rows_lo = split(rows)
    rows_p[0:KR, :] = rows_hi
    rows_p[KR : 2 * KR, :] = rows_lo
    masks = [fx * fy, fx * (1.0 - fy), (1.0 - fx) * fy, (1.0 - fx) * (1.0 - fy)]
    for g in range(4):
        m = masks[g].astype(bf16)
        rows_g[g * KR : (g + 1) * KR, :] = rows_hi * m
        rows_g[4 * KR + g * KR : 4 * KR + (g + 1) * KR, :] = rows_lo * m

    def cast(i, c):
        at = pl.ds(i * VB, VB)
        rows_at = pl.ds(i * VB * XL, VB * XL)
        pltpu.make_async_copy(dist.at[rows_at], draw.at[rows_at], dsem.at[i]).wait()
        for x in range(XL):
            hi, lo = split(draw[pl.ds(i * VB * XL + x, VB, stride=XL), :])
            fhi[at, x * NY : (x + 1) * NY] = hi
            flo[at, x * NY : (x + 1) * NY] = lo
        return c

    lax.fori_loop(0, NB, cast, 0)
    first = dot(rows_p[...], fhi[...])
    moment = first[0:KR] + first[KR : 2 * KR] + dot(rows_p[0:KR, :], flo[...])

    pl.semaphore_wait(barrier, 13)

    axes = ((px, lambda o: device(slab, o, py, pz)), (pz, lambda o: device(slab, px, py, o)))

    def exchange(buf, stage, it, piece):
        me, to = axes[(stage + piece) % 2]
        sent = []
        for d in range(1, 4):
            copy = pltpu.make_async_remote_copy(
                src_ref=buf.at[it, piece, me],
                dst_ref=buf.at[it, piece, me],
                send_sem=bsend.at[it, stage, piece, d - 1],
                recv_sem=brecv.at[it, stage, piece, d - 1],
                device_id=to((me + d) % 4),
                device_id_type=MESH,
            )
            copy.start()
            sent.append(copy)
        return sent

    def arrived(buf, stage, it, piece):
        me, to = axes[(stage + piece) % 2]
        for d in range(1, 4):
            source = (me + 4 - d) % 4
            pltpu.make_async_remote_copy(
                src_ref=buf.at[it, piece, source],
                dst_ref=buf.at[it, piece, source],
                send_sem=bsend.at[it, stage, piece, d - 1],
                recv_sem=brecv.at[it, stage, piece, d - 1],
                device_id=to(source),
                device_id_type=MESH,
            ).wait_recv()
        return (buf[it, piece, 0] + buf[it, piece, 1]) + (buf[it, piece, 2] + buf[it, piece, 3])

    def hand(it, piece, n, slot, y, s):
        index = (y * 4 + s + 8 - slot) % 8 - 1
        copy = pltpu.make_async_remote_copy(
            src_ref=b3.at[it, piece, slot],
            dst_ref=b3.at[it, piece, slot],
            send_sem=ysend.at[it, piece, n],
            recv_sem=yrecv.at[it, piece, index],
            device_id=device(s, px, y, pz),
            device_id_type=MESH,
        )
        copy.start()
        return copy

    def spread(it, piece):
        targets = [(1 - py, slab)]
        for y in (py, 1 - py):
            targets += [(y, beside), (y, beside + 1)]
        targets.append((py, partner))
        return [hand(it, piece, n, group, y, s) for n, (y, s) in enumerate(targets)]

    def forward_far(it):
        sent = []
        for piece in range(2):
            source = (group + 4) % 8
            pltpu.make_async_remote_copy(
                src_ref=b3.at[it, piece, source],
                dst_ref=b3.at[it, piece, source],
                send_sem=ysend.at[it, piece, 3],
                recv_sem=yrecv.at[it, piece, 3],
                device_id=yz[3],
                device_id_type=MESH,
            ).wait_recv()
            sent.append(hand(it, piece, 6, source, py, partner))
        return sent

    def spread_arrived(it, piece):
        for d in (1, 2, 3, 5, 6, 7):
            source = (group + 8 - d) % 8
            pltpu.make_async_remote_copy(
                src_ref=b3.at[it, piece, source],
                dst_ref=b3.at[it, piece, source],
                send_sem=ysend.at[it, piece, d - 1],
                recv_sem=yrecv.at[it, piece, d - 1],
                device_id=yz[d - 1],
                device_id_type=MESH,
            ).wait_recv()

    def start_reduce(it, value):
        sent = []
        for piece in range(2):
            b1[it, piece, axes[piece % 2][0]] = value[0:ROWS, piece * HALF : (piece + 1) * HALF]
            sent += exchange(b1, 0, it, piece)
        return sent

    def second_stage(it):
        sent = []
        for piece in range(2):
            total = arrived(b1, 0, it, piece)
            b2[it, piece, axes[(1 + piece) % 2][0]] = total
            sent += exchange(b2, 1, it, piece)
        return sent

    def third_stage(it):
        sent = []
        for piece in range(2):
            b3[it, piece, group] = arrived(b2, 1, it, piece)
            sent += spread(it, piece)
        return sent

    sent = start_reduce(0, moment)
    for d in range(1, 4):
        copy = pltpu.make_async_remote_copy(
            src_ref=collision,
            dst_ref=cbuf.at[slab],
            send_sem=csend.at[d - 1],
            recv_sem=crecv.at[d - 1],
            device_id=device((slab + d) % 4, px, py, pz),
            device_id_type=MESH,
        )
        copy.start()
        sent.append(copy)
    cbuf[slab] = collision[...]

    rows_t[...] = jnp.zeros_like(rows_t)
    inflow = wall_values[...] * wall_kind[...].astype(f32)
    rate_x = jnp.abs(cx) * NX
    rate_y = jnp.abs(cy) * NY
    rows_t[0:1, :] = rate_x
    ratio = rate_y / (1.0 + rate_y)
    powers = [ratio]
    for _ in range(SEG - 1):
        powers.append(powers[-1] * ratio)
    powers.append(powers[-1] * powers[-1])
    powers.append(powers[-1] * powers[-1])
    powers += [zero, 1.0 / (1.0 + rate_y)]
    for n, power in enumerate(powers):
        for i in range(NB):
            yrow[i, n : n + 1, :] = power[:, i * VB : (i + 1) * VB]
    rows_t[3:4, :] = jnp.where(low_side, inflow[0:1], inflow[1:2])
    rows_t[4:5, :] = fx
    rows_t[5:6, :] = fy
    for i in range(NB):
        at = slice(i * VB, (i + 1) * VB)
        col[at, :] = jnp.transpose(rows_t[:, at])
    factor = 4.0 / 45.0 * heat
    psi = jnp.concatenate(
        [one, 2.0 * cx, 2.0 * cy, 2.0 * cz, square - 1.5, factor * cx, factor * cy, factor * cz],
        axis=0,
    )
    psi_hi = psi.astype(bf16).astype(f32)
    psi_lo = psi - psi_hi
    for g in range(4):
        rows_t[g * 32 : g * 32 + 8, :] = psi_hi * masks[g]
        rows_t[g * 32 + 8 : g * 32 + 16, :] = psi_hi * masks[g]
        rows_t[g * 32 + 16 : g * 32 + 24, :] = psi_lo * masks[g]
        rows_t[g * 32 + 24 : g * 32 + 32, :] = psi_lo * masks[g]
    for i in range(NB):
        at = slice(i * VB, (i + 1) * VB)
        shp[at, :] = jnp.transpose(rows_t[:, at]).astype(bf16)

    lane = lanes((VB, NY))

    def send_out(buf, target, send, recv, it, i, to):
        at = pl.ds(i * CB, CB)
        pltpu.make_async_remote_copy(
            src_ref=buf.at[it, at],
            dst_ref=target.at[it, at],
            send_sem=send.at[it, i],
            recv_sem=recv.at[it, i],
            device_id=device(to, px, py, pz),
            device_id_type=MESH,
        ).start()

    def wait_in(target, send, recv, it, i):
        at = pl.ds(i * CB, CB)
        pltpu.make_async_remote_copy(
            src_ref=target.at[it, at],
            dst_ref=target.at[it, at],
            send_sem=send.at[it, i],
            recv_sem=recv.at[it, i],
            device_id=device(partner, px, py, pz),
            device_id_type=MESH,
        ).wait_recv()

    def wait_out(buf, target, send, recv, it, i):
        at = pl.ds(i * CB, CB)
        pltpu.make_async_remote_copy(
            src_ref=buf.at[it, at],
            dst_ref=target.at[it, at],
            send_sem=send.at[it, i],
            recv_sem=recv.at[it, i],
            device_id=device(partner, px, py, pz),
            device_id_type=MESH,
        ).wait_send()

    twice = jnp.concatenate([collision[...], collision[...]], axis=0)
    own, own_back = swept(twice), swept_back(twice)

    def pass_on(it, i):
        at = pl.ds(i * CB, CB)
        wait_in(near, nsend, nrecv, it, i)
        outa[it, at, :] = prod[at, :] * near[it, at, :] + gd[XL - 1, at, :]
        send_out(outa, far, fsend, frecv, it, i, across)

    def sweep_source(fields, at):
        total = inv_own[0, at, :] * fields[0]
        gd[0, at, :] = total
        for q in range(1, XL):
            total = fac[q, at, :] * total + inv_own[q, at, :] * fields[q]
            gd[q, at, :] = total

    def chain_step(it, c):
        @pl.when(edge)
        def _():
            at = pl.ds(c * CB, CB)
            outa[it, at, :] = prod[at, :] * near[it, at, :] + gd[XL - 1, at, :]
            send_out(outa, near, nsend, nrecv, it, c, partner)

        @pl.when(jnp.logical_and(middle, c >= LAG))
        def _():
            pass_on(it, c - LAG)

    def in_groups(block, it):
        def group_of(c, carry):
            for n in range(CB // VB):
                block(c * (CB // VB) + n, 0)
            if it is not None:
                chain_step(it, c)
            return carry
        lax.fori_loop(0, NC, group_of, 0)

    def prepare(i, c):
        at = pl.ds(i * VB, VB)
        cols = col[at, :]
        wide = lambda k: jnp.broadcast_to(cols[:, k : k + 1], (VB, NY))
        a = wide(0)
        ascale[at, :] = a
        run[at, :] = jnp.ones_like(a)
        fxv, fyv = wide(4), wide(5)
        fxs[at, :] = fxv
        fys[at, :] = fyv
        forward, upward = fxv > 0.5, fyv > 0.5

        @pl.when(edge)
        def _():
            for it in range(ITERS):
                near[it, at, :] = wide(3)

        index = jnp.where(upward, cell_at(lane), NY - 1 - cell_at(lane))
        product = None
        fields = []
        for q in range(XL):
            m = XL - 1 - q
            rate = jnp.where(
                forward,
                jnp.where(upward, own[q : q + 1], own_back[q : q + 1]),
                jnp.where(upward, own[m : m + 1], own_back[m : m + 1]),
            )
            inv = 1.0 / (1.0 + a + rate)
            f = a * inv
            inv_own[q, at, :] = inv
            fac[q, at, :] = f
            wgt[PAD + q, at, :] = rate * inv
            product = f if product is None else product * f
            picked = jnp.where(
                forward,
                draw[pl.ds(i * VB * XL + q, VB, stride=XL), :],
                draw[pl.ds(i * VB * XL + m, VB, stride=XL), :],
            )
            fields.append(jnp.take_along_axis(picked, index, axis=1))
        prod[at, :] = product
        sweep_source(fields, at)
        return c

    in_groups(prepare, 0)

    def chain_across(it):
        @pl.when(middle)
        def _():
            def step(i, c):
                pass_on(it, i)
                return c
            lax.fori_loop(NC - LAG, NC, step, 0)

    def chain_back(it):
        @pl.when(middle)
        def _():
            def step(i, c):
                at = pl.ds(i * CB, CB)
                wait_in(far, fsend, frecv, it, i)
                outb[it, at, :] = prod[at, :] * far[it, at, :] + gd[XL - 1, at, :]
                pltpu.make_async_remote_copy(
                    src_ref=outb.at[it, at],
                    dst_ref=far.at[it, at],
                    send_sem=nsend.at[it, i],
                    recv_sem=frecv.at[it, i],
                    device_id=device(partner, px, py, pz),
                    device_id_type=MESH,
                ).start()
                return c
            lax.fori_loop(0, NC, step, 0)

    def drain_chain(it):
        @pl.when(middle)
        def _():
            def step(i, c):
                wait_out(outa, far, fsend, frecv, it, i)
                wait_out(outb, far, nsend, frecv, it, i)
                return c
            lax.fori_loop(0, NC, step, 0)

        @pl.when(edge)
        def _():
            def step(i, c):
                wait_out(outa, near, nsend, nrecv, it, i)
                return c
            lax.fori_loop(0, NC, step, 0)

    sent += second_stage(0)
    chain_across(0)

    for d in range(1, 4):
        source = (slab + 4 - d) % 4
        pltpu.make_async_remote_copy(
            src_ref=collision,
            dst_ref=cbuf.at[source],
            send_sem=csend.at[d - 1],
            recv_sem=crecv.at[d - 1],
            device_id=device(source, px, py, pz),
            device_id_type=MESH,
        ).wait_recv()
    crow[...] = jnp.zeros_like(crow)
    everywhere = jnp.concatenate([cbuf[s] for s in range(SLABS)], axis=0)
    ahead_rows, back_rows = swept(everywhere), swept_back(everywhere)
    for i in range(NX):
        for n, source in enumerate((ahead_rows, back_rows, everywhere)):
            crow[n, PAD + i] = jnp.broadcast_to(source[i : i + 1], (8, NY))
    dpad[...] = jnp.zeros_like(dpad)
    for i in range(NX):
        stiff = 1.0 / crow[2, PAD + i]
        kappa_s[i] = stiff
        down_s[i] = 1.0 / (1.0 + 4.0 * stiff)

    def upstream(start, stop):
        def at_cell(n, c):
            r = PAD - 1 - n
            ahead = XL * slab + r
            behind = XL * slab + PAD + NX - 1 - r
            c_ff = crow[0, ahead][0:1]
            c_fb = crow[1, ahead][0:1]
            c_bf = crow[0, behind][0:1]
            c_bb = crow[1, behind][0:1]
            def block(i, c):
                at = pl.ds(i * VB, VB)
                a = ascale[at, :]
                forward, upward = fxs[at, :] > 0.5, fys[at, :] > 0.5
                rate = jnp.where(
                    forward, jnp.where(upward, c_ff, c_fb), jnp.where(upward, c_bf, c_bb)
                )
                inv = 1.0 / (1.0 + a + rate)
                through = run[at, :]
                wgt[r, at, :] = rate * inv * through
                run[at, :] = a * inv * through
                return c
            lax.fori_loop(0, NB, block, 0)
            return c
        lax.fori_loop(start, stop, at_cell, 0)

    upstream(0, 5)
    sent += third_stage(0)
    chain_back(0)
    upstream(5, PAD)
    sent += forward_far(0)

    cell = lanes((8, NY))
    sub = lax.broadcasted_iota(jnp.int32, (8, NY), 0)

    def above(value):
        return jnp.where(cell < NY - 1, pltpu.roll(value, NY - 1, 1), 0.0)

    def below(value):
        return jnp.where(cell >= 1, pltpu.roll(value, 1, 1), 0.0)

    def macro(it):
        for piece in range(2):
            spread_arrived(it, piece)
        head, flux = [], []
        for i in range(NX):
            s, x = i // XL, i % XL
            piece, at = x // 2, slice((x % 2) * NY, (x % 2 + 1) * NY)
            head.append(b3[it, piece, s, 0:8, at] + b3[it, piece, 4 + s, 0:8, at])
            flux.append(b3[it, piece, s, 8:ROWS, at] + b3[it, piece, 4 + s, 8:ROWS, at])
        nothing = jnp.zeros((8, NY), f32)
        along = [
            jnp.concatenate([a[1:2], b[0:3], a[5:6], a[5:8]], axis=0) for a, b in zip(head, flux)
        ]
        target, kappa, down = [], [], []
        for i in range(NX):
            a, b = head[i], flux[i]
            cross = jnp.concatenate([a[2:3], b[1:2], b[3:5], a[6:7], a[5:8]], axis=0)
            right = along[i + 1] if i + 1 < NX else nothing
            left = along[i - 1] if i > 0 else nothing
            target.append(a - (0.5 * (right - left) + 0.5 * (above(cross) - below(cross))))
            kappa.append(kappa_s[i])
            down.append(down_s[i])
        settled = head
        for _ in range(JACOBI):
            after = []
            for i in range(NX):
                right = settled[i + 1] if i + 1 < NX else nothing
                left = settled[i - 1] if i > 0 else nothing
                around = right + left + above(settled[i]) + below(settled[i])
                after.append((target[i] + kappa[i] * around) * down[i])
            settled = after
        for i in range(NX):
            drive = jnp.where(sub < 5, settled[i], head[i])
            drive_s[i] = drive
            hi, lo = split(swept(drive))
            dpad[0, PAD + i] = jnp.concatenate([hi, lo], axis=0)
            hi, lo = split(swept_back(drive))
            dpad[1, PAD + i] = jnp.concatenate([hi, lo], axis=0)
        for r in range(NX):
            ahead = XL * slab + r
            behind = XL * slab + PAD + NX - 1 - r
            at = slice(r * NY, (r + 1) * NY)
            for g, tile in enumerate(
                (dpad[0, ahead], dpad[1, ahead], dpad[0, behind], dpad[1, behind])
            ):
                rhs[g * 32 : g * 32 + 16, at] = tile
                rhs[g * 32 + 16 : g * 32 + 32, at] = tile

    segment = lax.broadcasted_iota(jnp.int32, (8, NY), 0)

    def along_y(g, table):
        columns = jnp.transpose(g)
        ratio, scale = table[0:1], table[SEG + 3 : SEG + 4]
        inner = []
        for t in range(SEG):
            h = columns[8 * t : 8 * t + 8] * scale
            inner.append(h + ratio * inner[-1] if t else h)
        ends = inner[-1]
        for n, step in enumerate((1, 2, 4)):
            moved = jnp.where(segment >= step, pltpu.roll(ends, step, 0), 0.0)
            k = SEG - 1 + n
            ends = ends + table[k : k + 1] * moved
        carry = jnp.where(segment >= 1, pltpu.roll(ends, 1, 0), 0.0)
        whole = [inner[t] + table[t : t + 1] * carry for t in range(SEG)]
        return jnp.transpose(jnp.concatenate(whole, axis=0))

    def main(it):
        last = it == ITERS - 1

        @pl.when(edge)
        def _():
            def ready(i, c):
                wait_in(far, fsend, frecv, it, i)
                return c
            lax.fori_loop(0, NC, ready, 0)

        def block(i, c):
            at = pl.ds(i * VB, VB)
            eq = dot(shp[at, :], rhs[...])
            enter = wgt[0, at, :] * eq[:, 0:NY]
            for r in range(1, PAD):
                enter = enter + wgt[r, at, :] * eq[:, r * NY : (r + 1) * NY]
            forward = fxs[at, :] > 0.5
            from_near = jnp.where(low_side, fxs[at, :], 1.0 - fxs[at, :]) > 0.5
            enter = enter + jnp.where(from_near, near[it, at, :], far[it, at, :])
            fields = []
            for q in range(XL):
                r = PAD + q
                enter = fac[q, at, :] * enter + wgt[r, at, :] * eq[:, r * NY : (r + 1) * NY]
                h = along_y(gd[q, at, :] + enter, yrow[i])
                fields.append(h)
                if not last:
                    hi, lo = split(h)
                    fhi[at, q * NY : (q + 1) * NY] = hi
                    flo[at, q * NY : (q + 1) * NY] = lo
            if last:
                index = jnp.where(fys[at, :] > 0.5, lane_of(lane), lane_of(NY - 1 - lane))
                for x in range(XL):
                    picked = jnp.where(forward, fields[x], fields[XL - 1 - x])
                    out[pl.ds(i * VB * XL + x, VB, stride=XL), :] = jnp.take_along_axis(
                        picked, index, axis=1
                    )
            else:
                sweep_source(fields, at)
            return c

        in_groups(block, None if last else it + 1)

    for it in range(ITERS):
        macro(it)
        main(it)
        if it < ITERS - 1:
            first = dot(rows_g[...], fhi[...])
            groups = first[0 : 4 * KR] + first[4 * KR : 8 * KR] + dot(rows_g[0 : 4 * KR, :], flo[...])
            turn = lambda t: jnp.concatenate(
                [t[:, x * NY : (x + 1) * NY] for x in reversed(range(XL))], axis=1
            )
            up = groups[0:KR] + turn(groups[2 * KR : 3 * KR])
            down = groups[KR : 2 * KR] + turn(groups[3 * KR : 4 * KR])
            spans = [slice(x * NY, (x + 1) * NY) for x in range(XL)]
            moment = jnp.concatenate(
                [restored(up[:, at]) + restored_back(down[:, at]) for at in spans], axis=1
            )
            sent += start_reduce(it + 1, moment)
            chain_across(it + 1)
            sent += second_stage(it + 1)
            chain_back(it + 1)
            sent += third_stage(it + 1)
            sent += forward_far(it + 1)
            for done in range(ITERS):
                drain_chain(done)
            for copy in sent:
                copy.wait_send()

    for x in range(XL):
        settled_out[:, x, :] = drive_s[XL * slab + x][0:5]


def copy_out(rows, settled, rows_out, settled_out, sem):
    copies = [
        pltpu.make_async_copy(settled, settled_out, sem.at[0]),
        pltpu.make_async_copy(rows, rows_out, sem.at[1]),
    ]
    for copy in copies:
        copy.start()
    for copy in copies:
        copy.wait()


def on_device(dist, speeds, weights, collision, wall_values, wall_kind):
    vmem = pl.BlockSpec(memory_space=pltpu.VMEM)
    hbm = pl.BlockSpec(memory_space=pltpu.HBM)
    dma = pltpu.SemaphoreType.DMA
    full = (V, NY)
    scratch = [
        pltpu.VMEM((V * XL, NY), f32),
        pltpu.VMEM((XL, *full), f32),
        pltpu.VMEM((V, XL * NY), bf16),
        pltpu.VMEM((V, XL * NY), bf16),
        pltpu.VMEM((XL, *full), f32),
        pltpu.VMEM((NX, *full), f32),
        pltpu.VMEM((XL, *full), f32),
        pltpu.VMEM(full, f32),
        pltpu.VMEM((NB, TABLE, VB), f32),
        pltpu.VMEM(full, f32),
        pltpu.VMEM(full, f32),
        pltpu.VMEM((NX, 8, NY), f32),
        pltpu.VMEM((NX, 8, NY), f32),
        pltpu.VMEM(full, f32),
        pltpu.VMEM(full, f32),
        pltpu.VMEM((ITERS, *full), f32),
        pltpu.VMEM((ITERS, *full), f32),
        pltpu.VMEM((ITERS, *full), f32),
        pltpu.VMEM((ITERS, *full), f32),
        pltpu.VMEM((128, V), f32),
        pltpu.VMEM((2 * KR, V), bf16),
        pltpu.VMEM((8 * KR, V), bf16),
        pltpu.VMEM((V, 128), bf16),
        pltpu.VMEM((V, 128), f32),
        pltpu.VMEM((ITERS, 2, 4, ROWS, HALF), f32),
        pltpu.VMEM((ITERS, 2, 4, ROWS, HALF), f32),
        pltpu.VMEM((ITERS, 2, 8, ROWS, HALF), f32),
        pltpu.VMEM((SLABS, XL, NY), f32),
        pltpu.VMEM((3, NX + 2 * PAD, 8, NY), f32),
        pltpu.VMEM((2, NX + 2 * PAD, 16, NY), bf16),
        pltpu.VMEM((128, NX * NY), bf16),
        pltpu.VMEM((NX, 8, NY), f32),
        pltpu.VMEM((3, V), f32),
        pltpu.VMEM((V,), f32),
        pltpu.VMEM((XL, NY), f32),
        pltpu.VMEM((2, V), f32),
        pltpu.VMEM((2, V), jnp.int32),
        dma((NB,)),
        dma((5,)),
        dma((ITERS, 2, 2, 3)),
        dma((ITERS, 2, 2, 3)),
        dma((ITERS, 2, 7)),
        dma((ITERS, 2, 7)),
        dma((3,)),
        dma((3,)),
        dma((ITERS, NC)),
        dma((ITERS, NC)),
        dma((ITERS, NC)),
        dma((ITERS, NC)),
    ]
    rows, settled = pl.pallas_call(
        transport_kernel,
        out_shape=(
            jax.ShapeDtypeStruct((V * XL, NY), f32),
            jax.ShapeDtypeStruct((5, XL, NY), f32),
        ),
        in_specs=[hbm] * 6,
        out_specs=(vmem, vmem),
        scratch_shapes=scratch,
        compiler_params=pltpu.CompilerParams(
            collective_id=0, has_side_effects=True, vmem_limit_bytes=50000000
        ),
        name="transport",
    )(*(
        pltpu.with_memory_space_constraint(value, pltpu.HBM)
        for value in (dist.reshape(V * XL, NY), speeds, weights, collision, wall_values, wall_kind)
    ))
    anywhere = pl.BlockSpec(memory_space=pl.ANY)
    rows, settled = pl.pallas_call(
        copy_out,
        out_shape=(
            jax.ShapeDtypeStruct((V * XL, NY), f32),
            jax.ShapeDtypeStruct((5, XL, NY), f32),
        ),
        in_specs=[anywhere, anywhere],
        out_specs=(hbm, hbm),
        scratch_shapes=[dma((2,))],
        compiler_params=pltpu.CompilerParams(vmem_limit_bytes=1024 * 1024),
        name="copy_out",
    )(rows, settled)
    return rows.reshape(V, XL, NY), settled


def solution(mesh):
    return jax.shard_map(
        on_device,
        mesh=mesh,
        in_specs=(
            P("vel", "slab", None),
            P(None, "vel"),
            P("vel"),
            P("slab", None),
            P(None, "vel"),
            P(None, "vel"),
        ),
        out_specs=(P("vel", "slab", None), P(None, "slab", None)),
        check_vma=False,
    )
```

```python
import jax
import jax.numpy as jnp
from jax import lax
from jax.experimental import pallas as pl
from jax.experimental.pallas import tpu as pltpu
from jax.sharding import PartitionSpec as P

VELS = 24576
ITERS = 2
JACOBI = 2
NX = 16
NY = 128
SLABS = 4
XL = NX // SLABS
V = VELS // 32
VB = 128
NB = V // VB
CB = 256
NC = V // CB
PAD = NX - XL
KR = 16
ROWS = 13
LAG = 1
HALF = XL * NY // 2
SEG = NY // 8
TABLE = SEG + 4

f32 = jnp.float32
bf16 = jnp.bfloat16
MESH = pl.DeviceIdType.MESH


def split(value):
    high = value.astype(bf16)
    return high, (value - high.astype(f32)).astype(bf16)


def dot(a, b):
    return jnp.dot(a, b, preferred_element_type=f32)


def lanes(shape):
    return lax.broadcasted_iota(jnp.int32, shape, 1)


def pick(value, index):
    return jnp.take_along_axis(value, index, axis=1)


def cell_at(lane):
    return (lane % 8) * SEG + lane // 8


def lane_of(cell):
    return (cell % SEG) * 8 + cell // SEG


def swept(value):
    return pick(value, cell_at(lanes(value.shape)))


def swept_back(value):
    return pick(value, NY - 1 - cell_at(lanes(value.shape)))


def restored(value):
    return pick(value, lane_of(lanes(value.shape)))


def restored_back(value):
    return pick(value, lane_of(NY - 1 - lanes(value.shape)))


def transport_kernel(
    dist, speeds_in, weights_in, collision_in, values_in, kind_in,
    out, settled_out,
    draw, gd, fhi, flo, fac, wgt, inv_own, prod, yrow, ascale, run, kappa_s, down_s, fxs, fys,
    near, far, outa, outb, rows_t, rows_p, rows_g, shp, col,
    b1, b2, b3, cbuf, crow, dpad, rhs, drive_s,
    speeds, weights, collision, wall_values, wall_kind,
    dsem, ssem, bsend, brecv, ysend, yrecv, csend, crecv, nsend, nrecv, fsend, frecv,
):
    slab = lax.axis_index("slab")
    vel = lax.axis_index("vel")
    px = vel // 8
    py = (vel // 4) % 2
    pz = vel % 4
    edge = jnp.logical_or(slab == 0, slab == SLABS - 1)
    middle = jnp.logical_and(slab > 0, slab < SLABS - 1)
    low_side = slab < 2
    partner = jnp.where(low_side, 1 - slab, 5 - slab)
    across = 3 - slab
    beside = jnp.where(low_side, 2, 0)

    def device(s, x, y, z):
        return {"slab": s, "vel": (x * 2 + y) * 4 + z}

    loads = [
        pltpu.make_async_copy(
            dist.at[pl.ds(i * VB * XL, VB * XL)], draw.at[pl.ds(i * VB * XL, VB * XL)], dsem.at[i]
        )
        for i in range(NB)
    ]
    small = [
        pltpu.make_async_copy(source, target, ssem.at[n])
        for n, (source, target) in enumerate((
            (speeds_in, speeds), (weights_in, weights), (collision_in, collision),
            (values_in, wall_values), (kind_in, wall_kind),
        ))
    ]
    for load in small + loads:
        load.start()

    peers = []
    for d in range(1, 4):
        peers.append(device(slab, (px + d) % 4, py, pz))
    for d in range(1, 4):
        peers.append(device(slab, px, py, (pz + d) % 4))
    group = py * 4 + slab
    yz = []
    for d in range(1, 8):
        other = (group + d) % 8
        yz.append(device(other % 4, px, other // 4, pz))
    barrier = pltpu.get_barrier_semaphore()
    for peer in peers + yz:
        pl.semaphore_signal(barrier, inc=1, device_id=peer, device_id_type=MESH)

    for load in small:
        load.wait()
    cx, cy, cz = speeds[0:1, :], speeds[1:2, :], speeds[2:3, :]
    wt = weights[...].reshape(1, V)
    square = cx * cx + cy * cy + cz * cz
    third = square / 3.0
    heat = square - 2.5
    one = jnp.ones_like(cx)
    zero = jnp.zeros_like(cx)
    phi = [
        one, cx, cy, cz, 2.0 / 3.0 * square - 1.0, cx * heat, cy * heat, cz * heat,
        cx * cx - third, cx * cy, cx * cz, cy * cy - third, cy * cz, zero, zero, zero,
    ]
    scale = wt / VELS
    fx = jnp.where(cx >= 0, 1.0, 0.0)
    fy = jnp.where(cy >= 0, 1.0, 0.0)
    rows = jnp.concatenate([p * scale for p in phi], axis=0)
    rows_hi, rows_lo = split(rows)
    rows_p[0:KR, :] = rows_hi
    rows_p[KR : 2 * KR, :] = rows_lo
    masks = [fx * fy, fx * (1.0 - fy), (1.0 - fx) * fy, (1.0 - fx) * (1.0 - fy)]
    for g in range(4):
        m = masks[g].astype(bf16)
        rows_g[g * KR : (g + 1) * KR, :] = rows_hi * m
        rows_g[4 * KR + g * KR : 4 * KR + (g + 1) * KR, :] = rows_lo * m

    def cast(i, c):
        at = pl.ds(i * VB, VB)
        rows_at = pl.ds(i * VB * XL, VB * XL)
        pltpu.make_async_copy(dist.at[rows_at], draw.at[rows_at], dsem.at[i]).wait()
        for x in range(XL):
            hi, lo = split(draw[pl.ds(i * VB * XL + x, VB, stride=XL), :])
            fhi[at, x * NY : (x + 1) * NY] = hi
            flo[at, x * NY : (x + 1) * NY] = lo
        return c

    lax.fori_loop(0, NB, cast, 0)
    first = dot(rows_p[...], fhi[...])
    moment = first[0:KR] + first[KR : 2 * KR] + dot(rows_p[0:KR, :], flo[...])

    pl.semaphore_wait(barrier, 13)

    axes = ((px, lambda o: device(slab, o, py, pz)), (pz, lambda o: device(slab, px, py, o)))

    def exchange(buf, stage, it, piece):
        me, to = axes[(stage + piece) % 2]
        sent = []
        for d in (2, 1, 3):
            copy = pltpu.make_async_remote_copy(
                src_ref=buf.at[it, piece, me],
                dst_ref=buf.at[it, piece, me],
                send_sem=bsend.at[it, stage, piece, d - 1],
                recv_sem=brecv.at[it, stage, piece, d - 1],
                device_id=to((me + d) % 4),
                device_id_type=MESH,
            )
            copy.start()
            sent.append(copy)
        return sent

    def arrived(buf, stage, it, piece):
        me, to = axes[(stage + piece) % 2]
        for d in range(1, 4):
            source = (me + 4 - d) % 4
            pltpu.make_async_remote_copy(
                src_ref=buf.at[it, piece, source],
                dst_ref=buf.at[it, piece, source],
                send_sem=bsend.at[it, stage, piece, d - 1],
                recv_sem=brecv.at[it, stage, piece, d - 1],
                device_id=to(source),
                device_id_type=MESH,
            ).wait_recv()
        return (buf[it, piece, 0] + buf[it, piece, 1]) + (buf[it, piece, 2] + buf[it, piece, 3])

    def hand(it, piece, n, slot, y, s):
        index = (y * 4 + s + 8 - slot) % 8 - 1
        copy = pltpu.make_async_remote_copy(
            src_ref=b3.at[it, piece, slot],
            dst_ref=b3.at[it, piece, slot],
            send_sem=ysend.at[it, piece, n],
            recv_sem=yrecv.at[it, piece, index],
            device_id=device(s, px, y, pz),
            device_id_type=MESH,
        )
        copy.start()
        return copy

    def spread(it, piece):
        targets = []
        for y in (py, 1 - py):
            targets += [(y, beside), (y, beside + 1)]
        targets.append((py, partner))
        return [hand(it, piece, n + 1, group, y, s) for n, (y, s) in enumerate(targets)]

    def forward_far(it):
        sent = []
        for piece in range(2):
            source = (group + 4) % 8
            pltpu.make_async_remote_copy(
                src_ref=b3.at[it, piece, source],
                dst_ref=b3.at[it, piece, source],
                send_sem=ysend.at[it, piece, 3],
                recv_sem=yrecv.at[it, piece, 3],
                device_id=yz[3],
                device_id_type=MESH,
            ).wait_recv()
            sent.append(hand(it, piece, 6, source, py, partner))
        return sent

    def spread_arrived(it, piece):
        for d in (1, 2, 3, 5, 6, 7):
            source = (group + 8 - d) % 8
            pltpu.make_async_remote_copy(
                src_ref=b3.at[it, piece, source],
                dst_ref=b3.at[it, piece, source],
                send_sem=ysend.at[it, piece, d - 1],
                recv_sem=yrecv.at[it, piece, d - 1],
                device_id=yz[d - 1],
                device_id_type=MESH,
            ).wait_recv()

    def start_reduce(it, value):
        sent = []
        for piece in range(2):
            b1[it, piece, axes[piece % 2][0]] = value[0:ROWS, piece * HALF : (piece + 1) * HALF]
            sent += exchange(b1, 0, it, piece)
        return sent

    def second_stage(it):
        sent = []
        for piece in range(2):
            total = arrived(b1, 0, it, piece)
            b2[it, piece, axes[(1 + piece) % 2][0]] = total
            sent += exchange(b2, 1, it, piece)
        return sent

    def third_stage(it):
        sent = []
        for piece in range(2):
            b3[it, piece, group] = arrived(b2, 1, it, piece)
            sent.append(hand(it, piece, 0, group, 1 - py, slab))
        for piece in range(2):
            sent += spread(it, piece)
        return sent

    sent = start_reduce(0, moment)
    for d in range(1, 4):
        copy = pltpu.make_async_remote_copy(
            src_ref=collision,
            dst_ref=cbuf.at[slab],
            send_sem=csend.at[d - 1],
            recv_sem=crecv.at[d - 1],
            device_id=device((slab + d) % 4, px, py, pz),
            device_id_type=MESH,
        )
        copy.start()
        sent.append(copy)
    cbuf[slab] = collision[...]

    rows_t[...] = jnp.zeros_like(rows_t)
    inflow = wall_values[...] * wall_kind[...].astype(f32)
    rate_x = jnp.abs(cx) * NX
    rate_y = jnp.abs(cy) * NY
    rows_t[0:1, :] = rate_x
    ratio = rate_y / (1.0 + rate_y)
    powers = [ratio]
    for _ in range(SEG - 1):
        powers.append(powers[-1] * ratio)
    powers.append(powers[-1] * powers[-1])
    powers.append(powers[-1] * powers[-1])
    powers += [zero, 1.0 / (1.0 + rate_y)]
    for n, power in enumerate(powers):
        for i in range(NB):
            yrow[i, n : n + 1, :] = power[:, i * VB : (i + 1) * VB]
    rows_t[3:4, :] = jnp.where(low_side, inflow[0:1], inflow[1:2])
    rows_t[4:5, :] = fx
    rows_t[5:6, :] = fy
    for i in range(NB):
        at = slice(i * VB, (i + 1) * VB)
        col[at, :] = jnp.transpose(rows_t[:, at])
    factor = 4.0 / 45.0 * heat
    psi = jnp.concatenate(
        [one, 2.0 * cx, 2.0 * cy, 2.0 * cz, square - 1.5, factor * cx, factor * cy, factor * cz],
        axis=0,
    )
    psi_hi = psi.astype(bf16).astype(f32)
    psi_lo = psi - psi_hi
    for g in range(4):
        rows_t[g * 32 : g * 32 + 8, :] = psi_hi * masks[g]
        rows_t[g * 32 + 8 : g * 32 + 16, :] = psi_hi * masks[g]
        rows_t[g * 32 + 16 : g * 32 + 24, :] = psi_lo * masks[g]
        rows_t[g * 32 + 24 : g * 32 + 32, :] = psi_lo * masks[g]
    for i in range(NB):
        at = slice(i * VB, (i + 1) * VB)
        shp[at, :] = jnp.transpose(rows_t[:, at]).astype(bf16)

    lane = lanes((VB, NY))

    def send_out(buf, target, send, recv, it, i, to):
        at = pl.ds(i * CB, CB)
        pltpu.make_async_remote_copy(
            src_ref=buf.at[it, at],
            dst_ref=target.at[it, at],
            send_sem=send.at[it, i],
            recv_sem=recv.at[it, i],
            device_id=device(to, px, py, pz),
            device_id_type=MESH,
        ).start()

    def wait_in(target, send, recv, it, i):
        at = pl.ds(i * CB, CB)
        pltpu.make_async_remote_copy(
            src_ref=target.at[it, at],
            dst_ref=target.at[it, at],
            send_sem=send.at[it, i],
            recv_sem=recv.at[it, i],
            device_id=device(partner, px, py, pz),
            device_id_type=MESH,
        ).wait_recv()

    def wait_out(buf, target, send, recv, it, i):
        at = pl.ds(i * CB, CB)
        pltpu.make_async_remote_copy(
            src_ref=buf.at[it, at],
            dst_ref=target.at[it, at],
            send_sem=send.at[it, i],
            recv_sem=recv.at[it, i],
            device_id=device(partner, px, py, pz),
            device_id_type=MESH,
        ).wait_send()

    twice = jnp.concatenate([collision[...], collision[...]], axis=0)
    own, own_back = swept(twice), swept_back(twice)

    def pass_on(it, i):
        at = pl.ds(i * CB, CB)
        wait_in(near, nsend, nrecv, it, i)
        outa[it, at, :] = prod[at, :] * near[it, at, :] + gd[XL - 1, at, :]
        send_out(outa, far, fsend, frecv, it, i, across)

    def sweep_source(fields, at):
        total = inv_own[0, at, :] * fields[0]
        gd[0, at, :] = total
        for q in range(1, XL):
            total = fac[q, at, :] * total + inv_own[q, at, :] * fields[q]
            gd[q, at, :] = total

    def chain_step(it, c):
        @pl.when(edge)
        def _():
            at = pl.ds(c * CB, CB)
            outa[it, at, :] = prod[at, :] * near[it, at, :] + gd[XL - 1, at, :]
            send_out(outa, near, nsend, nrecv, it, c, partner)

        @pl.when(jnp.logical_and(middle, c >= LAG))
        def _():
            pass_on(it, c - LAG)

    def in_groups(block, it):
        def group_of(c, carry):
            for n in range(CB // VB):
                block(c * (CB // VB) + n, 0)
            if it is not None:
                chain_step(it, c)
            return carry
        lax.fori_loop(0, NC, group_of, 0)

    def prepare(i, c):
        at = pl.ds(i * VB, VB)
        cols = col[at, :]
        wide = lambda k: jnp.broadcast_to(cols[:, k : k + 1], (VB, NY))
        a = wide(0)
        ascale[at, :] = a
        run[at, :] = jnp.ones_like(a)
        fxv, fyv = wide(4), wide(5)
        fxs[at, :] = fxv
        fys[at, :] = fyv
        forward, upward = fxv > 0.5, fyv > 0.5

        @pl.when(edge)
        def _():
            for it in range(ITERS):
                near[it, at, :] = wide(3)

        index = jnp.where(upward, cell_at(lane), NY - 1 - cell_at(lane))
        product = None
        fields = []
        for q in range(XL):
            m = XL - 1 - q
            rate = jnp.where(
                forward,
                jnp.where(upward, own[q : q + 1], own_back[q : q + 1]),
                jnp.where(upward, own[m : m + 1], own_back[m : m + 1]),
            )
            inv = 1.0 / (1.0 + a + rate)
            f = a * inv
            inv_own[q, at, :] = inv
            fac[q, at, :] = f
            wgt[PAD + q, at, :] = rate * inv
            product = f if product is None else product * f
            picked = jnp.where(
                forward,
                draw[pl.ds(i * VB * XL + q, VB, stride=XL), :],
                draw[pl.ds(i * VB * XL + m, VB, stride=XL), :],
            )
            fields.append(jnp.take_along_axis(picked, index, axis=1))
        prod[at, :] = product
        sweep_source(fields, at)
        return c

    in_groups(prepare, 0)

    def chain_across(it):
        @pl.when(middle)
        def _():
            def step(i, c):
                pass_on(it, i)
                return c
            lax.fori_loop(NC - LAG, NC, step, 0)

    def chain_back(it):
        @pl.when(middle)
        def _():
            def step(i, c):
                at = pl.ds(i * CB, CB)
                wait_in(far, fsend, frecv, it, i)
                outb[it, at, :] = prod[at, :] * far[it, at, :] + gd[XL - 1, at, :]
                pltpu.make_async_remote_copy(
                    src_ref=outb.at[it, at],
                    dst_ref=far.at[it, at],
                    send_sem=nsend.at[it, i],
                    recv_sem=frecv.at[it, i],
                    device_id=device(partner, px, py, pz),
                    device_id_type=MESH,
                ).start()
                return c
            lax.fori_loop(0, NC, step, 0)

    def drain_chain(it):
        @pl.when(middle)
        def _():
            def step(i, c):
                wait_out(outa, far, fsend, frecv, it, i)
                wait_out(outb, far, nsend, frecv, it, i)
                return c
            lax.fori_loop(0, NC, step, 0)

        @pl.when(edge)
        def _():
            def step(i, c):
                wait_out(outa, near, nsend, nrecv, it, i)
                return c
            lax.fori_loop(0, NC, step, 0)

    sent += second_stage(0)
    chain_across(0)

    for d in range(1, 4):
        source = (slab + 4 - d) % 4
        pltpu.make_async_remote_copy(
            src_ref=collision,
            dst_ref=cbuf.at[source],
            send_sem=csend.at[d - 1],
            recv_sem=crecv.at[d - 1],
            device_id=device(source, px, py, pz),
            device_id_type=MESH,
        ).wait_recv()
    crow[...] = jnp.zeros_like(crow)
    everywhere = jnp.concatenate([cbuf[s] for s in range(SLABS)], axis=0)
    ahead_rows, back_rows = swept(everywhere), swept_back(everywhere)
    for i in range(NX):
        for n, source in enumerate((ahead_rows, back_rows, everywhere)):
            crow[n, PAD + i] = jnp.broadcast_to(source[i : i + 1], (8, NY))
    dpad[...] = jnp.zeros_like(dpad)
    for i in range(NX):
        stiff = 1.0 / crow[2, PAD + i]
        kappa_s[i] = stiff
        down_s[i] = 1.0 / (1.0 + 4.0 * stiff)

    def upstream(start, stop):
        def at_cell(n, c):
            r = PAD - 1 - n
            ahead = XL * slab + r
            behind = XL * slab + PAD + NX - 1 - r
            c_ff = crow[0, ahead][0:1]
            c_fb = crow[1, ahead][0:1]
            c_bf = crow[0, behind][0:1]
            c_bb = crow[1, behind][0:1]
            def block(i, c):
                at = pl.ds(i * VB, VB)
                a = ascale[at, :]
                forward, upward = fxs[at, :] > 0.5, fys[at, :] > 0.5
                rate = jnp.where(
                    forward, jnp.where(upward, c_ff, c_fb), jnp.where(upward, c_bf, c_bb)
                )
                inv = 1.0 / (1.0 + a + rate)
                through = run[at, :]
                wgt[r, at, :] = rate * inv * through
                run[at, :] = a * inv * through
                return c
            lax.fori_loop(0, NB, block, 0)
            return c
        lax.fori_loop(start, stop, at_cell, 0)

    upstream(0, 5)
    sent += third_stage(0)
    chain_back(0)
    upstream(5, PAD)
    sent += forward_far(0)

    cell = lanes((8, NY))
    sub = lax.broadcasted_iota(jnp.int32, (8, NY), 0)

    def above(value):
        return jnp.where(cell < NY - 1, pltpu.roll(value, NY - 1, 1), 0.0)

    def below(value):
        return jnp.where(cell >= 1, pltpu.roll(value, 1, 1), 0.0)

    def macro(it):
        for piece in range(2):
            spread_arrived(it, piece)
        head, flux = [], []
        for i in range(NX):
            s, x = i // XL, i % XL
            piece, at = x // 2, slice((x % 2) * NY, (x % 2 + 1) * NY)
            head.append(b3[it, piece, s, 0:8, at] + b3[it, piece, 4 + s, 0:8, at])
            flux.append(b3[it, piece, s, 8:ROWS, at] + b3[it, piece, 4 + s, 8:ROWS, at])
        nothing = jnp.zeros((8, NY), f32)
        along = [
            jnp.concatenate([a[1:2], b[0:3], a[5:6], a[5:8]], axis=0) for a, b in zip(head, flux)
        ]
        target, kappa, down = [], [], []
        for i in range(NX):
            a, b = head[i], flux[i]
            cross = jnp.concatenate([a[2:3], b[1:2], b[3:5], a[6:7], a[5:8]], axis=0)
            right = along[i + 1] if i + 1 < NX else nothing
            left = along[i - 1] if i > 0 else nothing
            target.append(a - (0.5 * (right - left) + 0.5 * (above(cross) - below(cross))))
            kappa.append(kappa_s[i])
            down.append(down_s[i])
        settled = head
        for _ in range(JACOBI):
            after = []
            for i in range(NX):
                right = settled[i + 1] if i + 1 < NX else nothing
                left = settled[i - 1] if i > 0 else nothing
                around = right + left + above(settled[i]) + below(settled[i])
                after.append((target[i] + kappa[i] * around) * down[i])
            settled = after
        for i in range(NX):
            drive = jnp.where(sub < 5, settled[i], head[i])
            drive_s[i] = drive
            hi, lo = split(swept(drive))
            dpad[0, PAD + i] = jnp.concatenate([hi, lo], axis=0)
            hi, lo = split(swept_back(drive))
            dpad[1, PAD + i] = jnp.concatenate([hi, lo], axis=0)
        for r in range(NX):
            ahead = XL * slab + r
            behind = XL * slab + PAD + NX - 1 - r
            at = slice(r * NY, (r + 1) * NY)
            for g, tile in enumerate(
                (dpad[0, ahead], dpad[1, ahead], dpad[0, behind], dpad[1, behind])
            ):
                rhs[g * 32 : g * 32 + 16, at] = tile
                rhs[g * 32 + 16 : g * 32 + 32, at] = tile

    segment = lax.broadcasted_iota(jnp.int32, (8, NY), 0)

    def along_y(g, table):
        columns = jnp.transpose(g)
        ratio, scale = table[0:1], table[SEG + 3 : SEG + 4]
        inner = []
        for t in range(SEG):
            h = columns[8 * t : 8 * t + 8] * scale
            inner.append(h + ratio * inner[-1] if t else h)
        ends = inner[-1]
        for n, step in enumerate((1, 2, 4)):
            moved = jnp.where(segment >= step, pltpu.roll(ends, step, 0), 0.0)
            k = SEG - 1 + n
            ends = ends + table[k : k + 1] * moved
        carry = jnp.where(segment >= 1, pltpu.roll(ends, 1, 0), 0.0)
        whole = [inner[t] + table[t : t + 1] * carry for t in range(SEG)]
        return jnp.transpose(jnp.concatenate(whole, axis=0))

    def main(it):
        last = it == ITERS - 1

        @pl.when(edge)
        def _():
            def ready(i, c):
                wait_in(far, fsend, frecv, it, i)
                return c
            lax.fori_loop(0, NC, ready, 0)

        def block(i, c):
            at = pl.ds(i * VB, VB)
            eq = dot(shp[at, :], rhs[...])
            enter = wgt[0, at, :] * eq[:, 0:NY]
            for r in range(1, PAD):
                enter = enter + wgt[r, at, :] * eq[:, r * NY : (r + 1) * NY]
            forward = fxs[at, :] > 0.5
            from_near = jnp.where(low_side, fxs[at, :], 1.0 - fxs[at, :]) > 0.5
            enter = enter + jnp.where(from_near, near[it, at, :], far[it, at, :])
            fields = []
            for q in range(XL):
                r = PAD + q
                enter = fac[q, at, :] * enter + wgt[r, at, :] * eq[:, r * NY : (r + 1) * NY]
                h = along_y(gd[q, at, :] + enter, yrow[i])
                fields.append(h)
                if not last:
                    hi, lo = split(h)
                    fhi[at, q * NY : (q + 1) * NY] = hi
                    flo[at, q * NY : (q + 1) * NY] = lo
            if last:
                index = jnp.where(fys[at, :] > 0.5, lane_of(lane), lane_of(NY - 1 - lane))
                for x in range(XL):
                    picked = jnp.where(forward, fields[x], fields[XL - 1 - x])
                    out[pl.ds(i * VB * XL + x, VB, stride=XL), :] = jnp.take_along_axis(
                        picked, index, axis=1
                    )
            else:
                sweep_source(fields, at)
            return c

        in_groups(block, None if last else it + 1)

    for it in range(ITERS):
        macro(it)
        main(it)
        if it < ITERS - 1:
            first = dot(rows_g[...], fhi[...])
            groups = first[0 : 4 * KR] + first[4 * KR : 8 * KR] + dot(rows_g[0 : 4 * KR, :], flo[...])
            turn = lambda t: jnp.concatenate(
                [t[:, x * NY : (x + 1) * NY] for x in reversed(range(XL))], axis=1
            )
            up = groups[0:KR] + turn(groups[2 * KR : 3 * KR])
            down = groups[KR : 2 * KR] + turn(groups[3 * KR : 4 * KR])
            spans = [slice(x * NY, (x + 1) * NY) for x in range(XL)]
            moment = jnp.concatenate(
                [restored(up[:, at]) + restored_back(down[:, at]) for at in spans], axis=1
            )
            sent += start_reduce(it + 1, moment)
            chain_across(it + 1)
            sent += second_stage(it + 1)
            chain_back(it + 1)
            sent += third_stage(it + 1)
            sent += forward_far(it + 1)
            for done in range(ITERS):
                drain_chain(done)
            for copy in sent:
                copy.wait_send()

    for x in range(XL):
        settled_out[:, x, :] = drive_s[XL * slab + x][0:5]


def copy_out(rows, settled, rows_out, settled_out, sem):
    copies = [
        pltpu.make_async_copy(settled, settled_out, sem.at[0]),
        pltpu.make_async_copy(rows, rows_out, sem.at[1]),
    ]
    for copy in copies:
        copy.start()
    for copy in copies:
        copy.wait()


def on_device(dist, speeds, weights, collision, wall_values, wall_kind):
    vmem = pl.BlockSpec(memory_space=pltpu.VMEM)
    hbm = pl.BlockSpec(memory_space=pltpu.HBM)
    dma = pltpu.SemaphoreType.DMA
    full = (V, NY)
    scratch = [
        pltpu.VMEM((V * XL, NY), f32),
        pltpu.VMEM((XL, *full), f32),
        pltpu.VMEM((V, XL * NY), bf16),
        pltpu.VMEM((V, XL * NY), bf16),
        pltpu.VMEM((XL, *full), f32),
        pltpu.VMEM((NX, *full), f32),
        pltpu.VMEM((XL, *full), f32),
        pltpu.VMEM(full, f32),
        pltpu.VMEM((NB, TABLE, VB), f32),
        pltpu.VMEM(full, f32),
        pltpu.VMEM(full, f32),
        pltpu.VMEM((NX, 8, NY), f32),
        pltpu.VMEM((NX, 8, NY), f32),
        pltpu.VMEM(full, f32),
        pltpu.VMEM(full, f32),
        pltpu.VMEM((ITERS, *full), f32),
        pltpu.VMEM((ITERS, *full), f32),
        pltpu.VMEM((ITERS, *full), f32),
        pltpu.VMEM((ITERS, *full), f32),
        pltpu.VMEM((128, V), f32),
        pltpu.VMEM((2 * KR, V), bf16),
        pltpu.VMEM((8 * KR, V), bf16),
        pltpu.VMEM((V, 128), bf16),
        pltpu.VMEM((V, 128), f32),
        pltpu.VMEM((ITERS, 2, 4, ROWS, HALF), f32),
        pltpu.VMEM((ITERS, 2, 4, ROWS, HALF), f32),
        pltpu.VMEM((ITERS, 2, 8, ROWS, HALF), f32),
        pltpu.VMEM((SLABS, XL, NY), f32),
        pltpu.VMEM((3, NX + 2 * PAD, 8, NY), f32),
        pltpu.VMEM((2, NX + 2 * PAD, 16, NY), bf16),
        pltpu.VMEM((128, NX * NY), bf16),
        pltpu.VMEM((NX, 8, NY), f32),
        pltpu.VMEM((3, V), f32),
        pltpu.VMEM((V,), f32),
        pltpu.VMEM((XL, NY), f32),
        pltpu.VMEM((2, V), f32),
        pltpu.VMEM((2, V), jnp.int32),
        dma((NB,)),
        dma((5,)),
        dma((ITERS, 2, 2, 3)),
        dma((ITERS, 2, 2, 3)),
        dma((ITERS, 2, 7)),
        dma((ITERS, 2, 7)),
        dma((3,)),
        dma((3,)),
        dma((ITERS, NC)),
        dma((ITERS, NC)),
        dma((ITERS, NC)),
        dma((ITERS, NC)),
    ]
    rows, settled = pl.pallas_call(
        transport_kernel,
        out_shape=(
            jax.ShapeDtypeStruct((V * XL, NY), f32),
            jax.ShapeDtypeStruct((5, XL, NY), f32),
        ),
        in_specs=[hbm] * 6,
        out_specs=(vmem, vmem),
        scratch_shapes=scratch,
        compiler_params=pltpu.CompilerParams(
            collective_id=0, has_side_effects=True, vmem_limit_bytes=50000000
        ),
        name="transport",
    )(*(
        pltpu.with_memory_space_constraint(value, pltpu.HBM)
        for value in (dist.reshape(V * XL, NY), speeds, weights, collision, wall_values, wall_kind)
    ))
    anywhere = pl.BlockSpec(memory_space=pl.ANY)
    rows, settled = pl.pallas_call(
        copy_out,
        out_shape=(
            jax.ShapeDtypeStruct((V * XL, NY), f32),
            jax.ShapeDtypeStruct((5, XL, NY), f32),
        ),
        in_specs=[anywhere, anywhere],
        out_specs=(hbm, hbm),
        scratch_shapes=[dma((2,))],
        compiler_params=pltpu.CompilerParams(vmem_limit_bytes=1024 * 1024),
        name="copy_out",
    )(rows, settled)
    return rows.reshape(V, XL, NY), settled


def solution(mesh):
    return jax.shard_map(
        on_device,
        mesh=mesh,
        in_specs=(
            P("vel", "slab", None),
            P(None, "vel"),
            P("vel"),
            P("slab", None),
            P(None, "vel"),
            P(None, "vel"),
        ),
        out_specs=(P("vel", "slab", None), P(None, "slab", None)),
        check_vma=False,
    )
```

```python
import jax
import jax.numpy as jnp
from jax import lax
from jax.experimental import pallas as pl
from jax.experimental.pallas import tpu as pltpu
from jax.sharding import PartitionSpec as P

VELS = 24576
ITERS = 2
JACOBI = 2
NX = 16
NY = 128
SLABS = 4
XL = NX // SLABS
V = VELS // 32
VB = 128
NB = V // VB
CB = 256
NC = V // CB
PAD = NX - XL
KR = 16
ROWS = 13
LAG = 1
HALF = XL * NY // 2
SEG = NY // 8
TABLE = SEG + 4

f32 = jnp.float32
bf16 = jnp.bfloat16
MESH = pl.DeviceIdType.MESH


def split(value):
    high = value.astype(bf16)
    return high, (value - high.astype(f32)).astype(bf16)


def dot(a, b):
    return jnp.dot(a, b, preferred_element_type=f32)


def lanes(shape):
    return lax.broadcasted_iota(jnp.int32, shape, 1)


def pick(value, index):
    return jnp.take_along_axis(value, index, axis=1)


def cell_at(lane):
    return (lane % 8) * SEG + lane // 8


def lane_of(cell):
    return (cell % SEG) * 8 + cell // SEG


def swept(value):
    return pick(value, cell_at(lanes(value.shape)))


def swept_back(value):
    return pick(value, NY - 1 - cell_at(lanes(value.shape)))


def restored(value):
    return pick(value, lane_of(lanes(value.shape)))


def restored_back(value):
    return pick(value, lane_of(NY - 1 - lanes(value.shape)))


def transport_kernel(
    dist, speeds_in, weights_in, collision_in, values_in, kind_in,
    out, settled_out,
    draw, gd, fhi, flo, fac, wgt, inv_own, prod, yrow, ascale, run, kappa_s, down_s, fxs, fys,
    near, far, outa, outb, rows_t, rows_p, rows_g, shp, col,
    b1, b2, b3, cbuf, crow, dpad, rhs, drive_s,
    speeds, weights, collision, wall_values, wall_kind,
    dsem, ssem, bsend, brecv, ysend, yrecv, csend, crecv, nsend, nrecv, fsend, frecv,
):
    slab = lax.axis_index("slab")
    vel = lax.axis_index("vel")
    px = vel // 8
    py = (vel // 4) % 2
    pz = vel % 4
    edge = jnp.logical_or(slab == 0, slab == SLABS - 1)
    middle = jnp.logical_and(slab > 0, slab < SLABS - 1)
    low_side = slab < 2
    partner = jnp.where(low_side, 1 - slab, 5 - slab)
    across = 3 - slab
    beside = jnp.where(low_side, 2, 0)

    def device(s, x, y, z):
        return {"slab": s, "vel": (x * 2 + y) * 4 + z}

    loads = [
        pltpu.make_async_copy(
            dist.at[pl.ds(i * VB * XL, VB * XL)], draw.at[pl.ds(i * VB * XL, VB * XL)], dsem.at[i]
        )
        for i in range(NB)
    ]
    small = [
        pltpu.make_async_copy(source, target, ssem.at[n])
        for n, (source, target) in enumerate((
            (speeds_in, speeds), (weights_in, weights), (collision_in, collision),
            (values_in, wall_values), (kind_in, wall_kind),
        ))
    ]
    for load in small + loads:
        load.start()

    peers = []
    for d in range(1, 4):
        peers.append(device(slab, (px + d) % 4, py, pz))
    for d in range(1, 4):
        peers.append(device(slab, px, py, (pz + d) % 4))
    group = py * 4 + slab
    yz = []
    for d in range(1, 8):
        other = (group + d) % 8
        yz.append(device(other % 4, px, other // 4, pz))
    barrier = pltpu.get_barrier_semaphore()
    for peer in peers + yz:
        pl.semaphore_signal(barrier, inc=1, device_id=peer, device_id_type=MESH)

    for load in small:
        load.wait()
    cx, cy, cz = speeds[0:1, :], speeds[1:2, :], speeds[2:3, :]
    wt = weights[...].reshape(1, V)
    square = cx * cx + cy * cy + cz * cz
    third = square / 3.0
    heat = square - 2.5
    one = jnp.ones_like(cx)
    zero = jnp.zeros_like(cx)
    phi = [
        one, cx, cy, cz, 2.0 / 3.0 * square - 1.0, cx * heat, cy * heat, cz * heat,
        cx * cx - third, cx * cy, cx * cz, cy * cy - third, cy * cz, zero, zero, zero,
    ]
    scale = wt / VELS
    fx = jnp.where(cx >= 0, 1.0, 0.0)
    fy = jnp.where(cy >= 0, 1.0, 0.0)
    rows = jnp.concatenate([p * scale for p in phi], axis=0)
    rows_hi, rows_lo = split(rows)
    rows_p[0:KR, :] = rows_hi
    rows_p[KR : 2 * KR, :] = rows_lo
    masks = [fx * fy, fx * (1.0 - fy), (1.0 - fx) * fy, (1.0 - fx) * (1.0 - fy)]
    for g in range(4):
        m = masks[g].astype(bf16)
        rows_g[g * KR : (g + 1) * KR, :] = rows_hi * m
        rows_g[4 * KR + g * KR : 4 * KR + (g + 1) * KR, :] = rows_lo * m

    def cast(i, c):
        at = pl.ds(i * VB, VB)
        rows_at = pl.ds(i * VB * XL, VB * XL)
        pltpu.make_async_copy(dist.at[rows_at], draw.at[rows_at], dsem.at[i]).wait()
        for x in range(XL):
            hi, lo = split(draw[pl.ds(i * VB * XL + x, VB, stride=XL), :])
            fhi[at, x * NY : (x + 1) * NY] = hi
            flo[at, x * NY : (x + 1) * NY] = lo
        return c

    lax.fori_loop(0, NB, cast, 0)
    first = dot(rows_p[...], fhi[...])
    moment = first[0:KR] + first[KR : 2 * KR] + dot(rows_p[0:KR, :], flo[...])

    pl.semaphore_wait(barrier, 13)

    axes = ((px, lambda o: device(slab, o, py, pz)), (pz, lambda o: device(slab, px, py, o)))

    def exchange(buf, stage, it, piece):
        me, to = axes[(stage + piece) % 2]
        sent = []
        for d in (2, 1, 3):
            copy = pltpu.make_async_remote_copy(
                src_ref=buf.at[it, piece, me],
                dst_ref=buf.at[it, piece, me],
                send_sem=bsend.at[it, stage, piece, d - 1],
                recv_sem=brecv.at[it, stage, piece, d - 1],
                device_id=to((me + d) % 4),
                device_id_type=MESH,
            )
            copy.start()
            sent.append(copy)
        return sent

    def arrived(buf, stage, it, piece):
        me, to = axes[(stage + piece) % 2]
        for d in range(1, 4):
            source = (me + 4 - d) % 4
            pltpu.make_async_remote_copy(
                src_ref=buf.at[it, piece, source],
                dst_ref=buf.at[it, piece, source],
                send_sem=bsend.at[it, stage, piece, d - 1],
                recv_sem=brecv.at[it, stage, piece, d - 1],
                device_id=to(source),
                device_id_type=MESH,
            ).wait_recv()
        return (buf[it, piece, 0] + buf[it, piece, 1]) + (buf[it, piece, 2] + buf[it, piece, 3])

    def hand(it, piece, n, slot, y, s):
        index = (y * 4 + s + 8 - slot) % 8 - 1
        copy = pltpu.make_async_remote_copy(
            src_ref=b3.at[it, piece, slot],
            dst_ref=b3.at[it, piece, slot],
            send_sem=ysend.at[it, piece, n],
            recv_sem=yrecv.at[it, piece, index],
            device_id=device(s, px, y, pz),
            device_id_type=MESH,
        )
        copy.start()
        return copy

    def spread(it, piece):
        targets = []
        for y in (py, 1 - py):
            targets += [(y, beside), (y, beside + 1)]
        targets.append((py, partner))
        return [hand(it, piece, n + 1, group, y, s) for n, (y, s) in enumerate(targets)]

    def forward_far(it):
        sent = []
        for piece in range(2):
            source = (group + 4) % 8
            pltpu.make_async_remote_copy(
                src_ref=b3.at[it, piece, source],
                dst_ref=b3.at[it, piece, source],
                send_sem=ysend.at[it, piece, 3],
                recv_sem=yrecv.at[it, piece, 3],
                device_id=yz[3],
                device_id_type=MESH,
            ).wait_recv()
            sent.append(hand(it, piece, 6, source, py, partner))
        return sent

    def spread_arrived(it, piece):
        for d in (1, 2, 3, 5, 6, 7):
            source = (group + 8 - d) % 8
            pltpu.make_async_remote_copy(
                src_ref=b3.at[it, piece, source],
                dst_ref=b3.at[it, piece, source],
                send_sem=ysend.at[it, piece, d - 1],
                recv_sem=yrecv.at[it, piece, d - 1],
                device_id=yz[d - 1],
                device_id_type=MESH,
            ).wait_recv()

    def start_reduce(it, value):
        sent = []
        for piece in range(2):
            b1[it, piece, axes[piece % 2][0]] = value[0:ROWS, piece * HALF : (piece + 1) * HALF]
            sent += exchange(b1, 0, it, piece)
        return sent

    def second_stage(it):
        sent = []
        for piece in range(2):
            total = arrived(b1, 0, it, piece)
            b2[it, piece, axes[(1 + piece) % 2][0]] = total
            sent += exchange(b2, 1, it, piece)
        return sent

    def third_stage(it):
        sent = []
        for piece in range(2):
            b3[it, piece, group] = arrived(b2, 1, it, piece)
            sent.append(hand(it, piece, 0, group, 1 - py, slab))
        for piece in range(2):
            sent += spread(it, piece)
        return sent

    sent = start_reduce(0, moment)
    for d in range(1, 4):
        copy = pltpu.make_async_remote_copy(
            src_ref=collision,
            dst_ref=cbuf.at[slab],
            send_sem=csend.at[d - 1],
            recv_sem=crecv.at[d - 1],
            device_id=device((slab + d) % 4, px, py, pz),
            device_id_type=MESH,
        )
        copy.start()
        sent.append(copy)
    cbuf[slab] = collision[...]

    rows_t[...] = jnp.zeros_like(rows_t)
    inflow = wall_values[...] * wall_kind[...].astype(f32)
    rate_x = jnp.abs(cx) * NX
    rate_y = jnp.abs(cy) * NY
    rows_t[0:1, :] = rate_x
    ratio = rate_y / (1.0 + rate_y)
    powers = [ratio]
    for _ in range(SEG - 1):
        powers.append(powers[-1] * ratio)
    powers.append(powers[-1] * powers[-1])
    powers.append(powers[-1] * powers[-1])
    powers += [zero, 1.0 / (1.0 + rate_y)]
    for n, power in enumerate(powers):
        for i in range(NB):
            yrow[i, n : n + 1, :] = power[:, i * VB : (i + 1) * VB]
    rows_t[3:4, :] = jnp.where(low_side, inflow[0:1], inflow[1:2])
    rows_t[4:5, :] = fx
    rows_t[5:6, :] = fy
    for i in range(NB):
        at = slice(i * VB, (i + 1) * VB)
        col[at, :] = jnp.transpose(rows_t[:, at])
    factor = 4.0 / 45.0 * heat
    psi = jnp.concatenate(
        [one, 2.0 * cx, 2.0 * cy, 2.0 * cz, square - 1.5, factor * cx, factor * cy, factor * cz],
        axis=0,
    )
    psi_hi = psi.astype(bf16).astype(f32)
    psi_lo = psi - psi_hi
    for g in range(4):
        rows_t[g * 32 : g * 32 + 8, :] = psi_hi * masks[g]
        rows_t[g * 32 + 8 : g * 32 + 16, :] = psi_hi * masks[g]
        rows_t[g * 32 + 16 : g * 32 + 24, :] = psi_lo * masks[g]
        rows_t[g * 32 + 24 : g * 32 + 32, :] = psi_lo * masks[g]
    for i in range(NB):
        at = slice(i * VB, (i + 1) * VB)
        shp[at, :] = jnp.transpose(rows_t[:, at]).astype(bf16)

    lane = lanes((VB, NY))

    def send_out(buf, target, send, recv, it, i, to):
        at = pl.ds(i * CB, CB)
        pltpu.make_async_remote_copy(
            src_ref=buf.at[it, at],
            dst_ref=target.at[it, at],
            send_sem=send.at[it, i],
            recv_sem=recv.at[it, i],
            device_id=device(to, px, py, pz),
            device_id_type=MESH,
        ).start()

    def wait_in(target, send, recv, it, i):
        at = pl.ds(i * CB, CB)
        pltpu.make_async_remote_copy(
            src_ref=target.at[it, at],
            dst_ref=target.at[it, at],
            send_sem=send.at[it, i],
            recv_sem=recv.at[it, i],
            device_id=device(partner, px, py, pz),
            device_id_type=MESH,
        ).wait_recv()

    def wait_out(buf, target, send, recv, it, i):
        at = pl.ds(i * CB, CB)
        pltpu.make_async_remote_copy(
            src_ref=buf.at[it, at],
            dst_ref=target.at[it, at],
            send_sem=send.at[it, i],
            recv_sem=recv.at[it, i],
            device_id=device(partner, px, py, pz),
            device_id_type=MESH,
        ).wait_send()

    twice = jnp.concatenate([collision[...], collision[...]], axis=0)
    own, own_back = swept(twice), swept_back(twice)

    def pass_on(it, i):
        at = pl.ds(i * CB, CB)
        wait_in(near, nsend, nrecv, it, i)
        outa[it, at, :] = prod[at, :] * near[it, at, :] + gd[XL - 1, at, :]
        send_out(outa, far, fsend, frecv, it, i, across)

    def sweep_source(fields, at):
        total = inv_own[0, at, :] * fields[0]
        gd[0, at, :] = total
        for q in range(1, XL):
            total = fac[q, at, :] * total + inv_own[q, at, :] * fields[q]
            gd[q, at, :] = total

    def chain_step(it, c):
        @pl.when(edge)
        def _():
            at = pl.ds(c * CB, CB)
            outa[it, at, :] = prod[at, :] * near[it, at, :] + gd[XL - 1, at, :]
            send_out(outa, near, nsend, nrecv, it, c, partner)

        @pl.when(jnp.logical_and(middle, c >= LAG))
        def _():
            pass_on(it, c - LAG)

    def in_groups(block, it):
        def group_of(c, carry):
            for n in range(CB // VB):
                block(c * (CB // VB) + n, 0)
            if it is not None:
                chain_step(it, c)
            return carry
        lax.fori_loop(0, NC, group_of, 0)

    def prepare(i, c):
        at = pl.ds(i * VB, VB)
        cols = col[at, :]
        wide = lambda k: jnp.broadcast_to(cols[:, k : k + 1], (VB, NY))
        a = wide(0)
        ascale[at, :] = a
        run[at, :] = jnp.ones_like(a)
        fxv, fyv = wide(4), wide(5)
        fxs[at, :] = fxv
        fys[at, :] = fyv
        forward, upward = fxv > 0.5, fyv > 0.5

        @pl.when(edge)
        def _():
            for it in range(ITERS):
                near[it, at, :] = wide(3)

        index = jnp.where(upward, cell_at(lane), NY - 1 - cell_at(lane))
        product = None
        fields = []
        for q in range(XL):
            m = XL - 1 - q
            rate = jnp.where(
                forward,
                jnp.where(upward, own[q : q + 1], own_back[q : q + 1]),
                jnp.where(upward, own[m : m + 1], own_back[m : m + 1]),
            )
            inv = 1.0 / (1.0 + a + rate)
            f = a * inv
            inv_own[q, at, :] = inv
            fac[q, at, :] = f
            wgt[PAD + q, at, :] = rate * inv
            product = f if product is None else product * f
            picked = jnp.where(
                forward,
                draw[pl.ds(i * VB * XL + q, VB, stride=XL), :],
                draw[pl.ds(i * VB * XL + m, VB, stride=XL), :],
            )
            fields.append(jnp.take_along_axis(picked, index, axis=1))
        prod[at, :] = product
        sweep_source(fields, at)
        return c

    in_groups(prepare, 0)

    def chain_across(it):
        @pl.when(middle)
        def _():
            def step(i, c):
                pass_on(it, i)
                return c
            lax.fori_loop(NC - LAG, NC, step, 0)

    def chain_back(it):
        @pl.when(middle)
        def _():
            def step(i, c):
                at = pl.ds(i * CB, CB)
                wait_in(far, fsend, frecv, it, i)
                outb[it, at, :] = prod[at, :] * far[it, at, :] + gd[XL - 1, at, :]
                pltpu.make_async_remote_copy(
                    src_ref=outb.at[it, at],
                    dst_ref=far.at[it, at],
                    send_sem=nsend.at[it, i],
                    recv_sem=frecv.at[it, i],
                    device_id=device(partner, px, py, pz),
                    device_id_type=MESH,
                ).start()
                return c
            lax.fori_loop(0, NC, step, 0)

    def drain_chain(it):
        @pl.when(middle)
        def _():
            def step(i, c):
                wait_out(outa, far, fsend, frecv, it, i)
                wait_out(outb, far, nsend, frecv, it, i)
                return c
            lax.fori_loop(0, NC, step, 0)

        @pl.when(edge)
        def _():
            def step(i, c):
                wait_out(outa, near, nsend, nrecv, it, i)
                return c
            lax.fori_loop(0, NC, step, 0)

    sent += second_stage(0)
    chain_across(0)

    for d in range(1, 4):
        source = (slab + 4 - d) % 4
        pltpu.make_async_remote_copy(
            src_ref=collision,
            dst_ref=cbuf.at[source],
            send_sem=csend.at[d - 1],
            recv_sem=crecv.at[d - 1],
            device_id=device(source, px, py, pz),
            device_id_type=MESH,
        ).wait_recv()
    crow[...] = jnp.zeros_like(crow)
    everywhere = jnp.concatenate([cbuf[s] for s in range(SLABS)], axis=0)
    ahead_rows, back_rows = swept(everywhere), swept_back(everywhere)
    for i in range(NX):
        for n, source in enumerate((ahead_rows, back_rows, everywhere)):
            crow[n, PAD + i] = jnp.broadcast_to(source[i : i + 1], (8, NY))
    dpad[...] = jnp.zeros_like(dpad)
    for i in range(NX):
        stiff = 1.0 / crow[2, PAD + i]
        kappa_s[i] = stiff
        down_s[i] = 1.0 / (1.0 + 4.0 * stiff)

    def upstream(start, stop):
        def at_cell(n, c):
            r = PAD - 1 - n
            ahead = XL * slab + r
            behind = XL * slab + PAD + NX - 1 - r
            c_ff = crow[0, ahead][0:1]
            c_fb = crow[1, ahead][0:1]
            c_bf = crow[0, behind][0:1]
            c_bb = crow[1, behind][0:1]
            def block(i, c):
                at = pl.ds(i * VB, VB)
                a = ascale[at, :]
                forward, upward = fxs[at, :] > 0.5, fys[at, :] > 0.5
                rate = jnp.where(
                    forward, jnp.where(upward, c_ff, c_fb), jnp.where(upward, c_bf, c_bb)
                )
                inv = 1.0 / (1.0 + a + rate)
                through = run[at, :]
                wgt[r, at, :] = rate * inv * through
                run[at, :] = a * inv * through
                return c
            lax.fori_loop(0, NB, block, 0)
            return c
        lax.fori_loop(start, stop, at_cell, 0)

    upstream(0, 4)
    sent += third_stage(0)
    chain_back(0)
    upstream(4, 9)
    sent += forward_far(0)
    upstream(9, PAD)

    cell = lanes((8, NY))
    sub = lax.broadcasted_iota(jnp.int32, (8, NY), 0)

    def above(value):
        return jnp.where(cell < NY - 1, pltpu.roll(value, NY - 1, 1), 0.0)

    def below(value):
        return jnp.where(cell >= 1, pltpu.roll(value, 1, 1), 0.0)

    def macro(it):
        for piece in range(2):
            spread_arrived(it, piece)
        head, flux = [], []
        for i in range(NX):
            s, x = i // XL, i % XL
            piece, at = x // 2, slice((x % 2) * NY, (x % 2 + 1) * NY)
            head.append(b3[it, piece, s, 0:8, at] + b3[it, piece, 4 + s, 0:8, at])
            flux.append(b3[it, piece, s, 8:ROWS, at] + b3[it, piece, 4 + s, 8:ROWS, at])
        nothing = jnp.zeros((8, NY), f32)
        along = [
            jnp.concatenate([a[1:2], b[0:3], a[5:6], a[5:8]], axis=0) for a, b in zip(head, flux)
        ]
        target, kappa, down = [], [], []
        for i in range(NX):
            a, b = head[i], flux[i]
            cross = jnp.concatenate([a[2:3], b[1:2], b[3:5], a[6:7], a[5:8]], axis=0)
            right = along[i + 1] if i + 1 < NX else nothing
            left = along[i - 1] if i > 0 else nothing
            target.append(a - (0.5 * (right - left) + 0.5 * (above(cross) - below(cross))))
            kappa.append(kappa_s[i])
            down.append(down_s[i])
        settled = head
        for _ in range(JACOBI):
            after = []
            for i in range(NX):
                right = settled[i + 1] if i + 1 < NX else nothing
                left = settled[i - 1] if i > 0 else nothing
                around = right + left + above(settled[i]) + below(settled[i])
                after.append((target[i] + kappa[i] * around) * down[i])
            settled = after
        for i in range(NX):
            drive = jnp.where(sub < 5, settled[i], head[i])
            drive_s[i] = drive
            hi, lo = split(swept(drive))
            dpad[0, PAD + i] = jnp.concatenate([hi, lo], axis=0)
            hi, lo = split(swept_back(drive))
            dpad[1, PAD + i] = jnp.concatenate([hi, lo], axis=0)
        for r in range(NX):
            ahead = XL * slab + r
            behind = XL * slab + PAD + NX - 1 - r
            at = slice(r * NY, (r + 1) * NY)
            for g, tile in enumerate(
                (dpad[0, ahead], dpad[1, ahead], dpad[0, behind], dpad[1, behind])
            ):
                rhs[g * 32 : g * 32 + 16, at] = tile
                rhs[g * 32 + 16 : g * 32 + 32, at] = tile

    segment = lax.broadcasted_iota(jnp.int32, (8, NY), 0)

    def along_y(g, table):
        columns = jnp.transpose(g)
        ratio, scale = table[0:1], table[SEG + 3 : SEG + 4]
        inner = []
        for t in range(SEG):
            h = columns[8 * t : 8 * t + 8] * scale
            inner.append(h + ratio * inner[-1] if t else h)
        ends = inner[-1]
        for n, step in enumerate((1, 2, 4)):
            moved = jnp.where(segment >= step, pltpu.roll(ends, step, 0), 0.0)
            k = SEG - 1 + n
            ends = ends + table[k : k + 1] * moved
        carry = jnp.where(segment >= 1, pltpu.roll(ends, 1, 0), 0.0)
        whole = [inner[t] + table[t : t + 1] * carry for t in range(SEG)]
        return jnp.transpose(jnp.concatenate(whole, axis=0))

    def main(it):
        last = it == ITERS - 1

        @pl.when(edge)
        def _():
            def ready(i, c):
                wait_in(far, fsend, frecv, it, i)
                return c
            lax.fori_loop(0, NC, ready, 0)

        def block(i, c):
            at = pl.ds(i * VB, VB)
            eq = dot(shp[at, :], rhs[...])
            enter = wgt[0, at, :] * eq[:, 0:NY]
            for r in range(1, PAD):
                enter = enter + wgt[r, at, :] * eq[:, r * NY : (r + 1) * NY]
            forward = fxs[at, :] > 0.5
            from_near = jnp.where(low_side, fxs[at, :], 1.0 - fxs[at, :]) > 0.5
            enter = enter + jnp.where(from_near, near[it, at, :], far[it, at, :])
            fields = []
            for q in range(XL):
                r = PAD + q
                enter = fac[q, at, :] * enter + wgt[r, at, :] * eq[:, r * NY : (r + 1) * NY]
                h = along_y(gd[q, at, :] + enter, yrow[i])
                fields.append(h)
                if not last:
                    hi, lo = split(h)
                    fhi[at, q * NY : (q + 1) * NY] = hi
                    flo[at, q * NY : (q + 1) * NY] = lo
            if last:
                index = jnp.where(fys[at, :] > 0.5, lane_of(lane), lane_of(NY - 1 - lane))
                for x in range(XL):
                    picked = jnp.where(forward, fields[x], fields[XL - 1 - x])
                    out[pl.ds(i * VB * XL + x, VB, stride=XL), :] = jnp.take_along_axis(
                        picked, index, axis=1
                    )
            else:
                sweep_source(fields, at)
            return c

        in_groups(block, None if last else it + 1)

    for it in range(ITERS):
        macro(it)
        main(it)
        if it < ITERS - 1:
            first = dot(rows_g[...], fhi[...])
            groups = first[0 : 4 * KR] + first[4 * KR : 8 * KR] + dot(rows_g[0 : 4 * KR, :], flo[...])
            turn = lambda t: jnp.concatenate(
                [t[:, x * NY : (x + 1) * NY] for x in reversed(range(XL))], axis=1
            )
            up = groups[0:KR] + turn(groups[2 * KR : 3 * KR])
            down = groups[KR : 2 * KR] + turn(groups[3 * KR : 4 * KR])
            spans = [slice(x * NY, (x + 1) * NY) for x in range(XL)]
            moment = jnp.concatenate(
                [restored(up[:, at]) + restored_back(down[:, at]) for at in spans], axis=1
            )
            sent += start_reduce(it + 1, moment)
            chain_across(it + 1)
            sent += second_stage(it + 1)
            chain_back(it + 1)
            sent += third_stage(it + 1)
            sent += forward_far(it + 1)
            for done in range(ITERS):
                drain_chain(done)
            for copy in sent:
                copy.wait_send()

    for x in range(XL):
        settled_out[:, x, :] = drive_s[XL * slab + x][0:5]


def copy_out(rows, settled, rows_out, settled_out, sem):
    copies = [
        pltpu.make_async_copy(settled, settled_out, sem.at[0]),
        pltpu.make_async_copy(rows, rows_out, sem.at[1]),
    ]
    for copy in copies:
        copy.start()
    for copy in copies:
        copy.wait()


def on_device(dist, speeds, weights, collision, wall_values, wall_kind):
    vmem = pl.BlockSpec(memory_space=pltpu.VMEM)
    hbm = pl.BlockSpec(memory_space=pltpu.HBM)
    dma = pltpu.SemaphoreType.DMA
    full = (V, NY)
    scratch = [
        pltpu.VMEM((V * XL, NY), f32),
        pltpu.VMEM((XL, *full), f32),
        pltpu.VMEM((V, XL * NY), bf16),
        pltpu.VMEM((V, XL * NY), bf16),
        pltpu.VMEM((XL, *full), f32),
        pltpu.VMEM((NX, *full), f32),
        pltpu.VMEM((XL, *full), f32),
        pltpu.VMEM(full, f32),
        pltpu.VMEM((NB, TABLE, VB), f32),
        pltpu.VMEM(full, f32),
        pltpu.VMEM(full, f32),
        pltpu.VMEM((NX, 8, NY), f32),
        pltpu.VMEM((NX, 8, NY), f32),
        pltpu.VMEM(full, f32),
        pltpu.VMEM(full, f32),
        pltpu.VMEM((ITERS, *full), f32),
        pltpu.VMEM((ITERS, *full), f32),
        pltpu.VMEM((ITERS, *full), f32),
        pltpu.VMEM((ITERS, *full), f32),
        pltpu.VMEM((128, V), f32),
        pltpu.VMEM((2 * KR, V), bf16),
        pltpu.VMEM((8 * KR, V), bf16),
        pltpu.VMEM((V, 128), bf16),
        pltpu.VMEM((V, 128), f32),
        pltpu.VMEM((ITERS, 2, 4, ROWS, HALF), f32),
        pltpu.VMEM((ITERS, 2, 4, ROWS, HALF), f32),
        pltpu.VMEM((ITERS, 2, 8, ROWS, HALF), f32),
        pltpu.VMEM((SLABS, XL, NY), f32),
        pltpu.VMEM((3, NX + 2 * PAD, 8, NY), f32),
        pltpu.VMEM((2, NX + 2 * PAD, 16, NY), bf16),
        pltpu.VMEM((128, NX * NY), bf16),
        pltpu.VMEM((NX, 8, NY), f32),
        pltpu.VMEM((3, V), f32),
        pltpu.VMEM((V,), f32),
        pltpu.VMEM((XL, NY), f32),
        pltpu.VMEM((2, V), f32),
        pltpu.VMEM((2, V), jnp.int32),
        dma((NB,)),
        dma((5,)),
        dma((ITERS, 2, 2, 3)),
        dma((ITERS, 2, 2, 3)),
        dma((ITERS, 2, 7)),
        dma((ITERS, 2, 7)),
        dma((3,)),
        dma((3,)),
        dma((ITERS, NC)),
        dma((ITERS, NC)),
        dma((ITERS, NC)),
        dma((ITERS, NC)),
    ]
    rows, settled = pl.pallas_call(
        transport_kernel,
        out_shape=(
            jax.ShapeDtypeStruct((V * XL, NY), f32),
            jax.ShapeDtypeStruct((5, XL, NY), f32),
        ),
        in_specs=[hbm] * 6,
        out_specs=(vmem, vmem),
        scratch_shapes=scratch,
        compiler_params=pltpu.CompilerParams(
            collective_id=0, has_side_effects=True, vmem_limit_bytes=50000000
        ),
        name="transport",
    )(*(
        pltpu.with_memory_space_constraint(value, pltpu.HBM)
        for value in (dist.reshape(V * XL, NY), speeds, weights, collision, wall_values, wall_kind)
    ))
    anywhere = pl.BlockSpec(memory_space=pl.ANY)
    rows, settled = pl.pallas_call(
        copy_out,
        out_shape=(
            jax.ShapeDtypeStruct((V * XL, NY), f32),
            jax.ShapeDtypeStruct((5, XL, NY), f32),
        ),
        in_specs=[anywhere, anywhere],
        out_specs=(hbm, hbm),
        scratch_shapes=[dma((2,))],
        compiler_params=pltpu.CompilerParams(vmem_limit_bytes=1024 * 1024),
        name="copy_out",
    )(rows, settled)
    return rows.reshape(V, XL, NY), settled


def solution(mesh):
    return jax.shard_map(
        on_device,
        mesh=mesh,
        in_specs=(
            P("vel", "slab", None),
            P(None, "vel"),
            P("vel"),
            P("slab", None),
            P(None, "vel"),
            P(None, "vel"),
        ),
        out_specs=(P("vel", "slab", None), P(None, "slab", None)),
        check_vma=False,
    )
```
